32 devices in a mesh: view: 2 (over core), gz: 8 (over z, y), gy: 2 (over x).
Axes of the slice: x: 2, y: 2, z: 4, core: 2. Of those that a mesh axis runs over, the one named last changes fastest.
Arguments:
- observed: float32 [2, 512, 32, 256], P('view', 'gz', 'gy'), may hold values from 0.5 to 4
- start: float32 [512, 32, 256], P('gz', 'gy'), may hold values from 0.5 to 2
- spread_z: float32 [2, 31], P('view'), may hold values from 0.05 to 1
- spread_y: float32 [2, 7], P('view'), may hold values from 0.1 to 1
- spread_x: float32 [2, 7], P('view'), may hold values from 0.1 to 1
Outputs:
- estimate: float32 [512, 32, 256], P('gz', 'gy')
The draws below stay inside these ranges and needn't reach their ends.
All inputs are finite; a program needn't handle non-finite values.
Results may differ from the reference program's by a relative error of at most 0.0001.
Values sent between devices are 32-bit elements; how exact they have to be, the bound alone decides.
A program may use at most 64 MiB of HBM per device.

```python
import math
import jax
import jax.numpy as jnp
from jax import lax

NX = 256
KZ = 31
KY = 7
KX = 7
ITERS = 2
NZ = 512
NY = 32
N_VIEW = 2


def level_of(own_key, extent, pieces, least, top_value):
    loudness = 1.0
    for axis_at, shards_of in pieces:
        draws = jax.random.uniform(jax.random.fold_in(jax.random.fold_in(own_key, 6), axis_at), (shards_of,), jnp.float32, least / len(pieces), top_value / len(pieces))
        loudness = loudness * jnp.repeat(jnp.exp(draws), extent[axis_at] // shards_of).reshape((-1,) + (1,) * (len(extent) - 1 - axis_at))
    return loudness


def setup_inputs(seed: int = 0) -> dict:
    key_of = jax.random.split(jax.random.key(seed), 6)
    observed = jnp.clip(jnp.exp(math.log(4.0) - 2.0794415 * jax.random.uniform(key_of[0], (N_VIEW, NZ, NY, NX), jnp.float32) ** level_of(key_of[0], (N_VIEW, NZ, NY, NX), ((0, 2), (1, 8), (2, 2)), -0.2, 0.2)), 0.5, 4.0)
    start = jnp.clip(jnp.exp(math.log(2.0) - 1.3862944 * jax.random.uniform(key_of[1], (NZ, NY, NX), jnp.float32) ** level_of(key_of[1], (NZ, NY, NX), ((0, 8), (1, 2)), -0.2, 0.2)), 0.5, 2.0)
    spread_z = jnp.clip(jnp.exp(math.log(1.0) - 2.9957323 * jax.random.uniform(key_of[2], (N_VIEW, KZ), jnp.float32) ** level_of(key_of[2], (N_VIEW, KZ), ((0, 2),), -0.2, 0.2)), 0.05, 1.0)
    spread_y = jnp.clip(jnp.exp(math.log(1.0) - 2.3025851 * jax.random.uniform(key_of[3], (N_VIEW, KY), jnp.float32) ** level_of(key_of[3], (N_VIEW, KY), ((0, 2),), -0.2, 0.2)), 0.1, 1.0)
    spread_x = jnp.clip(jnp.exp(math.log(1.0) - 2.3025851 * jax.random.uniform(key_of[4], (N_VIEW, KX), jnp.float32) ** level_of(key_of[4], (N_VIEW, KX), ((0, 2),), -0.2, 0.2)), 0.1, 1.0)
    return dict(observed=observed, start=start, spread_z=spread_z, spread_y=spread_y, spread_x=spread_x)


def correlate(field, weights, along, margin):
    padding = [(0, 0), (0, 0), (0, 0)]
    padding[along] = (margin, margin)
    padded = jnp.pad(field, padding)
    taps = weights.shape[0]
    length = padded.shape[along] - taps + 1
    total = weights[0] * lax.slice_in_dim(padded, 0, length, 1, along)
    for offset in range(1, taps):
        total = total + weights[offset] * lax.slice_in_dim(padded, offset, offset + length, 1, along)
    return total


def blur(field, weight_z, weight_y, weight_x):
    field = correlate(field, weight_z, 0, KZ // 2)
    field = correlate(field, weight_y, 1, KY // 2)
    return correlate(field, weight_x, 2, KX // 2)


def normalized(profile):
    return profile / jnp.sum(profile)


def reference(observed, start, spread_z, spread_y, spread_x):
    estimate = start
    for sweep in range(ITERS):
        summed = jnp.zeros_like(start)
        for which_view in range(2):
            weight_z = normalized(spread_z[which_view])
            weight_y = normalized(spread_y[which_view])
            weight_x = normalized(spread_x[which_view])
            blurred = blur(estimate, weight_z, weight_y, weight_x)
            quotient = observed[which_view] / blurred
            summed = summed + blur(quotient, weight_z[::-1], weight_y[::-1], weight_x[::-1])
        estimate = estimate * (0.5 * summed)
    return estimate
```

```python
import contextlib
import functools

import jax
import jax.numpy as jnp
from jax import lax
from jax.experimental import pallas as pl
from jax.experimental.pallas import tpu as pltpu
from jax.sharding import PartitionSpec as P

ITERS = 2
MESH = pl.DeviceIdType.MESH
F32 = jnp.float32
BF16 = jnp.bfloat16


def scope(name):
    return contextlib.nullcontext()


def split(x):
    high = x.astype(BF16)
    return high, (x - high.astype(F32)).astype(BF16)


def kernel(dims, obs_hbm, start_hbm, sz_ref, sy_ref, sx_ref, out_hbm,
           raw_z, raw_y, raw_x, stage, land, obs_z, obs_t, mine, theirs, wf, wb, tx, zbuf, ybuf, qbuf,
           ebuf, cbuf, rybuf, rzbuf, lsem, osem, gsem, hsem, ssem, rsem, xssem, xrsem):
    NH, NY, NX, HZ, KZ, KY, KX, S, G = dims
    my, mz, mx = KY // 2, KZ // 2, KX // 2
    NE, NR, NQ = NH + 2 * HZ, NY + 2 * my, NY + 4 * my
    CH = NY // 2
    v = lax.axis_index("view")
    gy = lax.axis_index("gy")
    s = 2 * lax.axis_index("gz") + v
    up_z, dn_z = s < S - 1, s > 0
    up_y, dn_y = gy < G - 1, gy > 0
    f = lax.rem(gy, 2)
    has = (jnp.logical_or(jnp.logical_and(f == 0, up_y), jnp.logical_and(f == 1, dn_y)),
           jnp.logical_or(jnp.logical_and(f == 0, dn_y), jnp.logical_and(f == 1, up_y)))

    def row(i0, n=1):
        return i0 + f * (NR - 2 * i0 - n)

    def qrow(j0, n=1):
        return j0 + f * (NQ - 2 * j0 - n)

    def zdev(t):
        t = lax.rem(t + S, S)
        return {"view": lax.rem(t, 2), "gz": t // 2}

    zto = (zdev(s + 1), zdev(s - 1))
    step = 1 - 2 * f
    yto = ({"gy": lax.rem(gy + step + G, G)}, {"gy": lax.rem(gy - step + G, G)})
    partner = {"view": 1 - v}
    zhas, zfrom = (up_z, dn_z), (dn_z, up_z)

    def when(cond, fn):
        @pl.when(cond)
        def _():
            fn()

    def both(a, b):
        return jnp.logical_and(a, b)

    barrier = pltpu.get_barrier_semaphore()
    for there, to in ((up_z, zto[0]), (dn_z, zto[1]), (has[0], yto[0]), (has[1], yto[1])):
        @pl.when(there)
        def _(to=to):
            pl.semaphore_signal(barrier, inc=1, device_id=to, device_id_type=MESH)

    load_start = pltpu.make_async_copy(start_hbm.at[pl.ds(v * NH, NH)], stage.at[0], lsem.at[0])
    load_start.start()
    load_obs = pltpu.make_async_copy(obs_hbm.at[0, pl.ds(v * NH, NH)], obs_z.at[v], lsem.at[1])
    load_obs.start()
    loads = [pltpu.make_async_copy(ref, raw, lsem.at[3 + k])
             for k, (ref, raw) in enumerate(((sz_ref, raw_z), (sy_ref, raw_y), (sx_ref, raw_x)))]
    for load in loads:
        load.start()

    blocks = (CH * (1 - f), CH * f)

    def first(d, k):
        b0 = pl.multiple_of(blocks[k], CH)
        src0 = v * NH + (NH - mz, 0)[d]
        dst0 = (HZ - mz, 0)[d]
        return pltpu.make_async_remote_copy(
            src_ref=start_hbm.at[pl.ds(src0, mz), pl.ds(b0, CH)],
            dst_ref=land.at[d, pl.ds(dst0, mz), pl.ds(b0, CH)],
            send_sem=gsem.at[d, k], recv_sem=hsem.at[d, k], device_id=zto[d], device_id_type=MESH)

    peers = sum(there.astype(jnp.int32) for there in (up_z, dn_z, has[0], has[1]))
    with scope("Wbar"):
        pl.semaphore_wait(barrier, peers)
    for k in range(2):
        for d in range(2):
            when(zhas[d], first(d, k).start)

    land[0, 0:HZ - mz] = jnp.zeros((HZ - mz, NY, NX), F32)
    land[1, mz:HZ] = jnp.zeros((HZ - mz, NY, NX), F32)
    for d in range(2):
        def blank(d=d):
            for it in range(ITERS):
                z0 = (0, HZ + NH)[d]
                ebuf[it, :, z0:z0 + HZ, :] = jnp.zeros((NR, HZ, NX), F32)
        when(jnp.logical_not(zfrom[d]), blank)

        def blank_rows(d=d):
            zbuf[pl.ds(row((my + NY, 0)[d], my), my)] = jnp.zeros((my, NE, NX), F32)
        when(jnp.logical_not(has[d]), blank_rows)

    def copy(phase, m, src, dst, to):
        return pltpu.make_async_remote_copy(
            src_ref=src, dst_ref=dst, send_sem=ssem.at[phase, m], recv_sem=rsem.at[phase, m],
            device_id=to, device_id_type=MESH)

    ROWS = ((NY, my), (my, my), (2 * my, CH - 2 * my), (CH, 2 * my), (CH + 2 * my, NY - CH - 2 * my))
    NP = len(ROWS)
    ZED = ((HZ, NH), (0, HZ), (HZ + NH, HZ))
    zed_has = (None, dn_z, up_z)
    EDGE, HALO = (NY, my), (my + NY, 0)
    THERE = (f * (my + NY), (1 - f) * (my + NY))

    def gz(it, d, p):
        e = ebuf.at[it]
        src0, dst0 = ((NH, 0), (HZ, HZ + NH))[d]
        n = ROWS[p][1]
        r0 = row(*ROWS[p])
        return copy(2 * it, NP * d + p, e.at[pl.ds(r0, n), pl.ds(src0, HZ)],
                    e.at[pl.ds(r0, n), pl.ds(dst0, HZ)], zto[d])

    def gyc(it, d, p):
        e = ebuf.at[it]
        z0, n = ZED[p]
        return copy(2 * it, 2 * NP + 3 * d + p, e.at[pl.ds(row(EDGE[d], my), my), pl.ds(z0, n)],
                    e.at[pl.ds(THERE[d], my), pl.ds(z0, n)], yto[d])

    def sz(it, d, p):
        src0 = (HZ + NH, 0)[d]
        n = ROWS[p][1]
        r0 = row(*ROWS[p])
        return copy(2 * it + 1, NP * d + p, cbuf.at[it, pl.ds(r0, n), pl.ds(src0, HZ)],
                    rzbuf.at[it, d, pl.ds(r0 - my, n)], zto[d])

    def sy(it, d, p):
        z0, n = ZED[p]
        return copy(2 * it + 1, 2 * NP + 3 * d + p, cbuf.at[it, pl.ds(row(HALO[d], my), my), pl.ds(z0, n)],
                    rybuf.at[it, d, :, pl.ds(z0, n)], yto[d])

    def gather_piece(it, p):
        for d in range(2):
            when(zhas[d], gz(it, d, p).start)

    def gather_own(it):
        for d in range(2):
            when(has[d], gyc(it, d, 0).start)

    def relay(it, p, d):
        if p < 2:
            when(both(zfrom[d], has[p]), gyc(it, p, 1 + d).start)

    def gather_take(it, p):
        for d in range(2):
            when(zfrom[d], gz(it, d, p).wait_recv)
            relay(it, p, d)

    def first_take(k):
        b0 = pl.multiple_of(blocks[k], CH)
        for d in range(2):
            z0 = (0, HZ + NH)[d]

            def take(d=d, z0=z0):
                first(d, k).wait_recv()
                ebuf[0, pl.ds(my + b0, CH), z0:z0 + HZ, :] = jnp.transpose(land[d, :, pl.ds(b0, CH), :], (1, 0, 2))
            when(zfrom[d], take)
            relay(0, k, d)

    def gather_edge(it, d):
        when(has[d], gyc(it, d, 0).wait_recv)
        for q in range(2):
            when(both(zed_has[1 + q], has[d]), gyc(it, d, 1 + q).wait_recv)

            def blank(q=q):
                z0 = ZED[1 + q][0]
                ebuf[it, pl.ds(row(HALO[d], my), my), z0:z0 + HZ, :] = jnp.zeros((my, HZ, NX), F32)

    def sent(it):
        for d in range(2):
            for p in range(NP):
                if it > 0:
                    when(zhas[d], gz(it, d, p).wait_send)
                when(zhas[d], sz(it, d, p).wait_send)
            for y in (gyc, sy):
                when(has[d], y(it, d, 0).wait_send)
                for q in range(2):
                    when(both(zed_has[1 + q], has[d]), y(it, d, 1 + q).wait_send)

    def scatter_edge(it, d):
        for q in range(2):
            when(both(zed_has[1 + q], has[d]), sy(it, d, 1 + q).start)
        when(has[d], sy(it, d, 0).start)

    def scatter_piece(it, p):
        for d in range(2):
            when(zhas[d], sz(it, d, p).start)

    def scatter_end(it, p):
        r0 = row(*ROWS[p])
        for q in range(2):
            z0 = ZED[1 + q][0]

            def add(q=q, z0=z0):
                sy(it, p, 1 + q).wait_recv()
                cbuf[it, pl.ds(r0, my), z0:z0 + HZ, :] += rybuf[it, p, :, z0:z0 + HZ, :]
            when(both(zed_has[1 + q], has[p]), add)
            when(zed_has[1 + q], sz(it, 1 - q, p).start)

    def scatter_take(it, p):
        n = ROWS[p][1]
        r0 = row(*ROWS[p])
        if p < 2:
            def add_y():
                sy(it, p, 0).wait_recv()
                cbuf[it, pl.ds(r0, n), HZ:HZ + NH, :] += rybuf[it, p, :, HZ:HZ + NH, :]
            when(has[p], add_y)
        for d in range(2):
            z0 = (HZ, NH)[d]

            def add_z(d=d, z0=z0):
                sz(it, d, p).wait_recv()
                cbuf[it, pl.ds(r0, n), z0:z0 + HZ, :] += rzbuf[it, d, pl.ds(r0 - my, n)]
            when(zfrom[d], add_z)

    with scope("Wload"):
        load_start.wait()
    ebuf[0, my:my + NY, HZ:HZ + NH, :] = jnp.transpose(stage[0], (1, 0, 2))
    gather_own(0)
    mine[...] = jnp.zeros_like(mine)
    for k, (raw, taps) in enumerate(((raw_z, KZ), (raw_y, KY), (raw_x, KX))):
        loads[k].wait()
        mine[k:k + 1, 0:taps] = raw[...] / jnp.sum(raw[...], axis=1, keepdims=True)
    swap_prof = pltpu.make_async_remote_copy(
        src_ref=mine, dst_ref=theirs, send_sem=xssem.at[0], recv_sem=xrsem.at[0],
        device_id=partner, device_id_type=MESH)
    swap_prof.start()
    swap_obs = pltpu.make_async_remote_copy(
        src_ref=obs_hbm.at[0, pl.ds((1 - v) * NH, NH)], dst_ref=obs_z.at[v],
        send_sem=xssem.at[1], recv_sem=xrsem.at[1], device_id=partner, device_id_type=MESH)
    swap_obs.start()

    with scope("Wprof"):
        swap_prof.wait()
    own, other = mine[...], theirs[...]
    prof = (jnp.where(v == 0, own, other), jnp.where(v == 0, other, own))

    def tap(view, k, a):
        return prof[view][k:k + 1, a:a + 1]

    rows = lax.broadcasted_iota(jnp.int32, (NE, 3 * NE), 0)
    cols = lax.broadcasted_iota(jnp.int32, (NE, 3 * NE), 1)
    third = cols // NE
    cols = cols - third * NE

    def banded(diff, view, k, taps):
        w = jnp.zeros(diff.shape, F32)
        for a in range(taps):
            w = jnp.where(diff == a, tap(view, k, a), w)
        return w

    off = HZ - mz
    for ref, inner, outer in ((wf, rows, cols), (wb, cols, rows)):
        second = inner >= NH
        diff = outer - jnp.where(second, inner - NH, inner) - off
        w = jnp.where(second, banded(diff, 1, 0, KZ), banded(diff, 0, 0, KZ))
        high, low = split(w)
        ref[...] = jnp.where(third == 2, low.astype(F32), high.astype(F32)).astype(BF16)
    for view in range(2):
        for back in range(2):
            for r0 in range(0, NX, 64):
                r = lax.broadcasted_iota(jnp.int32, (64, NX), 0) + r0
                c = lax.broadcasted_iota(jnp.int32, (64, NX), 1)
                diff = (c - r if back else r - c) + mx
                high, low = split(banded(diff, view, 2, KX))
                tx[view, back, 0, r0:r0 + 64, :] = high
                tx[view, back, 1, r0:r0 + 64, :] = low
    wy = [[jnp.broadcast_to(tap(view, 1, b), (NH, NX)) for b in range(KY)] for view in range(2)]

    qbuf[0:2 * my] = jnp.zeros((2 * my, NE, NX), F32)
    qbuf[2 * my + NY:] = jnp.zeros((2 * my, NE, NX), F32)

    with scope("Wobs"):
        load_obs.wait()
        swap_obs.wait()
    for view in range(2):
        obs_t[view] = jnp.transpose(obs_z[view], (1, 0, 2))

    def xblur(high, low, view, back):
        both_ = jnp.concatenate([high, low], axis=0)
        n = high.shape[0]
        d = jnp.dot(both_, tx[view, back, 0], preferred_element_type=F32)
        d2 = jnp.dot(high, tx[view, back, 1], preferred_element_type=F32)
        return d[:n] + (d[n:] + d2)

    def stacked(x):
        high, low = split(x)
        return jnp.concatenate([high, low, high], axis=0)

    for it in range(ITERS):
        def zrows(i0, n, it=it):
            with scope(f"z{it}_{i0}"):
                r0 = row(i0, n)
                for y in range(n):
                    zbuf[r0 + y] = jnp.dot(wf[...], stacked(ebuf[it, r0 + y]), preferred_element_type=F32)

        def qrows(o0, n, it=it):
            with scope(f"q{it}_{o0}"):
                y0 = row(o0 + my, n) - my
                for view in range(2):
                    z0 = view * NH
                    for y in range(n):
                        acc = wy[view][0] * zbuf[y0 + y, z0:z0 + NH, :]
                        for b in range(1, KY):
                            acc = acc + wy[view][b] * zbuf[y0 + y + b, z0:z0 + NH, :]
                        high, low = split(acc)
                        ybuf[view, 0, y * NH:(y + 1) * NH, :] = high
                        ybuf[view, 1, y * NH:(y + 1) * NH, :] = low
                for view in range(2):
                    z0 = view * NH
                    m = n * NH
                    blurred = xblur(ybuf[view, 0, 0:m], ybuf[view, 1, 0:m], view, 0)
                    quotient = obs_t[view, pl.ds(y0, n)].reshape(m, NX) / blurred
                    high, low = split(quotient)
                    ybuf[view, 2, 0:m] = high
                    ybuf[view, 3, 0:m] = low
                    qbuf[pl.ds(2 * my + y0, n), z0:z0 + NH, :] = xblur(
                        ybuf[view, 2, 0:m], ybuf[view, 3, 0:m], view, 1).reshape(n, NH, NX)

        def crows(i0, n, it=it):
            with scope(f"c{it}_{i0}"):
                r0 = row(i0, n)
                for y in range(n):
                    r = r0 + y
                    parts = []
                    for view in range(2):
                        z0 = view * NH
                        acc = wy[view][0] * qbuf[r + 2 * my, z0:z0 + NH, :]
                        for b in range(1, KY):
                            acc = acc + wy[view][b] * qbuf[r + 2 * my - b, z0:z0 + NH, :]
                        parts.append(acc)
                    cbuf[it, r] = jnp.dot(wb[...], stacked(jnp.concatenate(parts, axis=0)),
                                          preferred_element_type=F32)

        if it == 0:
            with scope("Wg0_in"):
                first_take(0)
            zrows(my + CH, CH)
            with scope("Wg0_out"):
                first_take(1)
            zrows(my, CH)
        else:
            for p in (2, 1, 3):
                with scope(f"Wg{it}_{p}"):
                    gather_take(it, p)
                zrows(*ROWS[p])

        def low_edge(it=it):
            gather_edge(it, 1)
            zrows(0, my)
        when(has[1], low_edge)
        qrows(0, CH)

        def low_scatter(it=it):
            crows(0, my)
            scatter_edge(it, 1)
        when(has[1], low_scatter)
        crows(*ROWS[1])
        when(jnp.logical_not(has[1]), functools.partial(scatter_piece, it, 1))
        crows(*ROWS[2])
        scatter_piece(it, 2)
        if it > 0:
            for p in (0, 4):
                with scope(f"Wg{it}_{p}"):
                    gather_take(it, p)
                zrows(*ROWS[p])

        def high_edge(it=it):
            with scope(f"Wge{it}"):
                gather_edge(it, 0)
            zrows(my + NY, my)
        when(has[0], high_edge)
        qrows(CH, CH)

        def high_scatter(it=it):
            crows(my + NY, my)
            scatter_edge(it, 0)
        when(has[0], high_scatter)
        for p in (3, 4):
            crows(*ROWS[p])
            scatter_piece(it, p)
        crows(*ROWS[0])
        with scope(f"Wse{it}"):
            when(has[1], functools.partial(scatter_end, it, 1))
            scatter_end(it, 0)

        def update(p, it=it):
            n = ROWS[p][1]
            r0 = row(*ROWS[p])
            with scope(f"Wst{it}_{p}"):
                scatter_take(it, p)
            new = ebuf[it, pl.ds(r0, n), HZ:HZ + NH, :] * (0.5 * cbuf[it, pl.ds(r0, n), HZ:HZ + NH, :])
            if it + 1 < ITERS:
                ebuf[it + 1, pl.ds(r0, n), HZ:HZ + NH, :] = new
            else:
                zbuf[pl.ds(r0, n), 0:NH, :] = new

        if it + 1 < ITERS:
            for p in (1, 2, 3):
                update(p)
                gather_piece(it + 1, p)
            update(0)
            gather_piece(it + 1, 0)
            gather_own(it + 1)
            update(4)
            gather_piece(it + 1, 4)
        else:
            outs = []
            for n, p in enumerate((1, 2, 3, 4, 0)):
                update(p)
                r0 = row(*ROWS[p])
                rows_ = ROWS[p][1]
                src = zbuf.at[pl.ds(r0, rows_), pl.ds(0, NH)]
                dst = out_hbm.at[pl.ds(r0 - my, rows_), pl.ds(v * NH, NH)]
                outs.append(pltpu.make_async_copy(src, dst, osem.at[n]))
                outs.append(pltpu.make_async_remote_copy(
                    src_ref=src, dst_ref=dst, send_sem=xssem.at[2 + n], recv_sem=xrsem.at[2 + n],
                    device_id=partner, device_id_type=MESH))
                outs[-1].start()
                outs[-2].start()
            with scope("Wout"):
                for out in outs:
                    out.wait()
    for it in range(ITERS):
        sent(it)
    for k in range(2):
        for d in range(2):
            when(zhas[d], first(d, k).wait_send)


def on_device(S, G, observed, start, spread_z, spread_y, spread_x):
    NZ, NY, NX = start.shape
    KZ, KY, KX = spread_z.shape[1], spread_y.shape[1], spread_x.shape[1]
    NH = NZ // 2
    my = KY // 2
    HZ = -(-(KZ // 2) // 8) * 8
    NE, NR = NH + 2 * HZ, NY + 2 * my
    dims = (NH, NY, NX, HZ, KZ, KY, KX, S, G)
    vm = pltpu.VMEM
    hbm = pl.BlockSpec(memory_space=pltpu.HBM)
    out = pl.pallas_call(
        functools.partial(kernel, dims),
        out_shape=jax.ShapeDtypeStruct((NY, NZ, NX), F32),
        in_specs=[hbm] * 5,
        out_specs=hbm,
        scratch_shapes=[
            vm((1, KZ), F32), vm((1, KY), F32), vm((1, KX), F32),
            vm((1, NH, NY, NX), F32), vm((2, HZ, NY, NX), F32),
            vm((2, NH, NY, NX), F32), vm((2, NY, NH, NX), F32),
            vm((8, 128), F32), vm((8, 128), F32),
            vm((NE, 3 * NE), BF16), vm((NE, 3 * NE), BF16), vm((2, 2, 2, NX, NX), BF16),
            vm((NR, NE, NX), F32), vm((2, 4, NY // 2 * NH, NX), BF16), vm((NY + 4 * my, NE, NX), F32),
            vm((ITERS, NR, NE, NX), F32), vm((ITERS, NR, NE, NX), F32),
            vm((ITERS, 2, my, NE, NX), F32), vm((ITERS, 2, NY, HZ, NX), F32),
            pltpu.SemaphoreType.DMA((6,)), pltpu.SemaphoreType.DMA((5,)),
            pltpu.SemaphoreType.DMA((2, 2)), pltpu.SemaphoreType.DMA((2, 2)),
            pltpu.SemaphoreType.DMA((2 * ITERS, 16)), pltpu.SemaphoreType.DMA((2 * ITERS, 16)),
            pltpu.SemaphoreType.DMA((7,)), pltpu.SemaphoreType.DMA((7,)),
        ],
        compiler_params=pltpu.CompilerParams(
            collective_id=0, has_side_effects=True, vmem_limit_bytes=67043328),
    )(observed, start, spread_z, spread_y, spread_x)
    return jnp.transpose(out, (1, 0, 2))


def solution(mesh):
    S, G = 2 * mesh.shape["gz"], mesh.shape["gy"]
    return jax.shard_map(
        functools.partial(on_device, S, G),
        mesh=mesh,
        in_specs=(
            P("view", "gz", "gy", None),
            P("gz", "gy", None),
            P("view", None),
            P("view", None),
            P("view", None),
        ),
        out_specs=P("gz", "gy", None),
        check_vma=False,
    )
```

```python
import contextlib
import functools

import jax
import jax.numpy as jnp
from jax import lax
from jax.experimental import pallas as pl
from jax.experimental.pallas import tpu as pltpu
from jax.sharding import PartitionSpec as P

ITERS = 2
MESH = pl.DeviceIdType.MESH
F32 = jnp.float32
BF16 = jnp.bfloat16


def scope(name):
    return contextlib.nullcontext()


def split(x):
    high = x.astype(BF16)
    return high, (x - high.astype(F32)).astype(BF16)


def kernel(dims, obs_hbm, start_hbm, sz_ref, sy_ref, sx_ref, out_hbm,
           raw_z, raw_y, raw_x, stage, land, obs_z, obs_t, mine, theirs, wf, wb, tx, zbuf, ybuf, qbuf,
           ebuf, cbuf, rybuf, rzbuf, sbuf, lsem, osem, gsem, hsem, ssem, rsem, xssem, xrsem):
    NH, NY, NX, HZ, KZ, KY, KX, S, G = dims
    my, mz, mx = KY // 2, KZ // 2, KX // 2
    NE, NR, NQ = NH + 2 * HZ, NY + 2 * my, NY + 4 * my
    CH = NY // 2
    v = lax.axis_index("view")
    gy = lax.axis_index("gy")
    s = 2 * lax.axis_index("gz") + v
    up_z, dn_z = s < S - 1, s > 0
    up_y, dn_y = gy < G - 1, gy > 0
    f = lax.rem(gy, 2)
    has = (jnp.logical_or(jnp.logical_and(f == 0, up_y), jnp.logical_and(f == 1, dn_y)),
           jnp.logical_or(jnp.logical_and(f == 0, dn_y), jnp.logical_and(f == 1, up_y)))

    def row(i0, n=1):
        return i0 + f * (NR - 2 * i0 - n)

    def qrow(j0, n=1):
        return j0 + f * (NQ - 2 * j0 - n)

    def zdev(t):
        t = lax.rem(t + S, S)
        return {"view": lax.rem(t, 2), "gz": t // 2}

    zto = (zdev(s + 1), zdev(s - 1))
    step = 1 - 2 * f
    yto = ({"gy": lax.rem(gy + step + G, G)}, {"gy": lax.rem(gy - step + G, G)})
    partner = {"view": 1 - v}
    zout = dict(zdev(s - 1 + 2 * v))
    diag = tuple({**zout, **yto[d]} for d in range(2))
    zhas, zfrom = (up_z, dn_z), (dn_z, up_z)

    def when(cond, fn):
        @pl.when(cond)
        def _():
            fn()

    def both(a, b):
        return jnp.logical_and(a, b)

    barrier = pltpu.get_barrier_semaphore()
    greet = ((up_z, zto[0]), (dn_z, zto[1]), (has[0], yto[0]), (has[1], yto[1]))
    for there, to in greet:
        @pl.when(there)
        def _(to=to):
            pl.semaphore_signal(barrier, inc=1, device_id=to, device_id_type=MESH)

    load_start = pltpu.make_async_copy(start_hbm.at[pl.ds(v * NH, NH)], stage.at[0], lsem.at[0])
    load_start.start()
    load_obs = pltpu.make_async_copy(obs_hbm.at[0, pl.ds(v * NH, NH)], obs_z.at[v], lsem.at[1])
    load_obs.start()
    loads = [pltpu.make_async_copy(ref, raw, lsem.at[3 + k])
             for k, (ref, raw) in enumerate(((sz_ref, raw_z), (sy_ref, raw_y), (sx_ref, raw_x)))]
    for load in loads:
        load.start()

    blocks = (CH * (1 - f), CH * f)

    def first(d, k):
        b0 = pl.multiple_of(blocks[k], CH)
        src0 = v * NH + (NH - mz, 0)[d]
        dst0 = (HZ - mz, 0)[d]
        return pltpu.make_async_remote_copy(
            src_ref=start_hbm.at[pl.ds(src0, mz), pl.ds(b0, CH)],
            dst_ref=land.at[d, pl.ds(dst0, mz), pl.ds(b0, CH)],
            send_sem=gsem.at[d, k], recv_sem=hsem.at[d, k], device_id=zto[d], device_id_type=MESH)

    peers = sum(there.astype(jnp.int32) for there, _ in greet)
    with scope("Wbar"):
        pl.semaphore_wait(barrier, peers)
    for k in range(2):
        for d in range(2):
            when(zhas[d], first(d, k).start)

    land[0, 0:HZ - mz] = jnp.zeros((HZ - mz, NY, NX), F32)
    land[1, mz:HZ] = jnp.zeros((HZ - mz, NY, NX), F32)
    for d in range(2):
        def blank(d=d):
            for it in range(ITERS):
                z0 = (0, HZ + NH)[d]
                ebuf[it, :, z0:z0 + HZ, :] = jnp.zeros((NR, HZ, NX), F32)
        when(jnp.logical_not(zfrom[d]), blank)

        def blank_rows(d=d):
            zbuf[pl.ds(row((my + NY, 0)[d], my), my)] = jnp.zeros((my, NE, NX), F32)
        when(jnp.logical_not(has[d]), blank_rows)

    def copy(phase, m, src, dst, to):
        return pltpu.make_async_remote_copy(
            src_ref=src, dst_ref=dst, send_sem=ssem.at[phase, m], recv_sem=rsem.at[phase, m],
            device_id=to, device_id_type=MESH)

    ROWS = ((NY, my), (my, my), (2 * my, NY - 4 * my), (NY - 2 * my, my), (NY - my, my))
    OUT, MID = NY - 3 * my, 2 * my
    NP = len(ROWS)
    ZED = ((HZ, NH), (0, HZ), (HZ + NH, HZ))
    zed_has = (None, dn_z, up_z)
    EDGE, HALO = (NY, my), (my + NY, 0)
    THERE = (f * (my + NY), (1 - f) * (my + NY))

    def gz(it, d, p):
        e = ebuf.at[it]
        src0, dst0 = ((NH, 0), (HZ, HZ + NH))[d]
        n = ROWS[p][1]
        r0 = row(*ROWS[p])
        return copy(2 * it, NP * d + p, e.at[pl.ds(r0, n), pl.ds(src0, HZ)],
                    e.at[pl.ds(r0, n), pl.ds(dst0, HZ)], zto[d])

    def gyc(it, d, p):
        e = ebuf.at[it]
        z0, n = ZED[p]
        return copy(2 * it, 2 * NP + 3 * d + p, e.at[pl.ds(row(EDGE[d], my), my), pl.ds(z0, n)],
                    e.at[pl.ds(THERE[d], my), pl.ds(z0, n)], yto[d])

    def fwd(it, d, q):
        rows_ = pl.ds(row(HALO[d], my), my)
        e = ebuf.at[it]
        return copy(2 * it, 2 * NP + 6 + 2 * d + q, e.at[rows_, pl.ds((NH, HZ)[q], HZ)],
                    e.at[rows_, pl.ds((0, HZ + NH)[q], HZ)], partner)

    def sfwd(it, d, q):
        rows_ = pl.ds(row(HALO[d], my), my)
        return copy(2 * it + 1, 2 * NP + 6 + 2 * d + q, cbuf.at[it, rows_, pl.ds((HZ + NH, 0)[q], HZ)],
                    sbuf.at[it, d], partner)

    def diagonal(it, d, q):
        z0, n = ZED[1 + q]
        return copy(2 * it + 1, 2 * NP + 3 * d + 1 + q, cbuf.at[it, pl.ds(row(HALO[d], my), my), pl.ds(z0, n)],
                    rybuf.at[it, d, :, pl.ds(0, HZ)], diag[d])

    def sz(it, d, p):
        src0 = (HZ + NH, 0)[d]
        n = ROWS[p][1]
        r0 = row(*ROWS[p])
        return copy(2 * it + 1, NP * d + p, cbuf.at[it, pl.ds(r0, n), pl.ds(src0, HZ)],
                    rzbuf.at[it, d, pl.ds(r0 - my, n)], zto[d])

    def sy(it, d, p):
        z0, n = ZED[p]
        return copy(2 * it + 1, 2 * NP + 3 * d + p, cbuf.at[it, pl.ds(row(HALO[d], my), my), pl.ds(z0, n)],
                    rybuf.at[it, d, :, pl.ds(z0, n)], yto[d])

    def gather_piece(it, p):
        for d in range(2):
            when(zhas[d], gz(it, d, p).start)

    def gather_own(it):
        for d in range(2):
            when(has[d], gyc(it, d, 0).start)

    def relay(it, p, d):
        if p < 2:
            when(both(both(zfrom[d], has[p]), v == d), gyc(it, p, 1 + d).start)

    def gather_take(it, p):
        for d in range(2):
            when(zfrom[d], gz(it, d, p).wait_recv)
            relay(it, p, d)

    def first_take(k):
        b0 = pl.multiple_of(blocks[k], CH)
        for d in range(2):
            z0 = (0, HZ + NH)[d]

            def take(d=d, z0=z0):
                first(d, k).wait_recv()
                ebuf[0, pl.ds(my + b0, CH), z0:z0 + HZ, :] = jnp.transpose(land[d, :, pl.ds(b0, CH), :], (1, 0, 2))
            when(zfrom[d], take)
            relay(0, k, d)

    def edge_own(it, d):
        def go():
            gyc(it, d, 0).wait_recv()
            for q in range(2):
                when(v == q, fwd(it, d, q).start)
        when(has[d], go)

    def gather_edge(it, d):
        for q in range(2):
            when(both(both(zed_has[1 + q], has[d]), v == q), gyc(it, d, 1 + q).wait_recv)
            when(both(has[d], v == 1 - q), fwd(it, d, q).wait_recv)

    def sent(it):
        for d in range(2):
            for p in range(NP):
                if it > 0:
                    when(zhas[d], gz(it, d, p).wait_send)
                when(zhas[d], sz(it, d, p).wait_send)
            for y in (gyc, sy):
                when(has[d], y(it, d, 0).wait_send)
                for q in range(2):
                    corner = diagonal(it, d, q) if y is sy and it + 1 == ITERS else y(it, d, 1 + q)
                    when(both(both(zed_has[1 + q], has[d]), v == q), corner.wait_send)
            for y in (fwd, sfwd):
                for q in range(2):
                    when(both(has[d], v == q), y(it, d, q).wait_send)

    def scatter_edge(it, d):
        for q in range(2):
            corner = diagonal(it, d, q) if it + 1 == ITERS else sy(it, d, 1 + q)
            when(both(both(zed_has[1 + q], has[d]), v == q), corner.start)
            when(both(has[d], v == q), sfwd(it, d, q).start)

    def scatter_own(it, d):
        r0 = row(HALO[d], my)
        for q in range(2):
            def add(q=q):
                z0 = (HZ, NH)[q]
                sfwd(it, d, q).wait_recv()
                cbuf[it, pl.ds(r0, my), z0:z0 + HZ, :] += sbuf[it, d]
            when(both(has[d], v == 1 - q), add)
        when(has[d], sy(it, d, 0).start)

    def scatter_piece(it, p):
        for d in range(2):
            when(zhas[d], sz(it, d, p).start)

    def scatter_end(it, p):
        r0 = row(*ROWS[p])
        for q in range(2):
            z0 = ZED[1 + q][0]

            def add(q=q, z0=z0):
                sy(it, p, 1 + q).wait_recv()
                cbuf[it, pl.ds(r0, my), z0:z0 + HZ, :] += rybuf[it, p, :, z0:z0 + HZ, :]
            when(both(both(zed_has[1 + q], has[p]), v == q), add)
            when(both(zed_has[1 + q], v == q), sz(it, 1 - q, p).start)

    def scatter_near(it, p):
        for q in range(2):
            when(v == 1 - q, sz(it, 1 - q, p).start)

    def scatter_take(it, p):
        n = ROWS[p][1]
        r0 = row(*ROWS[p])
        if p < 2:
            def add_y():
                sy(it, p, 0).wait_recv()
                cbuf[it, pl.ds(r0, n), HZ:HZ + NH, :] += rybuf[it, p, :, HZ:HZ + NH, :]
            when(has[p], add_y)
            if it + 1 == ITERS:
                for q in range(2):
                    def add_diagonal(q=q):
                        z0 = (NH, HZ)[q]
                        diagonal(it, p, q).wait_recv()
                        cbuf[it, pl.ds(r0, n), z0:z0 + HZ, :] += rybuf[it, p, :, 0:HZ, :]
                    when(both(both(zed_has[2 - q], has[p]), v == 1 - q), add_diagonal)
        for d in range(2):
            z0 = (HZ, NH)[d]

            def add_z(d=d, z0=z0):
                sz(it, d, p).wait_recv()
                cbuf[it, pl.ds(r0, n), z0:z0 + HZ, :] += rzbuf[it, d, pl.ds(r0 - my, n)]
            when(zfrom[d], add_z)

    with scope("Wload"):
        load_start.wait()
    ebuf[0, my:my + NY, HZ:HZ + NH, :] = jnp.transpose(stage[0], (1, 0, 2))
    gather_own(0)
    mine[...] = jnp.zeros_like(mine)
    for k, (raw, taps) in enumerate(((raw_z, KZ), (raw_y, KY), (raw_x, KX))):
        loads[k].wait()
        mine[k:k + 1, 0:taps] = raw[...] / jnp.sum(raw[...], axis=1, keepdims=True)
    swap_prof = pltpu.make_async_remote_copy(
        src_ref=mine, dst_ref=theirs, send_sem=xssem.at[0], recv_sem=xrsem.at[0],
        device_id=partner, device_id_type=MESH)
    swap_prof.start()
    swap_obs = pltpu.make_async_remote_copy(
        src_ref=obs_hbm.at[0, pl.ds((1 - v) * NH, NH)], dst_ref=obs_z.at[v],
        send_sem=xssem.at[1], recv_sem=xrsem.at[1], device_id=partner, device_id_type=MESH)
    swap_obs.start()

    with scope("Wprof"):
        swap_prof.wait()
    own, other = mine[...], theirs[...]
    prof = (jnp.where(v == 0, own, other), jnp.where(v == 0, other, own))

    def tap(view, k, a):
        return prof[view][k:k + 1, a:a + 1]

    rows = lax.broadcasted_iota(jnp.int32, (NE, 3 * NE), 0)
    cols = lax.broadcasted_iota(jnp.int32, (NE, 3 * NE), 1)
    third = cols // NE
    cols = cols - third * NE

    def banded(diff, view, k, taps):
        w = jnp.zeros(diff.shape, F32)
        for a in range(taps):
            w = jnp.where(diff == a, tap(view, k, a), w)
        return w

    off = HZ - mz
    for ref, inner, outer in ((wf, rows, cols), (wb, cols, rows)):
        second = inner >= NH
        diff = outer - jnp.where(second, inner - NH, inner) - off
        w = jnp.where(second, banded(diff, 1, 0, KZ), banded(diff, 0, 0, KZ))
        high, low = split(w)
        ref[...] = jnp.where(third == 2, low.astype(F32), high.astype(F32)).astype(BF16)
    for view in range(2):
        for back in range(2):
            for r0 in range(0, NX, 64):
                r = lax.broadcasted_iota(jnp.int32, (64, NX), 0) + r0
                c = lax.broadcasted_iota(jnp.int32, (64, NX), 1)
                diff = (c - r if back else r - c) + mx
                high, low = split(banded(diff, view, 2, KX))
                tx[view, back, 0, r0:r0 + 64, :] = high
                tx[view, back, 1, r0:r0 + 64, :] = low
    wy = [[jnp.broadcast_to(tap(view, 1, b), (NH, NX)) for b in range(KY)] for view in range(2)]

    qbuf[0:2 * my] = jnp.zeros((2 * my, NE, NX), F32)
    qbuf[2 * my + NY:] = jnp.zeros((2 * my, NE, NX), F32)

    with scope("Wobs"):
        load_obs.wait()
        swap_obs.wait()
    for view in range(2):
        obs_t[view] = jnp.transpose(obs_z[view], (1, 0, 2))

    def xblur(high, low, view, back):
        both_ = jnp.concatenate([high, low], axis=0)
        n = high.shape[0]
        d = jnp.dot(both_, tx[view, back, 0], preferred_element_type=F32)
        d2 = jnp.dot(high, tx[view, back, 1], preferred_element_type=F32)
        return d[:n] + (d[n:] + d2)

    def stacked(x):
        high, low = split(x)
        return jnp.concatenate([high, low, high], axis=0)

    for it in range(ITERS):
        def zrows(i0, n, it=it):
            with scope(f"z{it}_{i0}"):
                r0 = row(i0, n)
                for y in range(n):
                    zbuf[r0 + y] = jnp.dot(wf[...], stacked(ebuf[it, r0 + y]), preferred_element_type=F32)

        def qrows(o0, n, it=it):
            with scope(f"q{it}_{o0}"):
                y0 = row(o0 + my, n) - my
                for view in range(2):
                    z0 = view * NH
                    for y in range(n):
                        acc = wy[view][0] * zbuf[y0 + y, z0:z0 + NH, :]
                        for b in range(1, KY):
                            acc = acc + wy[view][b] * zbuf[y0 + y + b, z0:z0 + NH, :]
                        high, low = split(acc)
                        ybuf[view, 0, y * NH:(y + 1) * NH, :] = high
                        ybuf[view, 1, y * NH:(y + 1) * NH, :] = low
                for view in range(2):
                    z0 = view * NH
                    m = n * NH
                    blurred = xblur(ybuf[view, 0, 0:m], ybuf[view, 1, 0:m], view, 0)
                    quotient = obs_t[view, pl.ds(y0, n)].reshape(m, NX) / blurred
                    high, low = split(quotient)
                    ybuf[view, 2, 0:m] = high
                    ybuf[view, 3, 0:m] = low
                    qbuf[pl.ds(2 * my + y0, n), z0:z0 + NH, :] = xblur(
                        ybuf[view, 2, 0:m], ybuf[view, 3, 0:m], view, 1).reshape(n, NH, NX)

        def crows(i0, n, it=it):
            with scope(f"c{it}_{i0}"):
                r0 = row(i0, n)
                for y in range(n):
                    r = r0 + y
                    parts = []
                    for view in range(2):
                        z0 = view * NH
                        acc = wy[view][0] * qbuf[r + 2 * my, z0:z0 + NH, :]
                        for b in range(1, KY):
                            acc = acc + wy[view][b] * qbuf[r + 2 * my - b, z0:z0 + NH, :]
                        parts.append(acc)
                    cbuf[it, r] = jnp.dot(wb[...], stacked(jnp.concatenate(parts, axis=0)),
                                          preferred_element_type=F32)

        if it == 0:
            with scope("Wg0_in"):
                first_take(0)
            zrows(my + CH, CH)
            with scope("Wge0own"):
                edge_own(it, 0)
            with scope("Wg0_out"):
                first_take(1)
            zrows(my, CH)
        else:
            for p in (1, 2, 3):
                with scope(f"Wg{it}_{p}"):
                    gather_take(it, p)
                zrows(*ROWS[p])

        def low_edge(it=it):
            edge_own(it, 1)
            gather_edge(it, 1)
            zrows(0, my)
        when(has[1], low_edge)
        def low_scatter(it=it):
            crows(0, my)
            scatter_edge(it, 1)

        def high_edge(it=it):
            with scope(f"Wge{it}"):
                gather_edge(it, 0)
            zrows(my + NY, my)

        def high_scatter(it=it):
            crows(my + NY, my)
            scatter_edge(it, 0)

        qrows(0, OUT)
        when(has[1], low_scatter)
        crows(*ROWS[1])
        when(jnp.logical_not(has[1]), functools.partial(scatter_piece, it, 1))
        if it == 0:
            qrows(OUT, MID)
            for p in (2, 3):
                crows(*ROWS[p])
                scatter_piece(it, p)
            when(has[0], high_edge)
            qrows(OUT + MID, my)
            when(has[0], high_scatter)
            crows(*ROWS[4])
            scatter_piece(it, 4)
            crows(*ROWS[0])
            scatter_near(it, 0)
            with scope(f"Wse{it}"):
                scatter_end(it, 0)
            scatter_own(it, 0)
        else:
            with scope(f"Wg{it}_0"):
                gather_take(it, 0)
            zrows(*ROWS[0])
            with scope(f"Wge{it}own"):
                edge_own(it, 0)
            with scope(f"Wg{it}_4"):
                gather_take(it, 4)
            zrows(*ROWS[4])
            qrows(OUT, MID)
            for p in (2, 3):
                crows(*ROWS[p])
                scatter_piece(it, p)
            when(has[0], high_edge)
            qrows(OUT + MID, my)
            when(has[0], high_scatter)
            for p in (0, 4):
                crows(*ROWS[p])
                scatter_piece(it, p)
            with scope(f"Wso{it}"):
                scatter_own(it, 0)

        def low_end(it=it):
            scatter_own(it, 1)
            if it + 1 < ITERS:
                scatter_near(it, 1)
                scatter_end(it, 1)
            else:
                scatter_piece(it, 1)
        when(has[1], low_end)

        def update(p, it=it):
            n = ROWS[p][1]
            r0 = row(*ROWS[p])
            with scope(f"Wst{it}_{p}"):
                scatter_take(it, p)
            new = ebuf[it, pl.ds(r0, n), HZ:HZ + NH, :] * (0.5 * cbuf[it, pl.ds(r0, n), HZ:HZ + NH, :])
            if it + 1 < ITERS:
                ebuf[it + 1, pl.ds(r0, n), HZ:HZ + NH, :] = new
            else:
                zbuf[pl.ds(r0, n), 0:NH, :] = new

        if it + 1 < ITERS:
            for p in (1, 2, 3):
                update(p)
                gather_piece(it + 1, p)
            update(0)
            gather_piece(it + 1, 0)
            gather_own(it + 1)
            update(4)
            gather_piece(it + 1, 4)
        else:
            outs = []
            for n, p in enumerate((1, 2, 3, 4, 0)):
                update(p)
                r0 = row(*ROWS[p])
                rows_ = ROWS[p][1]
                src = zbuf.at[pl.ds(r0, rows_), pl.ds(0, NH)]
                dst = out_hbm.at[pl.ds(r0 - my, rows_), pl.ds(v * NH, NH)]
                outs.append(pltpu.make_async_copy(src, dst, osem.at[n]))
                outs.append(pltpu.make_async_remote_copy(
                    src_ref=src, dst_ref=dst, send_sem=xssem.at[2 + n], recv_sem=xrsem.at[2 + n],
                    device_id=partner, device_id_type=MESH))
                outs[-1].start()
                outs[-2].start()
            with scope("Wout"):
                for out in outs:
                    out.wait()
    for it in range(ITERS):
        sent(it)
    for k in range(2):
        for d in range(2):
            when(zhas[d], first(d, k).wait_send)


def on_device(S, G, observed, start, spread_z, spread_y, spread_x):
    NZ, NY, NX = start.shape
    KZ, KY, KX = spread_z.shape[1], spread_y.shape[1], spread_x.shape[1]
    NH = NZ // 2
    my = KY // 2
    HZ = -(-(KZ // 2) // 8) * 8
    NE, NR = NH + 2 * HZ, NY + 2 * my
    dims = (NH, NY, NX, HZ, KZ, KY, KX, S, G)
    vm = pltpu.VMEM
    hbm = pl.BlockSpec(memory_space=pltpu.HBM)
    out = pl.pallas_call(
        functools.partial(kernel, dims),
        out_shape=jax.ShapeDtypeStruct((NY, NZ, NX), F32),
        in_specs=[hbm] * 5,
        out_specs=hbm,
        scratch_shapes=[
            vm((1, KZ), F32), vm((1, KY), F32), vm((1, KX), F32),
            vm((1, NH, NY, NX), F32), vm((2, HZ, NY, NX), F32),
            vm((2, NH, NY, NX), F32), vm((2, NY, NH, NX), F32),
            vm((8, 128), F32), vm((8, 128), F32),
            vm((NE, 3 * NE), BF16), vm((NE, 3 * NE), BF16), vm((2, 2, 2, NX, NX), BF16),
            vm((NR, NE, NX), F32), vm((2, 4, NY // 2 * NH, NX), BF16), vm((NY + 4 * my, NE, NX), F32),
            vm((ITERS, NR, NE, NX), F32), vm((ITERS, NR, NE, NX), F32),
            vm((ITERS, 2, my, NE, NX), F32), vm((ITERS, 2, NY, HZ, NX), F32), vm((ITERS, 2, my, HZ, NX), F32),
            pltpu.SemaphoreType.DMA((6,)), pltpu.SemaphoreType.DMA((5,)),
            pltpu.SemaphoreType.DMA((2, 2)), pltpu.SemaphoreType.DMA((2, 2)),
            pltpu.SemaphoreType.DMA((2 * ITERS, 20)), pltpu.SemaphoreType.DMA((2 * ITERS, 20)),
            pltpu.SemaphoreType.DMA((7,)), pltpu.SemaphoreType.DMA((7,)),
        ],
        compiler_params=pltpu.CompilerParams(
            collective_id=0, has_side_effects=True, vmem_limit_bytes=67043328),
    )(observed, start, spread_z, spread_y, spread_x)
    return jnp.transpose(out, (1, 0, 2))


def solution(mesh):
    S, G = 2 * mesh.shape["gz"], mesh.shape["gy"]
    return jax.shard_map(
        functools.partial(on_device, S, G),
        mesh=mesh,
        in_specs=(
            P("view", "gz", "gy", None),
            P("gz", "gy", None),
            P("view", None),
            P("view", None),
            P("view", None),
        ),
        out_specs=P("gz", "gy", None),
        check_vma=False,
    )
```

```python
import contextlib
import functools

import jax
import jax.numpy as jnp
from jax import lax
from jax.experimental import pallas as pl
from jax.experimental.pallas import tpu as pltpu
from jax.sharding import PartitionSpec as P

ITERS = 2
MESH = pl.DeviceIdType.MESH
F32 = jnp.float32
BF16 = jnp.bfloat16


def scope(name):
    return contextlib.nullcontext()


def split(x):
    high = x.astype(BF16)
    return high, (x - high.astype(F32)).astype(BF16)


def kernel(dims, obs_hbm, start_hbm, sz_ref, sy_ref, sx_ref, out_hbm,
           raw_z, raw_y, raw_x, stage, land, obs_z, obs_t, mine, theirs, wf, wb, tx, zbuf, ybuf, qbuf,
           ebuf, cbuf, rybuf, rzbuf, sbuf, lsem, osem, gsem, hsem, ssem, rsem, xssem, xrsem):
    NH, NY, NX, HZ, KZ, KY, KX, S, G = dims
    my, mz, mx = KY // 2, KZ // 2, KX // 2
    NE, NR, NQ = NH + 2 * HZ, NY + 2 * my, NY + 4 * my
    CH = NY // 2
    v = lax.axis_index("view")
    gy = lax.axis_index("gy")
    s = 2 * lax.axis_index("gz") + v
    up_z, dn_z = s < S - 1, s > 0
    up_y, dn_y = gy < G - 1, gy > 0
    f = lax.rem(gy, 2)
    has = (jnp.logical_or(jnp.logical_and(f == 0, up_y), jnp.logical_and(f == 1, dn_y)),
           jnp.logical_or(jnp.logical_and(f == 0, dn_y), jnp.logical_and(f == 1, up_y)))

    def row(i0, n=1):
        return i0 + f * (NR - 2 * i0 - n)

    def qrow(j0, n=1):
        return j0 + f * (NQ - 2 * j0 - n)

    def zdev(t):
        t = lax.rem(t + S, S)
        return {"view": lax.rem(t, 2), "gz": t // 2}

    zto = (zdev(s + 1), zdev(s - 1))
    step = 1 - 2 * f
    yto = ({"gy": lax.rem(gy + step + G, G)}, {"gy": lax.rem(gy - step + G, G)})
    partner = {"view": 1 - v}
    zout = dict(zdev(s - 1 + 2 * v))
    diag = tuple({**zout, **yto[d]} for d in range(2))
    zhas, zfrom = (up_z, dn_z), (dn_z, up_z)

    def when(cond, fn):
        @pl.when(cond)
        def _():
            fn()

    def both(a, b):
        return jnp.logical_and(a, b)

    barrier = pltpu.get_barrier_semaphore()
    greet = ((up_z, zto[0]), (dn_z, zto[1]), (has[0], yto[0]), (has[1], yto[1]))
    for there, to in greet:
        @pl.when(there)
        def _(to=to):
            pl.semaphore_signal(barrier, inc=1, device_id=to, device_id_type=MESH)

    load_start = pltpu.make_async_copy(start_hbm.at[pl.ds(v * NH, NH)], stage.at[0], lsem.at[0])
    load_start.start()
    load_obs = pltpu.make_async_copy(obs_hbm.at[0, pl.ds(v * NH, NH)], obs_z.at[v], lsem.at[1])
    load_obs.start()
    loads = [pltpu.make_async_copy(ref, raw, lsem.at[3 + k])
             for k, (ref, raw) in enumerate(((sz_ref, raw_z), (sy_ref, raw_y), (sx_ref, raw_x)))]
    for load in loads:
        load.start()

    blocks = (CH * (1 - f), CH * f)

    def first(d, k):
        b0 = pl.multiple_of(blocks[k], CH)
        src0 = v * NH + (NH - mz, 0)[d]
        dst0 = (HZ - mz, 0)[d]
        return pltpu.make_async_remote_copy(
            src_ref=start_hbm.at[pl.ds(src0, mz), pl.ds(b0, CH)],
            dst_ref=land.at[d, pl.ds(dst0, mz), pl.ds(b0, CH)],
            send_sem=gsem.at[d, k], recv_sem=hsem.at[d, k], device_id=zto[d], device_id_type=MESH)

    peers = sum(there.astype(jnp.int32) for there, _ in greet)
    with scope("Wbar"):
        pl.semaphore_wait(barrier, peers)
    for k in range(2):
        for d in range(2):
            when(zhas[d], first(d, k).start)

    land[0, 0:HZ - mz] = jnp.zeros((HZ - mz, NY, NX), F32)
    land[1, mz:HZ] = jnp.zeros((HZ - mz, NY, NX), F32)
    for d in range(2):
        def blank(d=d):
            for it in range(ITERS):
                z0 = (0, HZ + NH)[d]
                ebuf[it, :, z0:z0 + HZ, :] = jnp.zeros((NR, HZ, NX), F32)
        when(jnp.logical_not(zfrom[d]), blank)

        def blank_rows(d=d):
            zbuf[pl.ds(row((my + NY, 0)[d], my), my)] = jnp.zeros((my, NE, NX), F32)
        when(jnp.logical_not(has[d]), blank_rows)

    def copy(phase, m, src, dst, to):
        return pltpu.make_async_remote_copy(
            src_ref=src, dst_ref=dst, send_sem=ssem.at[phase, m], recv_sem=rsem.at[phase, m],
            device_id=to, device_id_type=MESH)

    ROWS = ((NY, my), (my, my), (2 * my, NY - 4 * my), (NY - 2 * my, my), (NY - my, my))
    OUT, MID = NY - 3 * my, 2 * my
    NP = len(ROWS)
    ZED = ((HZ, NH), (0, HZ), (HZ + NH, HZ))
    zed_has = (None, dn_z, up_z)
    EDGE, HALO = (NY, my), (my + NY, 0)
    THERE = (f * (my + NY), (1 - f) * (my + NY))

    def gz(it, d, p):
        e = ebuf.at[it]
        src0, dst0 = ((NH, 0), (HZ, HZ + NH))[d]
        n = ROWS[p][1]
        r0 = row(*ROWS[p])
        return copy(2 * it, NP * d + p, e.at[pl.ds(r0, n), pl.ds(src0, HZ)],
                    e.at[pl.ds(r0, n), pl.ds(dst0, HZ)], zto[d])

    def gyc(it, d, p):
        e = ebuf.at[it]
        z0, n = ZED[p]
        return copy(2 * it, 2 * NP + 3 * d + p, e.at[pl.ds(row(EDGE[d], my), my), pl.ds(z0, n)],
                    e.at[pl.ds(THERE[d], my), pl.ds(z0, n)], yto[d])

    def fwd(it, d, q):
        rows_ = pl.ds(row(HALO[d], my), my)
        e = ebuf.at[it]
        return copy(2 * it, 2 * NP + 6 + 2 * d + q, e.at[rows_, pl.ds((NH, HZ)[q], HZ)],
                    e.at[rows_, pl.ds((0, HZ + NH)[q], HZ)], partner)

    def sfwd(it, d, q):
        rows_ = pl.ds(row(HALO[d], my), my)
        return copy(2 * it + 1, 2 * NP + 6 + 2 * d + q, cbuf.at[it, rows_, pl.ds((HZ + NH, 0)[q], HZ)],
                    sbuf.at[it, d], partner)

    def diagonal(it, d, q):
        z0, n = ZED[1 + q]
        return copy(2 * it + 1, 2 * NP + 3 * d + 1 + q, cbuf.at[it, pl.ds(row(HALO[d], my), my), pl.ds(z0, n)],
                    rybuf.at[it, d, :, pl.ds(0, HZ)], diag[d])

    def sz(it, d, p):
        src0 = (HZ + NH, 0)[d]
        n = ROWS[p][1]
        r0 = row(*ROWS[p])
        return copy(2 * it + 1, NP * d + p, cbuf.at[it, pl.ds(r0, n), pl.ds(src0, HZ)],
                    rzbuf.at[it, d, pl.ds(r0 - my, n)], zto[d])

    def sy(it, d, p):
        z0, n = ZED[p]
        return copy(2 * it + 1, 2 * NP + 3 * d + p, cbuf.at[it, pl.ds(row(HALO[d], my), my), pl.ds(z0, n)],
                    rybuf.at[it, d, :, pl.ds(z0, n)], yto[d])

    def gather_piece(it, p):
        for d in range(2):
            when(zhas[d], gz(it, d, p).start)

    def gather_own(it):
        for d in range(2):
            when(has[d], gyc(it, d, 0).start)

    def relay(it, p, d):
        if p < 2:
            when(both(both(zfrom[d], has[p]), v == d), gyc(it, p, 1 + d).start)

    def gather_take(it, p):
        for d in range(2):
            when(zfrom[d], gz(it, d, p).wait_recv)
            relay(it, p, d)

    def first_take(k):
        b0 = pl.multiple_of(blocks[k], CH)
        for d in range(2):
            z0 = (0, HZ + NH)[d]

            def take(d=d, z0=z0):
                first(d, k).wait_recv()
                ebuf[0, pl.ds(my + b0, CH), z0:z0 + HZ, :] = jnp.transpose(land[d, :, pl.ds(b0, CH), :], (1, 0, 2))
            when(zfrom[d], take)
            relay(0, k, d)

    def edge_own(it, d):
        def go():
            gyc(it, d, 0).wait_recv()
            for q in range(2):
                when(v == q, fwd(it, d, q).start)
        when(has[d], go)

    def gather_edge(it, d):
        for q in range(2):
            when(both(both(zed_has[1 + q], has[d]), v == q), gyc(it, d, 1 + q).wait_recv)
            when(both(has[d], v == 1 - q), fwd(it, d, q).wait_recv)

    def sent(it):
        for d in range(2):
            for p in range(NP):
                if it > 0:
                    when(zhas[d], gz(it, d, p).wait_send)
                when(zhas[d], sz(it, d, p).wait_send)
            for y in (gyc, sy):
                when(has[d], y(it, d, 0).wait_send)
                for q in range(2):
                    corner = diagonal(it, d, q) if y is sy and it + 1 == ITERS else y(it, d, 1 + q)
                    when(both(both(zed_has[1 + q], has[d]), v == q), corner.wait_send)
            for y in (fwd, sfwd):
                for q in range(2):
                    when(both(has[d], v == q), y(it, d, q).wait_send)

    def scatter_edge(it, d):
        for q in range(2):
            corner = diagonal(it, d, q) if it + 1 == ITERS else sy(it, d, 1 + q)
            when(both(both(zed_has[1 + q], has[d]), v == q), corner.start)
            when(both(has[d], v == q), sfwd(it, d, q).start)

    def scatter_own(it, d):
        r0 = row(HALO[d], my)
        for q in range(2):
            def add(q=q):
                z0 = (HZ, NH)[q]
                sfwd(it, d, q).wait_recv()
                cbuf[it, pl.ds(r0, my), z0:z0 + HZ, :] += sbuf[it, d]
            when(both(has[d], v == 1 - q), add)
        when(has[d], sy(it, d, 0).start)

    def scatter_piece(it, p):
        for d in range(2):
            when(zhas[d], sz(it, d, p).start)

    def scatter_end(it, p):
        r0 = row(*ROWS[p])
        for q in range(2):
            z0 = ZED[1 + q][0]

            def add(q=q, z0=z0):
                sy(it, p, 1 + q).wait_recv()
                cbuf[it, pl.ds(r0, my), z0:z0 + HZ, :] += rybuf[it, p, :, z0:z0 + HZ, :]
            when(both(both(zed_has[1 + q], has[p]), v == q), add)
            when(both(zed_has[1 + q], v == q), sz(it, 1 - q, p).start)

    def scatter_near(it, p):
        for q in range(2):
            when(v == 1 - q, sz(it, 1 - q, p).start)

    def scatter_take(it, p):
        n = ROWS[p][1]
        r0 = row(*ROWS[p])
        if p < 2:
            def add_y():
                sy(it, p, 0).wait_recv()
                cbuf[it, pl.ds(r0, n), HZ:HZ + NH, :] += rybuf[it, p, :, HZ:HZ + NH, :]
            when(has[p], add_y)
            if it + 1 == ITERS:
                for q in range(2):
                    def add_diagonal(q=q):
                        z0 = (NH, HZ)[q]
                        diagonal(it, p, q).wait_recv()
                        cbuf[it, pl.ds(r0, n), z0:z0 + HZ, :] += rybuf[it, p, :, 0:HZ, :]
                    when(both(both(zed_has[2 - q], has[p]), v == 1 - q), add_diagonal)
        for d in range(2):
            z0 = (HZ, NH)[d]

            def add_z(d=d, z0=z0):
                sz(it, d, p).wait_recv()
                cbuf[it, pl.ds(r0, n), z0:z0 + HZ, :] += rzbuf[it, d, pl.ds(r0 - my, n)]
            when(zfrom[d], add_z)

    with scope("Wload"):
        load_start.wait()
    ebuf[0, my:my + NY, HZ:HZ + NH, :] = jnp.transpose(stage[0], (1, 0, 2))
    gather_own(0)
    mine[...] = jnp.zeros_like(mine)
    for k, (raw, taps) in enumerate(((raw_z, KZ), (raw_y, KY), (raw_x, KX))):
        loads[k].wait()
        mine[k:k + 1, 0:taps] = raw[...] / jnp.sum(raw[...], axis=1, keepdims=True)
    swap_prof = pltpu.make_async_remote_copy(
        src_ref=mine, dst_ref=theirs, send_sem=xssem.at[0], recv_sem=xrsem.at[0],
        device_id=partner, device_id_type=MESH)
    swap_prof.start()
    swap_obs = pltpu.make_async_remote_copy(
        src_ref=obs_hbm.at[0, pl.ds((1 - v) * NH, NH)], dst_ref=obs_z.at[v],
        send_sem=xssem.at[1], recv_sem=xrsem.at[1], device_id=partner, device_id_type=MESH)
    swap_obs.start()

    with scope("Wprof"):
        swap_prof.wait()
    own, other = mine[...], theirs[...]
    prof = (jnp.where(v == 0, own, other), jnp.where(v == 0, other, own))

    def tap(view, k, a):
        return prof[view][k:k + 1, a:a + 1]

    rows = lax.broadcasted_iota(jnp.int32, (NE, 3 * NE), 0)
    cols = lax.broadcasted_iota(jnp.int32, (NE, 3 * NE), 1)
    third = cols // NE
    cols = cols - third * NE

    def banded(diff, view, k, taps):
        w = jnp.zeros(diff.shape, F32)
        for a in range(taps):
            w = jnp.where(diff == a, tap(view, k, a), w)
        return w

    off = HZ - mz
    for ref, inner, outer in ((wf, rows, cols), (wb, cols, rows)):
        second = inner >= NH
        diff = outer - jnp.where(second, inner - NH, inner) - off
        w = jnp.where(second, banded(diff, 1, 0, KZ), banded(diff, 0, 0, KZ))
        high, low = split(w)
        ref[...] = jnp.where(third == 2, low.astype(F32), high.astype(F32)).astype(BF16)
    for view in range(2):
        for back in range(2):
            for r0 in range(0, NX, 64):
                r = lax.broadcasted_iota(jnp.int32, (64, NX), 0) + r0
                c = lax.broadcasted_iota(jnp.int32, (64, NX), 1)
                diff = (c - r if back else r - c) + mx
                high, low = split(banded(diff, view, 2, KX))
                tx[view, back, 0, r0:r0 + 64, :] = high
                tx[view, back, 1, r0:r0 + 64, :] = low
    wy = [[jnp.broadcast_to(tap(view, 1, b), (NH, NX)) for b in range(KY)] for view in range(2)]

    qbuf[0:2 * my] = jnp.zeros((2 * my, NE, NX), F32)
    qbuf[2 * my + NY:] = jnp.zeros((2 * my, NE, NX), F32)

    with scope("Wobs"):
        load_obs.wait()
        swap_obs.wait()
    for view in range(2):
        obs_t[view] = jnp.transpose(obs_z[view], (1, 0, 2))

    def xblur(high, low, view, back):
        both_ = jnp.concatenate([high, low], axis=0)
        n = high.shape[0]
        d = jnp.dot(both_, tx[view, back, 0], preferred_element_type=F32)
        d2 = jnp.dot(high, tx[view, back, 1], preferred_element_type=F32)
        return d[:n] + (d[n:] + d2)

    def stacked(x):
        high, low = split(x)
        return jnp.concatenate([high, low, high], axis=0)

    for it in range(ITERS):
        def zrows(i0, n, it=it):
            with scope(f"z{it}_{i0}"):
                r0 = row(i0, n)
                for y in range(n):
                    zbuf[r0 + y] = jnp.dot(wf[...], stacked(ebuf[it, r0 + y]), preferred_element_type=F32)

        def qrows(o0, n, it=it):
            with scope(f"q{it}_{o0}"):
                y0 = row(o0 + my, n) - my
                for view in range(2):
                    z0 = view * NH
                    for y in range(n):
                        acc = wy[view][0] * zbuf[y0 + y, z0:z0 + NH, :]
                        for b in range(1, KY):
                            acc = acc + wy[view][b] * zbuf[y0 + y + b, z0:z0 + NH, :]
                        high, low = split(acc)
                        ybuf[view, 0, y * NH:(y + 1) * NH, :] = high
                        ybuf[view, 1, y * NH:(y + 1) * NH, :] = low
                for view in range(2):
                    z0 = view * NH
                    m = n * NH
                    blurred = xblur(ybuf[view, 0, 0:m], ybuf[view, 1, 0:m], view, 0)
                    quotient = obs_t[view, pl.ds(y0, n)].reshape(m, NX) / blurred
                    high, low = split(quotient)
                    ybuf[view, 2, 0:m] = high
                    ybuf[view, 3, 0:m] = low
                    qbuf[pl.ds(2 * my + y0, n), z0:z0 + NH, :] = xblur(
                        ybuf[view, 2, 0:m], ybuf[view, 3, 0:m], view, 1).reshape(n, NH, NX)

        def crows(i0, n, it=it):
            with scope(f"c{it}_{i0}"):
                r0 = row(i0, n)
                for y in range(n):
                    r = r0 + y
                    parts = []
                    for view in range(2):
                        z0 = view * NH
                        acc = wy[view][0] * qbuf[r + 2 * my, z0:z0 + NH, :]
                        for b in range(1, KY):
                            acc = acc + wy[view][b] * qbuf[r + 2 * my - b, z0:z0 + NH, :]
                        parts.append(acc)
                    cbuf[it, r] = jnp.dot(wb[...], stacked(jnp.concatenate(parts, axis=0)),
                                          preferred_element_type=F32)

        if it == 0:
            with scope("Wg0_in"):
                first_take(0)
            zrows(my + CH, CH)
            with scope("Wge0own"):
                edge_own(it, 0)
            with scope("Wg0_out"):
                first_take(1)
            zrows(my, CH)
        else:
            for p in (1, 2, 3):
                with scope(f"Wg{it}_{p}"):
                    gather_take(it, p)
                zrows(*ROWS[p])

        def low_edge(it=it):
            edge_own(it, 1)
            gather_edge(it, 1)
            zrows(0, my)
        when(has[1], low_edge)
        def low_scatter(it=it):
            crows(0, my)
            scatter_edge(it, 1)

        def high_edge(it=it):
            with scope(f"Wge{it}"):
                gather_edge(it, 0)
            zrows(my + NY, my)

        def high_scatter(it=it):
            crows(my + NY, my)
            scatter_edge(it, 0)

        qrows(0, OUT)
        when(has[1], low_scatter)
        crows(*ROWS[1])
        when(jnp.logical_not(has[1]), functools.partial(scatter_piece, it, 1))
        if it == 0:
            qrows(OUT, MID)
            for p in (2, 3):
                crows(*ROWS[p])
                scatter_piece(it, p)
            when(has[0], high_edge)
            qrows(OUT + MID, my)
            when(has[0], high_scatter)
            crows(*ROWS[4])
            scatter_piece(it, 4)
            crows(*ROWS[0])
            scatter_near(it, 0)
            with scope(f"Wse{it}"):
                scatter_end(it, 0)
            scatter_own(it, 0)
        else:
            with scope(f"Wg{it}_0"):
                gather_take(it, 0)
            zrows(*ROWS[0])
            with scope(f"Wge{it}own"):
                edge_own(it, 0)
            with scope(f"Wg{it}_4"):
                gather_take(it, 4)
            zrows(*ROWS[4])
            qrows(OUT, MID)
            for p in (2, 3):
                crows(*ROWS[p])
                scatter_piece(it, p)
            when(has[0], high_edge)
            qrows(OUT + MID, my)
            when(has[0], high_scatter)
            for p in (0, 4):
                crows(*ROWS[p])
                scatter_piece(it, p)
            with scope(f"Wso{it}"):
                scatter_own(it, 0)

        def low_end(it=it):
            scatter_own(it, 1)
            if it + 1 < ITERS:
                scatter_near(it, 1)
                scatter_end(it, 1)
            else:
                scatter_piece(it, 1)
        when(has[1], low_end)

        def update(p, it=it):
            n = ROWS[p][1]
            r0 = row(*ROWS[p])
            with scope(f"Wst{it}_{p}"):
                scatter_take(it, p)
            new = ebuf[it, pl.ds(r0, n), HZ:HZ + NH, :] * (0.5 * cbuf[it, pl.ds(r0, n), HZ:HZ + NH, :])
            if it + 1 < ITERS:
                ebuf[it + 1, pl.ds(r0, n), HZ:HZ + NH, :] = new
            else:
                zbuf[pl.ds(r0, n), 0:NH, :] = new

        if it + 1 < ITERS:
            for p in (1, 2, 3):
                update(p)
                gather_piece(it + 1, p)
            update(0)
            gather_piece(it + 1, 0)
            gather_own(it + 1)
            update(4)
            gather_piece(it + 1, 4)
        else:
            outs = []
            for n, p in enumerate((1, 2, 3, 4, 0)):
                update(p)
                r0 = row(*ROWS[p])
                rows_ = ROWS[p][1]
                src = zbuf.at[pl.ds(r0, rows_), pl.ds(0, NH)]
                dst = out_hbm.at[pl.ds(r0 - my, rows_), pl.ds(v * NH, NH)]
                outs.append(pltpu.make_async_copy(src, dst, osem.at[n]))
                outs.append(pltpu.make_async_remote_copy(
                    src_ref=src, dst_ref=dst, send_sem=xssem.at[2 + n], recv_sem=xrsem.at[2 + n],
                    device_id=partner, device_id_type=MESH))
                outs[-1].start()
                outs[-2].start()
            with scope("Wout"):
                for out in outs:
                    out.wait()
    for it in range(ITERS):
        sent(it)
    for k in range(2):
        for d in range(2):
            when(zhas[d], first(d, k).wait_send)


def on_device(S, G, observed, start, spread_z, spread_y, spread_x):
    NZ, NY, NX = start.shape
    KZ, KY, KX = spread_z.shape[1], spread_y.shape[1], spread_x.shape[1]
    NH = NZ // 2
    my = KY // 2
    HZ = -(-(KZ // 2) // 8) * 8
    NE, NR = NH + 2 * HZ, NY + 2 * my
    dims = (NH, NY, NX, HZ, KZ, KY, KX, S, G)
    vm = pltpu.VMEM
    hbm = pl.BlockSpec(memory_space=pltpu.HBM)
    out = pl.pallas_call(
        functools.partial(kernel, dims),
        out_shape=jax.ShapeDtypeStruct((NY, NZ, NX), F32),
        in_specs=[hbm] * 5,
        out_specs=pl.BlockSpec(memory_space=pl.ANY),
        scratch_shapes=[
            vm((1, KZ), F32), vm((1, KY), F32), vm((1, KX), F32),
            vm((1, NH, NY, NX), F32), vm((2, HZ, NY, NX), F32),
            vm((2, NH, NY, NX), F32), vm((2, NY, NH, NX), F32),
            vm((8, 128), F32), vm((8, 128), F32),
            vm((NE, 3 * NE), BF16), vm((NE, 3 * NE), BF16), vm((2, 2, 2, NX, NX), BF16),
            vm((NR, NE, NX), F32), vm((2, 4, NY // 2 * NH, NX), BF16), vm((NY + 4 * my, NE, NX), F32),
            vm((ITERS, NR, NE, NX), F32), vm((ITERS, NR, NE, NX), F32),
            vm((ITERS, 2, my, NE, NX), F32), vm((ITERS, 2, NY, HZ, NX), F32), vm((ITERS, 2, my, HZ, NX), F32),
            pltpu.SemaphoreType.DMA((6,)), pltpu.SemaphoreType.DMA((5,)),
            pltpu.SemaphoreType.DMA((2, 2)), pltpu.SemaphoreType.DMA((2, 2)),
            pltpu.SemaphoreType.DMA((2 * ITERS, 20)), pltpu.SemaphoreType.DMA((2 * ITERS, 20)),
            pltpu.SemaphoreType.DMA((7,)), pltpu.SemaphoreType.DMA((7,)),
        ],
        compiler_params=pltpu.CompilerParams(
            collective_id=0, has_side_effects=True, vmem_limit_bytes=24 << 20),
    )(*(pltpu.with_memory_space_constraint(x, pltpu.HBM) for x in (observed, start, spread_z, spread_y, spread_x)))
    return jnp.transpose(out, (1, 0, 2))


def solution(mesh):
    S, G = 2 * mesh.shape["gz"], mesh.shape["gy"]
    return jax.shard_map(
        functools.partial(on_device, S, G),
        mesh=mesh,
        in_specs=(
            P("view", "gz", "gy", None),
            P("gz", "gy", None),
            P("view", None),
            P("view", None),
            P("view", None),
        ),
        out_specs=P("gz", "gy", None),
        check_vma=False,
    )
```

```python
import contextlib
import functools

import jax
import jax.numpy as jnp
from jax import lax
from jax.experimental import pallas as pl
from jax.experimental.pallas import tpu as pltpu
from jax.sharding import PartitionSpec as P

ITERS = 2
MESH = pl.DeviceIdType.MESH
F32 = jnp.float32
BF16 = jnp.bfloat16


def scope(name):
    return contextlib.nullcontext()


def split(x):
    high = x.astype(BF16)
    return high, (x - high.astype(F32)).astype(BF16)


def kernel(dims, obs_hbm, start_hbm, sz_ref, sy_ref, sx_ref, out_hbm,
           raw_z, raw_y, raw_x, stage, land, obs_z, obs_t, mine, theirs, wf, wb, tx, zbuf, ybuf, qbuf,
           ebuf, cbuf, rybuf, rzbuf, sbuf, lsem, ssem, rsem, xssem, xrsem):
    NH, NY, NX, HZ, KZ, KY, KX, S, G = dims
    my, mz, mx = KY // 2, KZ // 2, KX // 2
    NE, NR, NQ = NH + 2 * HZ, NY + 2 * my, NY + 4 * my
    CH, NP = NY // 2, 5
    v = lax.axis_index("view")
    gy = lax.axis_index("gy")
    s = 2 * lax.axis_index("gz") + v
    up_z, dn_z = s < S - 1, s > 0
    up_y, dn_y = gy < G - 1, gy > 0
    f = lax.rem(gy, 2)
    has = (jnp.logical_or(jnp.logical_and(f == 0, up_y), jnp.logical_and(f == 1, dn_y)),
           jnp.logical_or(jnp.logical_and(f == 0, dn_y), jnp.logical_and(f == 1, up_y)))

    def row(i0, n=1):
        return i0 + f * (NR - 2 * i0 - n)

    def qrow(j0, n=1):
        return j0 + f * (NQ - 2 * j0 - n)

    def zdev(t):
        t = lax.rem(t + S, S)
        return {"view": lax.rem(t, 2), "gz": t // 2}

    zto = (zdev(s + 1), zdev(s - 1))
    step = 1 - 2 * f
    yto = ({"gy": lax.rem(gy + step + G, G)}, {"gy": lax.rem(gy - step + G, G)})
    partner = {"view": 1 - v}
    zout = dict(zdev(s - 1 + 2 * v))
    diag = tuple({**zout, **yto[d]} for d in range(2))
    zhas, zfrom = (up_z, dn_z), (dn_z, up_z)

    def when(cond, fn):
        @pl.when(cond)
        def _():
            fn()

    def both(a, b):
        return jnp.logical_and(a, b)

    barrier = pltpu.get_barrier_semaphore()
    greet = ((up_z, zto[0]), (dn_z, zto[1]), (has[0], yto[0]), (has[1], yto[1]))
    for there, to in greet:
        @pl.when(there)
        def _(to=to):
            pl.semaphore_signal(barrier, inc=1, device_id=to, device_id_type=MESH)

    load_start = pltpu.make_async_copy(start_hbm.at[pl.ds(v * NH, NH)], stage.at[0], lsem.at[0])
    load_start.start()
    load_obs = pltpu.make_async_copy(obs_hbm.at[0, pl.ds(v * NH, NH)], obs_z.at[v], lsem.at[1])
    load_obs.start()
    loads = [pltpu.make_async_copy(ref, raw, lsem.at[2 + k])
             for k, (ref, raw) in enumerate(((sz_ref, raw_z), (sy_ref, raw_y), (sx_ref, raw_x)))]
    for load in loads:
        load.start()

    blocks = (CH * (1 - f), CH * f)

    def first(d, k):
        b0 = pl.multiple_of(blocks[k], CH)
        src0 = v * NH + (NH - mz, 0)[d]
        dst0 = (HZ - mz, 0)[d]
        return pltpu.make_async_remote_copy(
            src_ref=start_hbm.at[pl.ds(src0, mz), pl.ds(b0, CH)],
            dst_ref=land.at[d, pl.ds(dst0, mz), pl.ds(b0, CH)],
            send_sem=ssem.at[NP * d + k], recv_sem=rsem.at[NP * d + k], device_id=zto[d], device_id_type=MESH)

    peers = sum(there.astype(jnp.int32) for there, _ in greet)
    with scope("Wbar"):
        pl.semaphore_wait(barrier, peers)
    for k in range(2):
        for d in range(2):
            when(zhas[d], first(d, k).start)

    land[0, 0:HZ - mz] = jnp.zeros((HZ - mz, NY, NX), F32)
    land[1, mz:HZ] = jnp.zeros((HZ - mz, NY, NX), F32)
    for d in range(2):
        def blank(d=d):
            for it in range(ITERS):
                z0 = (0, HZ + NH)[d]
                ebuf[it, :, z0:z0 + HZ, :] = jnp.zeros((NR, HZ, NX), F32)
        when(jnp.logical_not(zfrom[d]), blank)

        def blank_rows(d=d):
            zbuf[pl.ds(row((my + NY, 0)[d], my), my)] = jnp.zeros((my, NE, NX), F32)
        when(jnp.logical_not(has[d]), blank_rows)

    def copy(send, recv, src, dst, to):
        return pltpu.make_async_remote_copy(
            src_ref=src, dst_ref=dst, send_sem=ssem.at[send], recv_sem=rsem.at[recv],
            device_id=to, device_id_type=MESH)

    ROWS = ((NY, my), (my, my), (2 * my, NY - 4 * my), (NY - 2 * my, my), (NY - my, my))
    OUT, MID = NY - 3 * my, 2 * my
    assert len(ROWS) == NP
    ZED = ((HZ, NH), (0, HZ), (HZ + NH, HZ))
    zed_has = (None, dn_z, up_z)
    EDGE, HALO = (NY, my), (my + NY, 0)
    THERE = (f * (my + NY), (1 - f) * (my + NY))

    def gz(it, d, p):
        e = ebuf.at[it]
        src0, dst0 = ((NH, 0), (HZ, HZ + NH))[d]
        n = ROWS[p][1]
        r0 = row(*ROWS[p])
        return copy(NP * d + p, NP * d + p, e.at[pl.ds(r0, n), pl.ds(src0, HZ)],
                    e.at[pl.ds(r0, n), pl.ds(dst0, HZ)], zto[d])

    def gyc(it, d, p):
        e = ebuf.at[it]
        z0, n = ZED[p]
        k = 2 * min(p, 1) + d
        return copy(2 * NP + k, 4 * NP + k, e.at[pl.ds(row(EDGE[d], my), my), pl.ds(z0, n)],
                    e.at[pl.ds(THERE[d], my), pl.ds(z0, n)], yto[d])

    def fwd(it, d, q):
        rows_ = pl.ds(row(HALO[d], my), my)
        e = ebuf.at[it]
        return copy(2 * NP + 4 + d, 4 * NP + 4 + d, e.at[rows_, pl.ds((NH, HZ)[q], HZ)],
                    e.at[rows_, pl.ds((0, HZ + NH)[q], HZ)], partner)

    def sfwd(it, d, q):
        rows_ = pl.ds(row(HALO[d], my), my)
        return copy(2 * NP + 4 + d, 4 * NP + 10 + d, cbuf.at[it, rows_, pl.ds((HZ + NH, 0)[q], HZ)],
                    sbuf.at[it, d], partner)

    def diagonal(it, d, q):
        z0, n = ZED[1 + q]
        return copy(2 * NP + 2 + d, 4 * NP + 8 + d, cbuf.at[it, pl.ds(row(HALO[d], my), my), pl.ds(z0, n)],
                    rybuf.at[it, d, :, pl.ds(0, HZ)], diag[d])

    def sz(it, d, p):
        src0 = (HZ + NH, 0)[d]
        n = ROWS[p][1]
        r0 = row(*ROWS[p])
        return copy(NP * d + p, 2 * NP + NP * d + p, cbuf.at[it, pl.ds(r0, n), pl.ds(src0, HZ)],
                    rzbuf.at[it, d, pl.ds(r0 - my, n)], zto[d])

    def sy(it, d, p):
        z0, n = ZED[p]
        k = 2 * min(p, 1) + d
        return copy(2 * NP + k, 4 * NP + 6 + k, cbuf.at[it, pl.ds(row(HALO[d], my), my), pl.ds(z0, n)],
                    rybuf.at[it, d, :, pl.ds(z0, n)], yto[d])

    def follow(before, now):
        if before is not None:
            before.wait_send()
        now.start()

    def send_gz(it, d, p):
        follow(sz(it - 1, d, p), gz(it, d, p))

    def send_sz(it, d, p):
        follow(gz(it, d, p) if it > 0 else first(d, p) if p < 2 else None, sz(it, d, p))

    def send_gy(it, d, p):
        follow(sy(it - 1, d, p) if it > 0 else None, gyc(it, d, p))

    def send_sy(it, d, p):
        now = diagonal(it, d, p - 1) if p > 0 and it + 1 == ITERS else sy(it, d, p)
        follow(gyc(it, d, p), now)

    def send_fwd(it, d, q):
        follow(sfwd(it - 1, d, q) if it > 0 else None, fwd(it, d, q))

    def send_sfwd(it, d, q):
        follow(fwd(it, d, q), sfwd(it, d, q))

    def gather_piece(it, p):
        for d in range(2):
            when(zhas[d], functools.partial(send_gz, it, d, p))

    def gather_own(it):
        for d in range(2):
            when(has[d], functools.partial(send_gy, it, d, 0))

    def relay(it, p, d):
        if p < 2:
            when(both(both(zfrom[d], has[p]), v == d), functools.partial(send_gy, it, p, 1 + d))

    def gather_take(it, p):
        for d in range(2):
            when(zfrom[d], gz(it, d, p).wait_recv)
            relay(it, p, d)

    def first_take(k):
        b0 = pl.multiple_of(blocks[k], CH)
        for d in range(2):
            z0 = (0, HZ + NH)[d]

            def take(d=d, z0=z0):
                first(d, k).wait_recv()
                ebuf[0, pl.ds(my + b0, CH), z0:z0 + HZ, :] = jnp.transpose(land[d, :, pl.ds(b0, CH), :], (1, 0, 2))
            when(zfrom[d], take)
            relay(0, k, d)

    def edge_own(it, d):
        def go():
            gyc(it, d, 0).wait_recv()
            for q in range(2):
                when(v == q, functools.partial(send_fwd, it, d, q))
        when(has[d], go)

    def gather_edge(it, d):
        for q in range(2):
            when(both(both(zed_has[1 + q], has[d]), v == q), gyc(it, d, 1 + q).wait_recv)
            when(both(has[d], v == 1 - q), fwd(it, d, q).wait_recv)

    def sent():
        it = ITERS - 1
        for d in range(2):
            def along_z(d=d):
                for p in range(NP):
                    sz(it, d, p).wait_send()
            when(zhas[d], along_z)

            def along_y(d=d):
                sy(it, d, 0).wait_send()
                for q in range(2):
                    when(both(zed_has[1 + q], v == q), diagonal(it, d, q).wait_send)
                    when(v == q, sfwd(it, d, q).wait_send)
            when(has[d], along_y)

    def scatter_edge(it, d):
        for q in range(2):
            when(both(both(zed_has[1 + q], has[d]), v == q), functools.partial(send_sy, it, d, 1 + q))
            when(both(has[d], v == q), functools.partial(send_sfwd, it, d, q))

    def scatter_own(it, d):
        r0 = row(HALO[d], my)
        for q in range(2):
            def add(q=q):
                z0 = (HZ, NH)[q]
                sfwd(it, d, q).wait_recv()
                cbuf[it, pl.ds(r0, my), z0:z0 + HZ, :] += sbuf[it, d]
            when(both(has[d], v == 1 - q), add)
        when(has[d], functools.partial(send_sy, it, d, 0))

    def scatter_piece(it, p):
        for d in range(2):
            when(zhas[d], functools.partial(send_sz, it, d, p))

    def scatter_end(it, p):
        r0 = row(*ROWS[p])
        for q in range(2):
            z0 = ZED[1 + q][0]

            def add(q=q, z0=z0):
                sy(it, p, 1 + q).wait_recv()
                cbuf[it, pl.ds(r0, my), z0:z0 + HZ, :] += rybuf[it, p, :, z0:z0 + HZ, :]
            when(both(both(zed_has[1 + q], has[p]), v == q), add)
            when(both(zed_has[1 + q], v == q), functools.partial(send_sz, it, 1 - q, p))

    def scatter_near(it, p):
        for q in range(2):
            when(v == 1 - q, functools.partial(send_sz, it, 1 - q, p))

    def scatter_take(it, p):
        n = ROWS[p][1]
        r0 = row(*ROWS[p])
        if p < 2:
            def add_y():
                sy(it, p, 0).wait_recv()
                cbuf[it, pl.ds(r0, n), HZ:HZ + NH, :] += rybuf[it, p, :, HZ:HZ + NH, :]
            when(has[p], add_y)
            if it + 1 == ITERS:
                for q in range(2):
                    def add_diagonal(q=q):
                        z0 = (NH, HZ)[q]
                        diagonal(it, p, q).wait_recv()
                        cbuf[it, pl.ds(r0, n), z0:z0 + HZ, :] += rybuf[it, p, :, 0:HZ, :]
                    when(both(both(zed_has[2 - q], has[p]), v == 1 - q), add_diagonal)
        for d in range(2):
            z0 = (HZ, NH)[d]

            def add_z(d=d, z0=z0):
                sz(it, d, p).wait_recv()
                cbuf[it, pl.ds(r0, n), z0:z0 + HZ, :] += rzbuf[it, d, pl.ds(r0 - my, n)]
            when(zfrom[d], add_z)

    with scope("Wload"):
        load_start.wait()
    ebuf[0, my:my + NY, HZ:HZ + NH, :] = jnp.transpose(stage[0], (1, 0, 2))
    gather_own(0)
    mine[...] = jnp.zeros_like(mine)
    for k, (raw, taps) in enumerate(((raw_z, KZ), (raw_y, KY), (raw_x, KX))):
        loads[k].wait()
        mine[k:k + 1, 0:taps] = raw[...] / jnp.sum(raw[...], axis=1, keepdims=True)
    swap_prof = pltpu.make_async_remote_copy(
        src_ref=mine, dst_ref=theirs, send_sem=xssem.at[0], recv_sem=xrsem.at[0],
        device_id=partner, device_id_type=MESH)
    swap_prof.start()
    swap_obs = pltpu.make_async_remote_copy(
        src_ref=obs_hbm.at[0, pl.ds((1 - v) * NH, NH)], dst_ref=obs_z.at[v],
        send_sem=xssem.at[1], recv_sem=xrsem.at[1], device_id=partner, device_id_type=MESH)
    swap_obs.start()

    with scope("Wprof"):
        swap_prof.wait()
    own, other = mine[...], theirs[...]
    prof = (jnp.where(v == 0, own, other), jnp.where(v == 0, other, own))

    def tap(view, k, a):
        return prof[view][k:k + 1, a:a + 1]

    rows = lax.broadcasted_iota(jnp.int32, (NE, 3 * NE), 0)
    cols = lax.broadcasted_iota(jnp.int32, (NE, 3 * NE), 1)
    third = cols // NE
    cols = cols - third * NE

    def banded(diff, view, k, taps):
        w = jnp.zeros(diff.shape, F32)
        for a in range(taps):
            w = jnp.where(diff == a, tap(view, k, a), w)
        return w

    off = HZ - mz
    for ref, inner, outer in ((wf, rows, cols), (wb, cols, rows)):
        second = inner >= NH
        diff = outer - jnp.where(second, inner - NH, inner) - off
        w = jnp.where(second, banded(diff, 1, 0, KZ), banded(diff, 0, 0, KZ))
        high, low = split(w)
        ref[...] = jnp.where(third == 2, low.astype(F32), high.astype(F32)).astype(BF16)
    for view in range(2):
        for back in range(2):
            for r0 in range(0, NX, 64):
                r = lax.broadcasted_iota(jnp.int32, (64, NX), 0) + r0
                c = lax.broadcasted_iota(jnp.int32, (64, NX), 1)
                diff = (c - r if back else r - c) + mx
                high, low = split(banded(diff, view, 2, KX))
                tx[view, back, 0, r0:r0 + 64, :] = high
                tx[view, back, 1, r0:r0 + 64, :] = low
    wy = [[jnp.broadcast_to(tap(view, 1, b), (NH, NX)) for b in range(KY)] for view in range(2)]

    qbuf[0:2 * my] = jnp.zeros((2 * my, NE, NX), F32)
    qbuf[2 * my + NY:] = jnp.zeros((2 * my, NE, NX), F32)

    with scope("Wobs"):
        load_obs.wait()
        swap_obs.wait()
    for view in range(2):
        obs_t[view] = jnp.transpose(obs_z[view], (1, 0, 2))

    def xblur(high, low, view, back):
        both_ = jnp.concatenate([high, low], axis=0)
        n = high.shape[0]
        d = jnp.dot(both_, tx[view, back, 0], preferred_element_type=F32)
        d2 = jnp.dot(high, tx[view, back, 1], preferred_element_type=F32)
        return d[:n] + (d[n:] + d2)

    def stacked(x):
        high, low = split(x)
        return jnp.concatenate([high, low, high], axis=0)

    for it in range(ITERS):
        def zrows(i0, n, it=it):
            with scope(f"z{it}_{i0}"):
                r0 = row(i0, n)
                for y in range(n):
                    zbuf[r0 + y] = jnp.dot(wf[...], stacked(ebuf[it, r0 + y]), preferred_element_type=F32)

        def qrows(o0, n, it=it):
            with scope(f"q{it}_{o0}"):
                y0 = row(o0 + my, n) - my
                for view in range(2):
                    z0 = view * NH
                    for y in range(n):
                        acc = wy[view][0] * zbuf[y0 + y, z0:z0 + NH, :]
                        for b in range(1, KY):
                            acc = acc + wy[view][b] * zbuf[y0 + y + b, z0:z0 + NH, :]
                        high, low = split(acc)
                        ybuf[view, 0, y * NH:(y + 1) * NH, :] = high
                        ybuf[view, 1, y * NH:(y + 1) * NH, :] = low
                for view in range(2):
                    z0 = view * NH
                    m = n * NH
                    blurred = xblur(ybuf[view, 0, 0:m], ybuf[view, 1, 0:m], view, 0)
                    quotient = obs_t[view, pl.ds(y0, n)].reshape(m, NX) / blurred
                    high, low = split(quotient)
                    ybuf[view, 2, 0:m] = high
                    ybuf[view, 3, 0:m] = low
                    qbuf[pl.ds(2 * my + y0, n), z0:z0 + NH, :] = xblur(
                        ybuf[view, 2, 0:m], ybuf[view, 3, 0:m], view, 1).reshape(n, NH, NX)

        def crows(i0, n, it=it):
            with scope(f"c{it}_{i0}"):
                r0 = row(i0, n)
                for y in range(n):
                    r = r0 + y
                    parts = []
                    for view in range(2):
                        z0 = view * NH
                        acc = wy[view][0] * qbuf[r + 2 * my, z0:z0 + NH, :]
                        for b in range(1, KY):
                            acc = acc + wy[view][b] * qbuf[r + 2 * my - b, z0:z0 + NH, :]
                        parts.append(acc)
                    cbuf[it, r] = jnp.dot(wb[...], stacked(jnp.concatenate(parts, axis=0)),
                                          preferred_element_type=F32)

        if it == 0:
            with scope("Wg0_in"):
                first_take(0)
            zrows(my + CH, CH)
            with scope("Wge0own"):
                edge_own(it, 0)
            with scope("Wg0_out"):
                first_take(1)
            zrows(my, CH)
        else:
            for p in (1, 2, 3):
                with scope(f"Wg{it}_{p}"):
                    gather_take(it, p)
                zrows(*ROWS[p])

        def low_edge(it=it):
            edge_own(it, 1)
            gather_edge(it, 1)
            zrows(0, my)
        when(has[1], low_edge)
        def low_scatter(it=it):
            crows(0, my)
            scatter_edge(it, 1)

        def high_edge(it=it):
            with scope(f"Wge{it}"):
                gather_edge(it, 0)
            zrows(my + NY, my)

        def high_scatter(it=it):
            crows(my + NY, my)
            scatter_edge(it, 0)

        qrows(0, OUT)
        when(has[1], low_scatter)
        crows(*ROWS[1])
        when(jnp.logical_not(has[1]), functools.partial(scatter_piece, it, 1))
        if it == 0:
            qrows(OUT, MID)
            for p in (2, 3):
                crows(*ROWS[p])
                scatter_piece(it, p)
            when(has[0], high_edge)
            qrows(OUT + MID, my)
            when(has[0], high_scatter)
            crows(*ROWS[4])
            scatter_piece(it, 4)
            crows(*ROWS[0])
            scatter_near(it, 0)
            with scope(f"Wse{it}"):
                scatter_end(it, 0)
            scatter_own(it, 0)
        else:
            with scope(f"Wg{it}_0"):
                gather_take(it, 0)
            zrows(*ROWS[0])
            with scope(f"Wge{it}own"):
                edge_own(it, 0)
            with scope(f"Wg{it}_4"):
                gather_take(it, 4)
            zrows(*ROWS[4])
            qrows(OUT, MID)
            for p in (2, 3):
                crows(*ROWS[p])
                scatter_piece(it, p)
            when(has[0], high_edge)
            qrows(OUT + MID, my)
            when(has[0], high_scatter)
            for p in (0, 4):
                crows(*ROWS[p])
                scatter_piece(it, p)
            with scope(f"Wso{it}"):
                scatter_own(it, 0)

        def low_end(it=it):
            scatter_own(it, 1)
            if it + 1 < ITERS:
                scatter_near(it, 1)
                scatter_end(it, 1)
            else:
                scatter_piece(it, 1)
        when(has[1], low_end)
        def update(p, it=it):
            n = ROWS[p][1]
            r0 = row(*ROWS[p])
            with scope(f"Wst{it}_{p}"):
                scatter_take(it, p)
            new = ebuf[it, pl.ds(r0, n), HZ:HZ + NH, :] * (0.5 * cbuf[it, pl.ds(r0, n), HZ:HZ + NH, :])
            if it + 1 < ITERS:
                ebuf[it + 1, pl.ds(r0, n), HZ:HZ + NH, :] = new
            else:
                zbuf[pl.ds(r0, n), 0:NH, :] = new

        if it + 1 < ITERS:
            for p in (1, 2, 3):
                update(p)
                gather_piece(it + 1, p)
            update(0)
            gather_piece(it + 1, 0)
            gather_own(it + 1)
            update(4)
            gather_piece(it + 1, 4)
        else:
            outs = []
            for n, (pieces, i0, rows_) in enumerate((((1, 2, 3), my, NY - 2 * my), ((4, 0), NY - my, 2 * my))):
                for p in pieces:
                    update(p)
                r0 = row(i0, rows_)
                src = zbuf.at[pl.ds(r0, rows_), pl.ds(0, NH)]
                dst = out_hbm.at[pl.ds(r0 - my, rows_), pl.ds(v * NH, NH)]
                outs.append(pltpu.make_async_copy(src, dst, lsem.at[n]))
                outs.append(pltpu.make_async_remote_copy(
                    src_ref=src, dst_ref=dst, send_sem=xssem.at[n], recv_sem=xrsem.at[n],
                    device_id=partner, device_id_type=MESH))
                outs[-1].start()
                outs[-2].start()
            with scope("Wsent2"):
                sent()
            with scope("Wout"):
                for out in outs:
                    out.wait()


def on_device(S, G, observed, start, spread_z, spread_y, spread_x):
    NZ, NY, NX = start.shape
    KZ, KY, KX = spread_z.shape[1], spread_y.shape[1], spread_x.shape[1]
    NH = NZ // 2
    my = KY // 2
    HZ = -(-(KZ // 2) // 8) * 8
    NE, NR = NH + 2 * HZ, NY + 2 * my
    dims = (NH, NY, NX, HZ, KZ, KY, KX, S, G)
    vm = pltpu.VMEM
    hbm = pl.BlockSpec(memory_space=pltpu.HBM)
    out = pl.pallas_call(
        functools.partial(kernel, dims),
        out_shape=jax.ShapeDtypeStruct((NY, NZ, NX), F32),
        in_specs=[hbm] * 5,
        out_specs=pl.BlockSpec(memory_space=pl.ANY),
        scratch_shapes=[
            vm((1, KZ), F32), vm((1, KY), F32), vm((1, KX), F32),
            vm((1, NH, NY, NX), F32), vm((2, HZ, NY, NX), F32),
            vm((2, NH, NY, NX), F32), vm((2, NY, NH, NX), F32),
            vm((8, 128), F32), vm((8, 128), F32),
            vm((NE, 3 * NE), BF16), vm((NE, 3 * NE), BF16), vm((2, 2, 2, NX, NX), BF16),
            vm((NR, NE, NX), F32), vm((2, 4, NY // 2 * NH, NX), BF16), vm((NY + 4 * my, NE, NX), F32),
            vm((ITERS, NR, NE, NX), F32), vm((ITERS, NR, NE, NX), F32),
            vm((ITERS, 2, my, NE, NX), F32), vm((ITERS, 2, NY, HZ, NX), F32), vm((ITERS, 2, my, HZ, NX), F32),
            pltpu.SemaphoreType.DMA((5,)), pltpu.SemaphoreType.DMA((16,)), pltpu.SemaphoreType.DMA((32,)),
            pltpu.SemaphoreType.DMA((2,)), pltpu.SemaphoreType.DMA((2,)),
        ],
        compiler_params=pltpu.CompilerParams(
            collective_id=0, has_side_effects=True, vmem_limit_bytes=24 << 20),
    )(*(pltpu.with_memory_space_constraint(x, pltpu.HBM) for x in (observed, start, spread_z, spread_y, spread_x)))
    return jnp.transpose(out, (1, 0, 2))


def solution(mesh):
    S, G = 2 * mesh.shape["gz"], mesh.shape["gy"]
    return jax.shard_map(
        functools.partial(on_device, S, G),
        mesh=mesh,
        in_specs=(
            P("view", "gz", "gy", None),
            P("gz", "gy", None),
            P("view", None),
            P("view", None),
            P("view", None),
        ),
        out_specs=P("gz", "gy", None),
        check_vma=False,
    )
```

```python
import contextlib
import functools

import jax
import jax.numpy as jnp
from jax import lax
from jax.experimental import pallas as pl
from jax.experimental.pallas import tpu as pltpu
from jax.sharding import PartitionSpec as P

ITERS = 2
MESH = pl.DeviceIdType.MESH
F32 = jnp.float32
BF16 = jnp.bfloat16


def scope(name):
    return contextlib.nullcontext()


def split(x):
    high = x.astype(BF16)
    return high, (x - high.astype(F32)).astype(BF16)


def kernel(dims, obs_hbm, start_hbm, sz_ref, sy_ref, sx_ref, out_hbm,
           raw_z, raw_y, raw_x, stage, land, obs_z, obs_t, mine, theirs, wf, wb, tx, zbuf, ybuf, qbuf,
           ebuf, cbuf, rybuf, rzbuf, sbuf, lsem, ssem, rsem, xssem, xrsem):
    NH, NY, NX, HZ, KZ, KY, KX, S, G = dims
    my, mz, mx = KY // 2, KZ // 2, KX // 2
    NE, NR, NQ = NH + 2 * HZ, NY + 2 * my, NY + 4 * my
    CH, NP = NY // 2, 4
    v = lax.axis_index("view")
    gy = lax.axis_index("gy")
    s = 2 * lax.axis_index("gz") + v
    up_z, dn_z = s < S - 1, s > 0
    up_y, dn_y = gy < G - 1, gy > 0
    f = lax.rem(gy, 2)
    has = (jnp.logical_or(jnp.logical_and(f == 0, up_y), jnp.logical_and(f == 1, dn_y)),
           jnp.logical_or(jnp.logical_and(f == 0, dn_y), jnp.logical_and(f == 1, up_y)))

    def row(i0, n=1):
        return i0 + f * (NR - 2 * i0 - n)

    def qrow(j0, n=1):
        return j0 + f * (NQ - 2 * j0 - n)

    def zdev(t):
        t = lax.rem(t + S, S)
        return {"view": lax.rem(t, 2), "gz": t // 2}

    zto = (zdev(s + 1), zdev(s - 1))
    step = 1 - 2 * f
    yto = ({"gy": lax.rem(gy + step + G, G)}, {"gy": lax.rem(gy - step + G, G)})
    partner = {"view": 1 - v}
    zout = dict(zdev(s - 1 + 2 * v))
    diag = tuple({**zout, **yto[d]} for d in range(2))
    zhas, zfrom = (up_z, dn_z), (dn_z, up_z)

    def when(cond, fn):
        @pl.when(cond)
        def _():
            fn()

    def both(a, b):
        return jnp.logical_and(a, b)

    barrier = pltpu.get_barrier_semaphore()
    greet = ((up_z, zto[0]), (dn_z, zto[1]), (has[0], yto[0]), (has[1], yto[1]))
    for there, to in greet:
        @pl.when(there)
        def _(to=to):
            pl.semaphore_signal(barrier, inc=1, device_id=to, device_id_type=MESH)

    load_start = pltpu.make_async_copy(start_hbm.at[pl.ds(v * NH, NH)], stage.at[0], lsem.at[0])
    load_start.start()
    load_obs = pltpu.make_async_copy(obs_hbm.at[0, pl.ds(v * NH, NH)], obs_z.at[v], lsem.at[1])
    load_obs.start()
    loads = [pltpu.make_async_copy(ref, raw, lsem.at[2 + k])
             for k, (ref, raw) in enumerate(((sz_ref, raw_z), (sy_ref, raw_y), (sx_ref, raw_x)))]
    for load in loads:
        load.start()

    blocks = (CH * (1 - f), CH * f)

    def first(d, k):
        b0 = pl.multiple_of(blocks[k], CH)
        src0 = v * NH + (NH - mz, 0)[d]
        dst0 = (HZ - mz, 0)[d]
        return pltpu.make_async_remote_copy(
            src_ref=start_hbm.at[pl.ds(src0, mz), pl.ds(b0, CH)],
            dst_ref=land.at[d, pl.ds(dst0, mz), pl.ds(b0, CH)],
            send_sem=ssem.at[NP * d + k], recv_sem=rsem.at[NP * d + k], device_id=zto[d], device_id_type=MESH)

    peers = sum(there.astype(jnp.int32) for there, _ in greet)
    with scope("Wbar"):
        pl.semaphore_wait(barrier, peers)
    for k in range(2):
        for d in range(2):
            when(zhas[d], first(d, k).start)

    land[0, 0:HZ - mz] = jnp.zeros((HZ - mz, NY, NX), F32)
    land[1, mz:HZ] = jnp.zeros((HZ - mz, NY, NX), F32)
    for d in range(2):
        def blank(d=d):
            for it in range(ITERS):
                z0 = (0, HZ + NH)[d]
                ebuf[it, :, z0:z0 + HZ, :] = jnp.zeros((NR, HZ, NX), F32)
        when(jnp.logical_not(zfrom[d]), blank)

        def blank_rows(d=d):
            zbuf[pl.ds(row((my + NY, 0)[d], my), my)] = jnp.zeros((my, NE, NX), F32)
        when(jnp.logical_not(has[d]), blank_rows)

    def copy(send, recv, src, dst, to):
        return pltpu.make_async_remote_copy(
            src_ref=src, dst_ref=dst, send_sem=ssem.at[send], recv_sem=rsem.at[recv],
            device_id=to, device_id_type=MESH)

    ROWS = ((NY, my), (my, my), (2 * my, NY - 3 * my), (NY - my, my))
    OUT, MID = NY - 3 * my, 2 * my
    assert len(ROWS) == NP
    ZED = ((HZ, NH), (0, HZ), (HZ + NH, HZ))
    zed_has = (None, dn_z, up_z)
    EDGE, HALO = (NY, my), (my + NY, 0)
    THERE = (f * (my + NY), (1 - f) * (my + NY))

    def gz(it, d, p):
        e = ebuf.at[it]
        src0, dst0 = ((NH, 0), (HZ, HZ + NH))[d]
        n = ROWS[p][1]
        r0 = row(*ROWS[p])
        return copy(NP * d + p, NP * d + p, e.at[pl.ds(r0, n), pl.ds(src0, HZ)],
                    e.at[pl.ds(r0, n), pl.ds(dst0, HZ)], zto[d])

    def gyc(it, d, p):
        e = ebuf.at[it]
        z0, n = ZED[p]
        k = 2 * min(p, 1) + d
        return copy(2 * NP + k, 4 * NP + k, e.at[pl.ds(row(EDGE[d], my), my), pl.ds(z0, n)],
                    e.at[pl.ds(THERE[d], my), pl.ds(z0, n)], yto[d])

    def fwd(it, d, q):
        rows_ = pl.ds(row(HALO[d], my), my)
        e = ebuf.at[it]
        return copy(2 * NP + 4 + d, 4 * NP + 4 + d, e.at[rows_, pl.ds((NH, HZ)[q], HZ)],
                    e.at[rows_, pl.ds((0, HZ + NH)[q], HZ)], partner)

    def sfwd(it, d, q):
        rows_ = pl.ds(row(HALO[d], my), my)
        return copy(2 * NP + 4 + d, 4 * NP + 10 + d, cbuf.at[it, rows_, pl.ds((HZ + NH, 0)[q], HZ)],
                    sbuf.at[it, d], partner)

    def diagonal(it, d, q):
        z0, n = ZED[1 + q]
        return copy(2 * NP + 2 + d, 4 * NP + 8 + d, cbuf.at[it, pl.ds(row(HALO[d], my), my), pl.ds(z0, n)],
                    rybuf.at[it, d, :, pl.ds(0, HZ)], diag[d])

    def sz(it, d, p):
        src0 = (HZ + NH, 0)[d]
        n = ROWS[p][1]
        r0 = row(*ROWS[p])
        return copy(NP * d + p, 2 * NP + NP * d + p, cbuf.at[it, pl.ds(r0, n), pl.ds(src0, HZ)],
                    rzbuf.at[it, d, pl.ds(r0 - my, n)], zto[d])

    def sy(it, d, p):
        z0, n = ZED[p]
        k = 2 * min(p, 1) + d
        return copy(2 * NP + k, 4 * NP + 6 + k, cbuf.at[it, pl.ds(row(HALO[d], my), my), pl.ds(z0, n)],
                    rybuf.at[it, d, :, pl.ds(z0, n)], yto[d])

    def follow(before, now):
        if before is not None:
            before.wait_send()
        now.start()

    def send_gz(it, d, p):
        follow(sz(it - 1, d, p), gz(it, d, p))

    def send_sz(it, d, p):
        follow(gz(it, d, p) if it > 0 else first(d, p) if p < 2 else None, sz(it, d, p))

    def send_gy(it, d, p):
        follow(sy(it - 1, d, p) if it > 0 else None, gyc(it, d, p))

    def send_sy(it, d, p):
        now = diagonal(it, d, p - 1) if p > 0 and it + 1 == ITERS else sy(it, d, p)
        follow(gyc(it, d, p), now)

    def send_fwd(it, d, q):
        follow(sfwd(it - 1, d, q) if it > 0 else None, fwd(it, d, q))

    def send_sfwd(it, d, q):
        follow(fwd(it, d, q), sfwd(it, d, q))

    def gather_piece(it, p):
        for d in range(2):
            when(zhas[d], functools.partial(send_gz, it, d, p))

    def gather_own(it):
        for d in range(2):
            when(has[d], functools.partial(send_gy, it, d, 0))

    def relay(it, p, d):
        if p < 2:
            when(both(both(zfrom[d], has[p]), v == d), functools.partial(send_gy, it, p, 1 + d))

    def gather_take(it, p):
        for d in range(2):
            when(zfrom[d], gz(it, d, p).wait_recv)
            relay(it, p, d)

    def first_take(k):
        b0 = pl.multiple_of(blocks[k], CH)
        for d in range(2):
            z0 = (0, HZ + NH)[d]

            def take(d=d, z0=z0):
                first(d, k).wait_recv()
                ebuf[0, pl.ds(my + b0, CH), z0:z0 + HZ, :] = jnp.transpose(land[d, :, pl.ds(b0, CH), :], (1, 0, 2))
            when(zfrom[d], take)
            relay(0, k, d)

    def edge_own(it, d):
        def go():
            gyc(it, d, 0).wait_recv()
            for q in range(2):
                when(v == q, functools.partial(send_fwd, it, d, q))
        when(has[d], go)

    def gather_edge(it, d):
        for q in range(2):
            when(both(both(zed_has[1 + q], has[d]), v == q), gyc(it, d, 1 + q).wait_recv)
            when(both(has[d], v == 1 - q), fwd(it, d, q).wait_recv)

    def sent():
        it = ITERS - 1
        for d in range(2):
            def along_z(d=d):
                for p in range(NP):
                    sz(it, d, p).wait_send()
            when(zhas[d], along_z)

            def along_y(d=d):
                sy(it, d, 0).wait_send()
                for q in range(2):
                    when(both(zed_has[1 + q], v == q), diagonal(it, d, q).wait_send)
                    when(v == q, sfwd(it, d, q).wait_send)
            when(has[d], along_y)

    def scatter_edge(it, d):
        for q in range(2):
            when(both(both(zed_has[1 + q], has[d]), v == q), functools.partial(send_sy, it, d, 1 + q))
            when(both(has[d], v == q), functools.partial(send_sfwd, it, d, q))

    def scatter_own(it, d):
        r0 = row(HALO[d], my)
        for q in range(2):
            def add(q=q):
                z0 = (HZ, NH)[q]
                sfwd(it, d, q).wait_recv()
                cbuf[it, pl.ds(r0, my), z0:z0 + HZ, :] += sbuf[it, d]
            when(both(has[d], v == 1 - q), add)
        when(has[d], functools.partial(send_sy, it, d, 0))

    def scatter_piece(it, p):
        for d in range(2):
            when(zhas[d], functools.partial(send_sz, it, d, p))

    def scatter_end(it, p):
        r0 = row(*ROWS[p])
        for q in range(2):
            z0 = ZED[1 + q][0]

            def add(q=q, z0=z0):
                sy(it, p, 1 + q).wait_recv()
                cbuf[it, pl.ds(r0, my), z0:z0 + HZ, :] += rybuf[it, p, :, z0:z0 + HZ, :]
            when(both(both(zed_has[1 + q], has[p]), v == q), add)
            when(both(zed_has[1 + q], v == q), functools.partial(send_sz, it, 1 - q, p))

    def scatter_near(it, p):
        for q in range(2):
            when(v == 1 - q, functools.partial(send_sz, it, 1 - q, p))

    def scatter_take(it, p):
        n = ROWS[p][1]
        r0 = row(*ROWS[p])
        if p < 2:
            def add_y():
                sy(it, p, 0).wait_recv()
                cbuf[it, pl.ds(r0, n), HZ:HZ + NH, :] += rybuf[it, p, :, HZ:HZ + NH, :]
            when(has[p], add_y)
            if it + 1 == ITERS:
                for q in range(2):
                    def add_diagonal(q=q):
                        z0 = (NH, HZ)[q]
                        diagonal(it, p, q).wait_recv()
                        cbuf[it, pl.ds(r0, n), z0:z0 + HZ, :] += rybuf[it, p, :, 0:HZ, :]
                    when(both(both(zed_has[2 - q], has[p]), v == 1 - q), add_diagonal)
        for d in range(2):
            z0 = (HZ, NH)[d]

            def add_z(d=d, z0=z0):
                sz(it, d, p).wait_recv()
                cbuf[it, pl.ds(r0, n), z0:z0 + HZ, :] += rzbuf[it, d, pl.ds(r0 - my, n)]
            when(zfrom[d], add_z)

    with scope("Wload"):
        load_start.wait()
    ebuf[0, my:my + NY, HZ:HZ + NH, :] = jnp.transpose(stage[0], (1, 0, 2))
    gather_own(0)
    mine[...] = jnp.zeros_like(mine)
    for k, (raw, taps) in enumerate(((raw_z, KZ), (raw_y, KY), (raw_x, KX))):
        loads[k].wait()
        mine[k:k + 1, 0:taps] = raw[...] / jnp.sum(raw[...], axis=1, keepdims=True)
    swap_prof = pltpu.make_async_remote_copy(
        src_ref=mine, dst_ref=theirs, send_sem=xssem.at[0], recv_sem=xrsem.at[0],
        device_id=partner, device_id_type=MESH)
    swap_prof.start()
    swap_obs = pltpu.make_async_remote_copy(
        src_ref=obs_hbm.at[0, pl.ds((1 - v) * NH, NH)], dst_ref=obs_z.at[v],
        send_sem=xssem.at[1], recv_sem=xrsem.at[1], device_id=partner, device_id_type=MESH)
    swap_obs.start()

    with scope("Wprof"):
        swap_prof.wait()
    own, other = mine[...], theirs[...]
    prof = (jnp.where(v == 0, own, other), jnp.where(v == 0, other, own))

    def tap(view, k, a):
        return prof[view][k:k + 1, a:a + 1]

    rows = lax.broadcasted_iota(jnp.int32, (NE, 3 * NE), 0)
    cols = lax.broadcasted_iota(jnp.int32, (NE, 3 * NE), 1)
    third = cols // NE
    cols = cols - third * NE

    def banded(diff, view, k, taps):
        w = jnp.zeros(diff.shape, F32)
        for a in range(taps):
            w = jnp.where(diff == a, tap(view, k, a), w)
        return w

    off = HZ - mz
    for ref, inner, outer in ((wf, rows, cols), (wb, cols, rows)):
        second = inner >= NH
        diff = outer - jnp.where(second, inner - NH, inner) - off
        w = jnp.where(second, banded(diff, 1, 0, KZ), banded(diff, 0, 0, KZ))
        high, low = split(w)
        ref[...] = jnp.where(third == 2, low.astype(F32), high.astype(F32)).astype(BF16)
    for view in range(2):
        for back in range(2):
            for r0 in range(0, NX, 64):
                r = lax.broadcasted_iota(jnp.int32, (64, NX), 0) + r0
                c = lax.broadcasted_iota(jnp.int32, (64, NX), 1)
                diff = (c - r if back else r - c) + mx
                high, low = split(banded(diff, view, 2, KX))
                tx[view, back, 0, r0:r0 + 64, :] = high
                tx[view, back, 1, r0:r0 + 64, :] = low
    wy = [[jnp.broadcast_to(tap(view, 1, b), (NH, NX)) for b in range(KY)] for view in range(2)]

    qbuf[0:2 * my] = jnp.zeros((2 * my, NE, NX), F32)
    qbuf[2 * my + NY:] = jnp.zeros((2 * my, NE, NX), F32)

    with scope("Wobs"):
        load_obs.wait()
        swap_obs.wait()
    for view in range(2):
        obs_t[view] = jnp.transpose(obs_z[view], (1, 0, 2))

    def xblur(high, low, view, back):
        both_ = jnp.concatenate([high, low], axis=0)
        n = high.shape[0]
        d = jnp.dot(both_, tx[view, back, 0], preferred_element_type=F32)
        d2 = jnp.dot(high, tx[view, back, 1], preferred_element_type=F32)
        return d[:n] + (d[n:] + d2)

    def stacked(x):
        high, low = split(x)
        return jnp.concatenate([high, low, high], axis=0)

    for it in range(ITERS):
        def zrows(i0, n, it=it):
            with scope(f"z{it}_{i0}"):
                r0 = row(i0, n)
                for y in range(n):
                    zbuf[r0 + y] = jnp.dot(wf[...], stacked(ebuf[it, r0 + y]), preferred_element_type=F32)

        def qrows(o0, n, it=it):
            with scope(f"q{it}_{o0}"):
                y0 = row(o0 + my, n) - my
                for view in range(2):
                    z0 = view * NH
                    for y in range(n):
                        acc = wy[view][0] * zbuf[y0 + y, z0:z0 + NH, :]
                        for b in range(1, KY):
                            acc = acc + wy[view][b] * zbuf[y0 + y + b, z0:z0 + NH, :]
                        high, low = split(acc)
                        ybuf[view, 0, y * NH:(y + 1) * NH, :] = high
                        ybuf[view, 1, y * NH:(y + 1) * NH, :] = low
                for view in range(2):
                    z0 = view * NH
                    m = n * NH
                    blurred = xblur(ybuf[view, 0, 0:m], ybuf[view, 1, 0:m], view, 0)
                    quotient = obs_t[view, pl.ds(y0, n)].reshape(m, NX) / blurred
                    high, low = split(quotient)
                    ybuf[view, 2, 0:m] = high
                    ybuf[view, 3, 0:m] = low
                    qbuf[pl.ds(2 * my + y0, n), z0:z0 + NH, :] = xblur(
                        ybuf[view, 2, 0:m], ybuf[view, 3, 0:m], view, 1).reshape(n, NH, NX)

        def crows(i0, n, it=it):
            with scope(f"c{it}_{i0}"):
                r0 = row(i0, n)
                for y in range(n):
                    r = r0 + y
                    parts = []
                    for view in range(2):
                        z0 = view * NH
                        acc = wy[view][0] * qbuf[r + 2 * my, z0:z0 + NH, :]
                        for b in range(1, KY):
                            acc = acc + wy[view][b] * qbuf[r + 2 * my - b, z0:z0 + NH, :]
                        parts.append(acc)
                    cbuf[it, r] = jnp.dot(wb[...], stacked(jnp.concatenate(parts, axis=0)),
                                          preferred_element_type=F32)

        if it == 0:
            with scope("Wg0_in"):
                first_take(0)
            zrows(my + CH, CH)
            with scope("Wge0own"):
                edge_own(it, 0)
            with scope("Wg0_out"):
                first_take(1)
            zrows(my, CH)
        else:
            for p in (1, 2):
                with scope(f"Wg{it}_{p}"):
                    gather_take(it, p)
                zrows(*ROWS[p])

        def low_edge(it=it):
            edge_own(it, 1)
            gather_edge(it, 1)
            zrows(0, my)
        when(has[1], low_edge)
        def low_scatter(it=it):
            crows(0, my)
            scatter_edge(it, 1)

        def high_edge(it=it):
            with scope(f"Wge{it}"):
                gather_edge(it, 0)
            zrows(my + NY, my)

        def high_scatter(it=it):
            crows(my + NY, my)
            scatter_edge(it, 0)

        qrows(0, OUT)
        when(has[1], low_scatter)
        crows(*ROWS[1])
        when(jnp.logical_not(has[1]), functools.partial(scatter_piece, it, 1))
        if it == 0:
            qrows(OUT, MID)
            crows(*ROWS[2])
            scatter_piece(it, 2)
            when(has[0], high_edge)
            qrows(OUT + MID, my)
            when(has[0], high_scatter)
            crows(NY - my, 2 * my)
            scatter_piece(it, 3)
            scatter_near(it, 0)
            with scope(f"Wse{it}"):
                scatter_end(it, 0)
            scatter_own(it, 0)
        else:
            with scope(f"Wg{it}_0"):
                gather_take(it, 0)
            with scope(f"Wge{it}own"):
                edge_own(it, 0)
            with scope(f"Wg{it}_3"):
                gather_take(it, 3)
            zrows(NY - my, 2 * my)
            qrows(OUT, MID)
            crows(*ROWS[2])
            scatter_piece(it, 2)
            when(has[0], high_edge)
            qrows(OUT + MID, my)
            when(has[0], high_scatter)
            crows(NY - my, 2 * my)
            scatter_piece(it, 0)
            scatter_piece(it, 3)
            with scope(f"Wso{it}"):
                scatter_own(it, 0)

        def low_end(it=it):
            scatter_own(it, 1)
            if it + 1 < ITERS:
                scatter_near(it, 1)
                scatter_end(it, 1)
            else:
                scatter_piece(it, 1)
        when(has[1], low_end)
        def update(p, it=it):
            n = ROWS[p][1]
            r0 = row(*ROWS[p])
            with scope(f"Wst{it}_{p}"):
                scatter_take(it, p)
            new = ebuf[it, pl.ds(r0, n), HZ:HZ + NH, :] * (0.5 * cbuf[it, pl.ds(r0, n), HZ:HZ + NH, :])
            if it + 1 < ITERS:
                ebuf[it + 1, pl.ds(r0, n), HZ:HZ + NH, :] = new
            else:
                zbuf[pl.ds(r0, n), 0:NH, :] = new

        if it + 1 < ITERS:
            for p in (1, 2):
                update(p)
                gather_piece(it + 1, p)
            update(0)
            gather_piece(it + 1, 0)
            gather_own(it + 1)
            update(3)
            gather_piece(it + 1, 3)
        else:
            outs = []
            for k, pieces in enumerate(((1, 2), (3, 0))):
                for p in pieces:
                    update(p)
                b0 = pl.multiple_of(blocks[1 - k], CH)
                stage[0, :, pl.ds(b0, CH), :] = jnp.transpose(zbuf[pl.ds(my + b0, CH), 0:NH, :], (1, 0, 2))
                src = stage.at[0, :, pl.ds(b0, CH)]
                dst = out_hbm.at[pl.ds(v * NH, NH), pl.ds(b0, CH)]
                outs.append(pltpu.make_async_copy(src, dst, lsem.at[k]))
                outs.append(pltpu.make_async_remote_copy(
                    src_ref=src, dst_ref=dst, send_sem=xssem.at[k], recv_sem=xrsem.at[k],
                    device_id=partner, device_id_type=MESH))
                outs[-1].start()
                outs[-2].start()
            with scope("Wsent2"):
                sent()
            with scope("Wout"):
                for out in outs:
                    out.wait()


def store(src, dst, sem):
    copy = pltpu.make_async_copy(src, dst, sem)
    copy.start()
    copy.wait()


def on_device(S, G, observed, start, spread_z, spread_y, spread_x):
    NZ, NY, NX = start.shape
    KZ, KY, KX = spread_z.shape[1], spread_y.shape[1], spread_x.shape[1]
    NH = NZ // 2
    my = KY // 2
    HZ = -(-(KZ // 2) // 8) * 8
    NE, NR = NH + 2 * HZ, NY + 2 * my
    dims = (NH, NY, NX, HZ, KZ, KY, KX, S, G)
    vm = pltpu.VMEM
    hbm = pl.BlockSpec(memory_space=pltpu.HBM)
    out = pl.pallas_call(
        functools.partial(kernel, dims),
        out_shape=jax.ShapeDtypeStruct((NZ, NY, NX), F32),
        in_specs=[hbm] * 5,
        out_specs=pl.BlockSpec(memory_space=pl.ANY),
        scratch_shapes=[
            vm((1, KZ), F32), vm((1, KY), F32), vm((1, KX), F32),
            vm((1, NH, NY, NX), F32), vm((2, HZ, NY, NX), F32),
            vm((2, NH, NY, NX), F32), vm((2, NY, NH, NX), F32),
            vm((8, 128), F32), vm((8, 128), F32),
            vm((NE, 3 * NE), BF16), vm((NE, 3 * NE), BF16), vm((2, 2, 2, NX, NX), BF16),
            vm((NR, NE, NX), F32), vm((2, 4, NY // 2 * NH, NX), BF16), vm((NY + 4 * my, NE, NX), F32),
            vm((ITERS, NR, NE, NX), F32), vm((ITERS, NR, NE, NX), F32),
            vm((ITERS, 2, my, NE, NX), F32), vm((ITERS, 2, NY, HZ, NX), F32), vm((ITERS, 2, my, HZ, NX), F32),
            pltpu.SemaphoreType.DMA((5,)), pltpu.SemaphoreType.DMA((14,)), pltpu.SemaphoreType.DMA((28,)),
            pltpu.SemaphoreType.DMA((2,)), pltpu.SemaphoreType.DMA((2,)),
        ],
        compiler_params=pltpu.CompilerParams(
            collective_id=0, has_side_effects=True, vmem_limit_bytes=24 << 20),
    )(*(pltpu.with_memory_space_constraint(x, pltpu.HBM) for x in (observed, start, spread_z, spread_y, spread_x)))
    return pl.pallas_call(
        store,
        out_shape=jax.ShapeDtypeStruct((NZ, NY, NX), F32),
        in_specs=[pl.BlockSpec(memory_space=pl.ANY)],
        out_specs=hbm,
        scratch_shapes=[pltpu.SemaphoreType.DMA],
        compiler_params=pltpu.CompilerParams(vmem_limit_bytes=4 << 20),
    )(out)


def solution(mesh):
    S, G = 2 * mesh.shape["gz"], mesh.shape["gy"]
    return jax.shard_map(
        functools.partial(on_device, S, G),
        mesh=mesh,
        in_specs=(
            P("view", "gz", "gy", None),
            P("gz", "gy", None),
            P("view", None),
            P("view", None),
            P("view", None),
        ),
        out_specs=P("gz", "gy", None),
        check_vma=False,
    )
```

```python
import contextlib
import functools

import jax
import jax.numpy as jnp
from jax import lax
from jax.experimental import pallas as pl
from jax.experimental.pallas import tpu as pltpu
from jax.sharding import PartitionSpec as P

ITERS = 2
MESH = pl.DeviceIdType.MESH
F32 = jnp.float32
BF16 = jnp.bfloat16


def scope(name):
    return contextlib.nullcontext()


def split(x):
    high = x.astype(BF16)
    return high, (x - high.astype(F32)).astype(BF16)


def kernel(dims, obs_hbm, start_hbm, sz_ref, sy_ref, sx_ref, out_hbm,
           raw_z, raw_y, raw_x, stage, land, obs_z, obs_t, mine, theirs, wf, wb, tx, zbuf, ybuf, qbuf,
           ebuf, cbuf, rybuf, rzbuf, sbuf, lsem, ssem, rsem, xssem, xrsem):
    NH, NY, NX, HZ, KZ, KY, KX, S, G = dims
    my, mz, mx = KY // 2, KZ // 2, KX // 2
    NE, NR, NQ = NH + 2 * HZ, NY + 2 * my, NY + 4 * my
    CH, NP = NY // 2, 5
    v = lax.axis_index("view")
    gy = lax.axis_index("gy")
    s = 2 * lax.axis_index("gz") + v
    up_z, dn_z = s < S - 1, s > 0
    up_y, dn_y = gy < G - 1, gy > 0
    f = lax.rem(gy, 2)
    has = (jnp.logical_or(jnp.logical_and(f == 0, up_y), jnp.logical_and(f == 1, dn_y)),
           jnp.logical_or(jnp.logical_and(f == 0, dn_y), jnp.logical_and(f == 1, up_y)))

    def row(i0, n=1):
        return i0 + f * (NR - 2 * i0 - n)

    def qrow(j0, n=1):
        return j0 + f * (NQ - 2 * j0 - n)

    def zdev(t):
        t = lax.rem(t + S, S)
        return {"view": lax.rem(t, 2), "gz": t // 2}

    zto = (zdev(s + 1), zdev(s - 1))
    step = 1 - 2 * f
    yto = ({"gy": lax.rem(gy + step + G, G)}, {"gy": lax.rem(gy - step + G, G)})
    partner = {"view": 1 - v}
    zout = dict(zdev(s - 1 + 2 * v))
    diag = tuple({**zout, **yto[d]} for d in range(2))
    zhas, zfrom = (up_z, dn_z), (dn_z, up_z)

    def when(cond, fn):
        @pl.when(cond)
        def _():
            fn()

    def both(a, b):
        return jnp.logical_and(a, b)

    barrier = pltpu.get_barrier_semaphore()
    greet = ((up_z, zto[0]), (dn_z, zto[1]), (has[0], yto[0]), (has[1], yto[1]))
    for there, to in greet:
        @pl.when(there)
        def _(to=to):
            pl.semaphore_signal(barrier, inc=1, device_id=to, device_id_type=MESH)

    load_start = pltpu.make_async_copy(start_hbm.at[pl.ds(v * NH, NH)], stage.at[0], lsem.at[0])
    load_start.start()
    load_obs = pltpu.make_async_copy(obs_hbm.at[0, pl.ds(v * NH, NH)], obs_z.at[v], lsem.at[1])
    load_obs.start()
    loads = [pltpu.make_async_copy(ref, raw, lsem.at[2 + k])
             for k, (ref, raw) in enumerate(((sz_ref, raw_z), (sy_ref, raw_y), (sx_ref, raw_x)))]
    for load in loads:
        load.start()

    blocks = (CH * (1 - f), CH * f)

    def first(d, k):
        b0 = pl.multiple_of(blocks[k], CH)
        src0 = v * NH + (NH - mz, 0)[d]
        dst0 = (HZ - mz, 0)[d]
        return pltpu.make_async_remote_copy(
            src_ref=start_hbm.at[pl.ds(src0, mz), pl.ds(b0, CH)],
            dst_ref=land.at[d, pl.ds(dst0, mz), pl.ds(b0, CH)],
            send_sem=ssem.at[NP * d + k], recv_sem=rsem.at[NP * d + k], device_id=zto[d], device_id_type=MESH)

    peers = sum(there.astype(jnp.int32) for there, _ in greet)
    with scope("Wbar"):
        pl.semaphore_wait(barrier, peers)
    for k in range(2):
        for d in range(2):
            when(zhas[d], first(d, k).start)

    land[0, 0:HZ - mz] = jnp.zeros((HZ - mz, NY, NX), F32)
    land[1, mz:HZ] = jnp.zeros((HZ - mz, NY, NX), F32)
    for d in range(2):
        def blank(d=d):
            for it in range(ITERS):
                z0 = (0, HZ + NH)[d]
                ebuf[it, :, z0:z0 + HZ, :] = jnp.zeros((NR, HZ, NX), F32)
        when(jnp.logical_not(zfrom[d]), blank)

        def blank_rows(d=d):
            zbuf[pl.ds(row((my + NY, 0)[d], my), my)] = jnp.zeros((my, NE, NX), F32)
        when(jnp.logical_not(has[d]), blank_rows)

    def copy(send, recv, src, dst, to):
        return pltpu.make_async_remote_copy(
            src_ref=src, dst_ref=dst, send_sem=ssem.at[send], recv_sem=rsem.at[recv],
            device_id=to, device_id_type=MESH)

    ROWS = ((NY, my), (my, my + 1), (2 * my + 1, NY - 4 * my - 1), (NY - 2 * my, my), (NY - my, my))
    OUT, MID = NY - 3 * my, 2 * my
    assert len(ROWS) == NP
    ZED = ((HZ, NH), (0, HZ), (HZ + NH, HZ))
    zed_has = (None, dn_z, up_z)
    EDGE, HALO = (NY, my), (my + NY, 0)
    THERE = (f * (my + NY), (1 - f) * (my + NY))

    def gz(it, d, p):
        e = ebuf.at[it]
        src0, dst0 = ((NH, 0), (HZ, HZ + NH))[d]
        n = ROWS[p][1]
        r0 = row(*ROWS[p])
        return copy(NP * d + p, NP * d + p, e.at[pl.ds(r0, n), pl.ds(src0, HZ)],
                    e.at[pl.ds(r0, n), pl.ds(dst0, HZ)], zto[d])

    def gyc(it, d, p):
        e = ebuf.at[it]
        z0, n = ZED[p]
        k = 2 * min(p, 1) + d
        return copy(2 * NP + k, 4 * NP + k, e.at[pl.ds(row(EDGE[d], my), my), pl.ds(z0, n)],
                    e.at[pl.ds(THERE[d], my), pl.ds(z0, n)], yto[d])

    def fwd(it, d, q):
        rows_ = pl.ds(row(HALO[d], my), my)
        e = ebuf.at[it]
        return copy(2 * NP + 4 + d, 4 * NP + 4 + d, e.at[rows_, pl.ds((NH, HZ)[q], HZ)],
                    e.at[rows_, pl.ds((0, HZ + NH)[q], HZ)], partner)

    def sfwd(it, d, q):
        rows_ = pl.ds(row(HALO[d], my), my)
        return copy(2 * NP + 4 + d, 4 * NP + 10 + d, cbuf.at[it, rows_, pl.ds((HZ + NH, 0)[q], HZ)],
                    sbuf.at[it, d], partner)

    def diagonal(it, d, q):
        z0, n = ZED[1 + q]
        return copy(2 * NP + 2 + d, 4 * NP + 8 + d, cbuf.at[it, pl.ds(row(HALO[d], my), my), pl.ds(z0, n)],
                    rybuf.at[it, d, :, pl.ds(0, HZ)], diag[d])

    def sz(it, d, p):
        src0 = (HZ + NH, 0)[d]
        n = ROWS[p][1]
        r0 = row(*ROWS[p])
        return copy(NP * d + p, 2 * NP + NP * d + p, cbuf.at[it, pl.ds(r0, n), pl.ds(src0, HZ)],
                    rzbuf.at[it, d, pl.ds(r0 - my, n)], zto[d])

    def sy(it, d, p):
        z0, n = ZED[p]
        k = 2 * min(p, 1) + d
        return copy(2 * NP + k, 4 * NP + 6 + k, cbuf.at[it, pl.ds(row(HALO[d], my), my), pl.ds(z0, n)],
                    rybuf.at[it, d, :, pl.ds(z0, n)], yto[d])

    def follow(before, now):
        if before is not None:
            before.wait_send()
        now.start()

    def send_gz(it, d, p):
        follow(sz(it - 1, d, p), gz(it, d, p))

    def send_sz(it, d, p):
        follow(gz(it, d, p) if it > 0 else first(d, p) if p < 2 else None, sz(it, d, p))

    def send_gy(it, d, p):
        follow(sy(it - 1, d, p) if it > 0 else None, gyc(it, d, p))

    def send_sy(it, d, p):
        now = diagonal(it, d, p - 1) if p > 0 and it + 1 == ITERS else sy(it, d, p)
        follow(gyc(it, d, p), now)

    def send_fwd(it, d, q):
        follow(sfwd(it - 1, d, q) if it > 0 else None, fwd(it, d, q))

    def send_sfwd(it, d, q):
        follow(fwd(it, d, q), sfwd(it, d, q))

    def gather_piece(it, p):
        for d in range(2):
            when(zhas[d], functools.partial(send_gz, it, d, p))

    def gather_own(it):
        for d in range(2):
            when(has[d], functools.partial(send_gy, it, d, 0))

    def relay(it, p, d):
        if p < 2:
            when(both(both(zfrom[d], has[p]), v == d), functools.partial(send_gy, it, p, 1 + d))

    def gather_take(it, p):
        for d in range(2):
            when(zfrom[d], gz(it, d, p).wait_recv)
            relay(it, p, d)

    def first_take(k):
        b0 = pl.multiple_of(blocks[k], CH)
        for d in range(2):
            z0 = (0, HZ + NH)[d]

            def take(d=d, z0=z0):
                first(d, k).wait_recv()
                ebuf[0, pl.ds(my + b0, CH), z0:z0 + HZ, :] = jnp.transpose(land[d, :, pl.ds(b0, CH), :], (1, 0, 2))
            when(zfrom[d], take)
            relay(0, k, d)

    def edge_own(it, d):
        def go():
            gyc(it, d, 0).wait_recv()
            for q in range(2):
                when(v == q, functools.partial(send_fwd, it, d, q))
        when(has[d], go)

    def gather_edge(it, d):
        for q in range(2):
            when(both(both(zed_has[1 + q], has[d]), v == q), gyc(it, d, 1 + q).wait_recv)
            when(both(has[d], v == 1 - q), fwd(it, d, q).wait_recv)

    def sent():
        it = ITERS - 1
        for d in range(2):
            def along_z(d=d):
                for p in range(NP):
                    sz(it, d, p).wait_send()
            when(zhas[d], along_z)

            def along_y(d=d):
                sy(it, d, 0).wait_send()
                for q in range(2):
                    when(both(zed_has[1 + q], v == q), diagonal(it, d, q).wait_send)
                    when(v == q, sfwd(it, d, q).wait_send)
            when(has[d], along_y)

    def scatter_edge(it, d):
        for q in range(2):
            when(both(both(zed_has[1 + q], has[d]), v == q), functools.partial(send_sy, it, d, 1 + q))
            when(both(has[d], v == q), functools.partial(send_sfwd, it, d, q))

    def scatter_own(it, d):
        r0 = row(HALO[d], my)
        for q in range(2):
            def add(q=q):
                z0 = (HZ, NH)[q]
                sfwd(it, d, q).wait_recv()
                cbuf[it, pl.ds(r0, my), z0:z0 + HZ, :] += sbuf[it, d]
            when(both(has[d], v == 1 - q), add)
        when(has[d], functools.partial(send_sy, it, d, 0))

    def scatter_piece(it, p):
        for d in range(2):
            when(zhas[d], functools.partial(send_sz, it, d, p))

    def scatter_end(it, p):
        r0 = row(EDGE[p], my)
        for q in range(2):
            z0 = ZED[1 + q][0]

            def add(q=q, z0=z0):
                sy(it, p, 1 + q).wait_recv()
                cbuf[it, pl.ds(r0, my), z0:z0 + HZ, :] += rybuf[it, p, :, z0:z0 + HZ, :]
            when(both(both(zed_has[1 + q], has[p]), v == q), add)
            when(both(zed_has[1 + q], v == q), functools.partial(send_sz, it, 1 - q, p))

    def scatter_near(it, p):
        for q in range(2):
            when(v == 1 - q, functools.partial(send_sz, it, 1 - q, p))

    def scatter_take(it, p):
        n = ROWS[p][1]
        r0 = row(*ROWS[p])
        if p < 2:
            def add_y():
                sy(it, p, 0).wait_recv()
                cbuf[it, pl.ds(row(EDGE[p], my), my), HZ:HZ + NH, :] += rybuf[it, p, :, HZ:HZ + NH, :]
            when(has[p], add_y)
            if it + 1 == ITERS:
                for q in range(2):
                    def add_diagonal(q=q):
                        z0 = (NH, HZ)[q]
                        diagonal(it, p, q).wait_recv()
                        cbuf[it, pl.ds(row(EDGE[p], my), my), z0:z0 + HZ, :] += rybuf[it, p, :, 0:HZ, :]
                    when(both(both(zed_has[2 - q], has[p]), v == 1 - q), add_diagonal)
        for d in range(2):
            z0 = (HZ, NH)[d]

            def add_z(d=d, z0=z0):
                sz(it, d, p).wait_recv()
                cbuf[it, pl.ds(r0, n), z0:z0 + HZ, :] += rzbuf[it, d, pl.ds(r0 - my, n)]
            when(zfrom[d], add_z)

    with scope("Wload"):
        load_start.wait()
    ebuf[0, my:my + NY, HZ:HZ + NH, :] = jnp.transpose(stage[0], (1, 0, 2))
    gather_own(0)
    mine[...] = jnp.zeros_like(mine)
    for k, (raw, taps) in enumerate(((raw_z, KZ), (raw_y, KY), (raw_x, KX))):
        loads[k].wait()
        mine[k:k + 1, 0:taps] = raw[...] / jnp.sum(raw[...], axis=1, keepdims=True)
    swap_prof = pltpu.make_async_remote_copy(
        src_ref=mine, dst_ref=theirs, send_sem=xssem.at[0], recv_sem=xrsem.at[0],
        device_id=partner, device_id_type=MESH)
    swap_prof.start()
    swap_obs = pltpu.make_async_remote_copy(
        src_ref=obs_hbm.at[0, pl.ds((1 - v) * NH, NH)], dst_ref=obs_z.at[v],
        send_sem=xssem.at[1], recv_sem=xrsem.at[1], device_id=partner, device_id_type=MESH)
    swap_obs.start()

    with scope("Wprof"):
        swap_prof.wait()
    own, other = mine[...], theirs[...]
    prof = (jnp.where(v == 0, own, other), jnp.where(v == 0, other, own))

    def tap(view, k, a):
        return prof[view][k:k + 1, a:a + 1]

    rows = lax.broadcasted_iota(jnp.int32, (NE, 3 * NE), 0)
    cols = lax.broadcasted_iota(jnp.int32, (NE, 3 * NE), 1)
    third = cols // NE
    cols = cols - third * NE

    def banded(diff, view, k, taps):
        w = jnp.zeros(diff.shape, F32)
        for a in range(taps):
            w = jnp.where(diff == a, tap(view, k, a), w)
        return w

    off = HZ - mz
    for ref, inner, outer in ((wf, rows, cols), (wb, cols, rows)):
        second = inner >= NH
        diff = outer - jnp.where(second, inner - NH, inner) - off
        w = jnp.where(second, banded(diff, 1, 0, KZ), banded(diff, 0, 0, KZ))
        high, low = split(w)
        ref[...] = jnp.where(third == 2, low.astype(F32), high.astype(F32)).astype(BF16)
    for view in range(2):
        for back in range(2):
            for r0 in range(0, NX, 64):
                r = lax.broadcasted_iota(jnp.int32, (64, NX), 0) + r0
                c = lax.broadcasted_iota(jnp.int32, (64, NX), 1)
                diff = (c - r if back else r - c) + mx
                high, low = split(banded(diff, view, 2, KX))
                tx[view, back, 0, r0:r0 + 64, :] = high
                tx[view, back, 1, r0:r0 + 64, :] = low
    wy = [[jnp.broadcast_to(tap(view, 1, b), (NH, NX)) for b in range(KY)] for view in range(2)]

    qbuf[0:2 * my] = jnp.zeros((2 * my, NE, NX), F32)
    qbuf[2 * my + NY:] = jnp.zeros((2 * my, NE, NX), F32)

    with scope("Wobs"):
        load_obs.wait()
        swap_obs.wait()
    for view in range(2):
        obs_t[view] = jnp.transpose(obs_z[view], (1, 0, 2))

    def xblur(high, low, view, back):
        both_ = jnp.concatenate([high, low], axis=0)
        n = high.shape[0]
        d = jnp.dot(both_, tx[view, back, 0], preferred_element_type=F32)
        d2 = jnp.dot(high, tx[view, back, 1], preferred_element_type=F32)
        return d[:n] + (d[n:] + d2)

    def stacked(x):
        high, low = split(x)
        return jnp.concatenate([high, low, high], axis=0)

    for it in range(ITERS):
        def zrows(i0, n, it=it):
            with scope(f"z{it}_{i0}"):
                r0 = row(i0, n)
                for y in range(n):
                    zbuf[r0 + y] = jnp.dot(wf[...], stacked(ebuf[it, r0 + y]), preferred_element_type=F32)

        def qrows(o0, n, it=it):
            with scope(f"q{it}_{o0}"):
                y0 = row(o0 + my, n) - my
                for view in range(2):
                    z0 = view * NH
                    for y in range(n):
                        acc = wy[view][0] * zbuf[y0 + y, z0:z0 + NH, :]
                        for b in range(1, KY):
                            acc = acc + wy[view][b] * zbuf[y0 + y + b, z0:z0 + NH, :]
                        high, low = split(acc)
                        ybuf[view, 0, y * NH:(y + 1) * NH, :] = high
                        ybuf[view, 1, y * NH:(y + 1) * NH, :] = low
                for view in range(2):
                    z0 = view * NH
                    m = n * NH
                    blurred = xblur(ybuf[view, 0, 0:m], ybuf[view, 1, 0:m], view, 0)
                    quotient = obs_t[view, pl.ds(y0, n)].reshape(m, NX) / blurred
                    high, low = split(quotient)
                    ybuf[view, 2, 0:m] = high
                    ybuf[view, 3, 0:m] = low
                    qbuf[pl.ds(2 * my + y0, n), z0:z0 + NH, :] = xblur(
                        ybuf[view, 2, 0:m], ybuf[view, 3, 0:m], view, 1).reshape(n, NH, NX)

        def crows(i0, n, it=it):
            with scope(f"c{it}_{i0}"):
                r0 = row(i0, n)
                for y in range(n):
                    r = r0 + y
                    parts = []
                    for view in range(2):
                        z0 = view * NH
                        acc = wy[view][0] * qbuf[r + 2 * my, z0:z0 + NH, :]
                        for b in range(1, KY):
                            acc = acc + wy[view][b] * qbuf[r + 2 * my - b, z0:z0 + NH, :]
                        parts.append(acc)
                    cbuf[it, r] = jnp.dot(wb[...], stacked(jnp.concatenate(parts, axis=0)),
                                          preferred_element_type=F32)

        def low_edge(it=it):
            edge_own(it, 1)
            gather_edge(it, 1)
            zrows(0, my)
        if it == 0:
            with scope("Wg0_in"):
                first_take(0)
            zrows(my + CH, CH)
            with scope("Wge0own"):
                edge_own(it, 0)
            with scope("Wg0_out"):
                first_take(1)
            zrows(my, CH)
            when(has[1], low_edge)
            qrows(0, OUT)
        else:
            for p in (1, 2):
                with scope(f"Wg{it}_{p}"):
                    gather_take(it, p)
                zrows(*ROWS[p])
            when(has[1], low_edge)
            qrows(0, my + 1)
            with scope(f"Wg{it}_3"):
                gather_take(it, 3)
            zrows(*ROWS[3])
            qrows(my + 1, OUT - my - 1)

        def low_scatter(it=it):
            crows(0, my)
            scatter_edge(it, 1)

        def high_edge(it=it):
            with scope(f"Wge{it}"):
                gather_edge(it, 0)
            zrows(my + NY, my)

        def high_scatter(it=it):
            crows(my + NY, my)
            scatter_edge(it, 0)

        when(has[1], low_scatter)
        crows(*ROWS[1])
        when(jnp.logical_not(has[1]), functools.partial(scatter_piece, it, 1))
        if it == 0:
            qrows(OUT, MID)
            crows(2 * my + 1, NY - 3 * my - 1)
            scatter_piece(it, 2)
            scatter_piece(it, 3)
            when(has[0], high_edge)
            qrows(OUT + MID, my)
            when(has[0], high_scatter)
            crows(NY - my, 2 * my)
            scatter_piece(it, 4)
            scatter_near(it, 0)
            with scope(f"Wse{it}"):
                scatter_end(it, 0)
            scatter_own(it, 0)
        else:
            with scope(f"Wg{it}_0"):
                gather_take(it, 0)
            with scope(f"Wge{it}own"):
                edge_own(it, 0)
            with scope(f"Wg{it}_4"):
                gather_take(it, 4)
            zrows(NY - my, 2 * my)
            qrows(OUT, MID)
            crows(2 * my + 1, NY - 3 * my - 1)
            scatter_piece(it, 2)
            scatter_piece(it, 3)
            when(has[0], high_edge)
            qrows(OUT + MID, my)
            when(has[0], high_scatter)
            crows(NY - my, 2 * my)
            scatter_piece(it, 0)
            scatter_piece(it, 4)
            with scope(f"Wso{it}"):
                scatter_own(it, 0)

        def low_end(it=it):
            scatter_own(it, 1)
            if it + 1 < ITERS:
                scatter_near(it, 1)
                scatter_end(it, 1)
            else:
                scatter_piece(it, 1)
        when(has[1], low_end)
        def update(p, it=it):
            n = ROWS[p][1]
            r0 = row(*ROWS[p])
            with scope(f"Wst{it}_{p}"):
                scatter_take(it, p)
            new = ebuf[it, pl.ds(r0, n), HZ:HZ + NH, :] * (0.5 * cbuf[it, pl.ds(r0, n), HZ:HZ + NH, :])
            if it + 1 < ITERS:
                ebuf[it + 1, pl.ds(r0, n), HZ:HZ + NH, :] = new
            else:
                zbuf[pl.ds(r0, n), 0:NH, :] = new

        if it + 1 < ITERS:
            for p in (1, 2, 3):
                update(p)
                gather_piece(it + 1, p)
            update(0)
            gather_piece(it + 1, 0)
            gather_own(it + 1)
            update(4)
            gather_piece(it + 1, 4)
        else:
            outs = []
            for k, pieces in enumerate(((1, 2, 3), (4, 0))):
                for p in pieces:
                    update(p)
                b0 = pl.multiple_of(blocks[1 - k], CH)
                stage[0, :, pl.ds(b0, CH), :] = jnp.transpose(zbuf[pl.ds(my + b0, CH), 0:NH, :], (1, 0, 2))
                src = stage.at[0, :, pl.ds(b0, CH)]
                dst = out_hbm.at[pl.ds(v * NH, NH), pl.ds(b0, CH)]
                outs.append(pltpu.make_async_copy(src, dst, lsem.at[k]))
                outs.append(pltpu.make_async_remote_copy(
                    src_ref=src, dst_ref=dst, send_sem=xssem.at[k], recv_sem=xrsem.at[k],
                    device_id=partner, device_id_type=MESH))
                outs[-1].start()
                outs[-2].start()
            with scope("Wsent2"):
                sent()
            with scope("Wout"):
                for out in outs:
                    out.wait()


def store(src, dst, sem):
    copy = pltpu.make_async_copy(src, dst, sem)
    copy.start()
    copy.wait()


def on_device(S, G, observed, start, spread_z, spread_y, spread_x):
    NZ, NY, NX = start.shape
    KZ, KY, KX = spread_z.shape[1], spread_y.shape[1], spread_x.shape[1]
    NH = NZ // 2
    my = KY // 2
    HZ = -(-(KZ // 2) // 8) * 8
    NE, NR = NH + 2 * HZ, NY + 2 * my
    dims = (NH, NY, NX, HZ, KZ, KY, KX, S, G)
    vm = pltpu.VMEM
    hbm = pl.BlockSpec(memory_space=pltpu.HBM)
    out = pl.pallas_call(
        functools.partial(kernel, dims),
        out_shape=jax.ShapeDtypeStruct((NZ, NY, NX), F32),
        in_specs=[hbm] * 5,
        out_specs=pl.BlockSpec(memory_space=pl.ANY),
        scratch_shapes=[
            vm((1, KZ), F32), vm((1, KY), F32), vm((1, KX), F32),
            vm((1, NH, NY, NX), F32), vm((2, HZ, NY, NX), F32),
            vm((2, NH, NY, NX), F32), vm((2, NY, NH, NX), F32),
            vm((8, 128), F32), vm((8, 128), F32),
            vm((NE, 3 * NE), BF16), vm((NE, 3 * NE), BF16), vm((2, 2, 2, NX, NX), BF16),
            vm((NR, NE, NX), F32), vm((2, 4, NY // 2 * NH, NX), BF16), vm((NY + 4 * my, NE, NX), F32),
            vm((ITERS, NR, NE, NX), F32), vm((ITERS, NR, NE, NX), F32),
            vm((ITERS, 2, my, NE, NX), F32), vm((ITERS, 2, NY, HZ, NX), F32), vm((ITERS, 2, my, HZ, NX), F32),
            pltpu.SemaphoreType.DMA((5,)), pltpu.SemaphoreType.DMA((16,)), pltpu.SemaphoreType.DMA((32,)),
            pltpu.SemaphoreType.DMA((2,)), pltpu.SemaphoreType.DMA((2,)),
        ],
        compiler_params=pltpu.CompilerParams(
            collective_id=0, has_side_effects=True, vmem_limit_bytes=24 << 20),
    )(*(pltpu.with_memory_space_constraint(x, pltpu.HBM) for x in (observed, start, spread_z, spread_y, spread_x)))
    return pl.pallas_call(
        store,
        out_shape=jax.ShapeDtypeStruct((NZ, NY, NX), F32),
        in_specs=[pl.BlockSpec(memory_space=pl.ANY)],
        out_specs=hbm,
        scratch_shapes=[pltpu.SemaphoreType.DMA],
        compiler_params=pltpu.CompilerParams(vmem_limit_bytes=4 << 20),
    )(out)


def solution(mesh):
    S, G = 2 * mesh.shape["gz"], mesh.shape["gy"]
    return jax.shard_map(
        functools.partial(on_device, S, G),
        mesh=mesh,
        in_specs=(
            P("view", "gz", "gy", None),
            P("gz", "gy", None),
            P("view", None),
            P("view", None),
            P("view", None),
        ),
        out_specs=P("gz", "gy", None),
        check_vma=False,
    )
```

```python
import contextlib
import functools

import jax
import jax.numpy as jnp
from jax import lax
from jax.experimental import pallas as pl
from jax.experimental.pallas import tpu as pltpu
from jax.sharding import PartitionSpec as P

ITERS = 2
MESH = pl.DeviceIdType.MESH
F32 = jnp.float32
BF16 = jnp.bfloat16


def scope(name):
    return contextlib.nullcontext()


def split(x):
    high = x.astype(BF16)
    return high, (x - high.astype(F32)).astype(BF16)


def kernel(dims, obs_hbm, start_hbm, sz_ref, sy_ref, sx_ref, out_hbm,
           raw_z, raw_y, raw_x, stage, land, obs_z, obs_t, mine, theirs, wf, wb, tx, zbuf, ybuf, qbuf,
           ebuf, cbuf, rybuf, rzbuf, sbuf, lsem, ssem, rsem, xssem, xrsem):
    NH, NY, NX, HZ, KZ, KY, KX, S, G = dims
    my, mz, mx = KY // 2, KZ // 2, KX // 2
    NE, NR, NQ = NH + 2 * HZ, NY + 2 * my, NY + 4 * my
    CH, NP = NY // 2, 5
    assert NH >= 2 * HZ
    v = lax.axis_index("view")
    gy = lax.axis_index("gy")
    s = 2 * lax.axis_index("gz") + v
    up_z, dn_z = s < S - 1, s > 0
    up_y, dn_y = gy < G - 1, gy > 0
    f = lax.rem(gy, 2)
    has = (jnp.logical_or(jnp.logical_and(f == 0, up_y), jnp.logical_and(f == 1, dn_y)),
           jnp.logical_or(jnp.logical_and(f == 0, dn_y), jnp.logical_and(f == 1, up_y)))

    def row(i0, n=1):
        return i0 + f * (NR - 2 * i0 - n)

    def qrow(j0, n=1):
        return j0 + f * (NQ - 2 * j0 - n)

    def zdev(t):
        t = lax.rem(t + S, S)
        return {"view": lax.rem(t, 2), "gz": t // 2}

    zto = (zdev(s + 1), zdev(s - 1))
    step = 1 - 2 * f
    yto = ({"gy": lax.rem(gy + step + G, G)}, {"gy": lax.rem(gy - step + G, G)})
    partner = {"view": 1 - v}
    zout = dict(zdev(s - 1 + 2 * v))
    diag = tuple({**zout, **yto[d]} for d in range(2))
    zhas, zfrom = (up_z, dn_z), (dn_z, up_z)

    def when(cond, fn):
        @pl.when(cond)
        def _():
            fn()

    def both(a, b):
        return jnp.logical_and(a, b)

    barrier = pltpu.get_barrier_semaphore()
    greet = ((up_z, zto[0]), (dn_z, zto[1]), (has[0], yto[0]), (has[1], yto[1]))
    for there, to in greet:
        @pl.when(there)
        def _(to=to):
            pl.semaphore_signal(barrier, inc=1, device_id=to, device_id_type=MESH)

    load_start = pltpu.make_async_copy(start_hbm.at[pl.ds(v * NH, NH)], stage.at[0], lsem.at[0])
    load_start.start()
    load_obs = pltpu.make_async_copy(obs_hbm.at[0, pl.ds(v * NH, NH)], obs_z.at[v], lsem.at[1])
    load_obs.start()
    loads = [pltpu.make_async_copy(ref, raw, lsem.at[2 + k])
             for k, (ref, raw) in enumerate(((sz_ref, raw_z), (sy_ref, raw_y), (sx_ref, raw_x)))]
    for load in loads:
        load.start()

    blocks = (CH * (1 - f), CH * f)

    def first(d, k):
        b0 = pl.multiple_of(blocks[k], CH)
        src0 = v * NH + (NH - mz, 0)[d]
        dst0 = (HZ - mz, 0)[d]
        return pltpu.make_async_remote_copy(
            src_ref=start_hbm.at[pl.ds(src0, mz), pl.ds(b0, CH)],
            dst_ref=land.at[d, pl.ds(dst0, mz), pl.ds(b0, CH)],
            send_sem=ssem.at[NP * d + k], recv_sem=rsem.at[NP * d + k], device_id=zto[d], device_id_type=MESH)

    peers = sum(there.astype(jnp.int32) for there, _ in greet)
    with scope("Wbar"):
        pl.semaphore_wait(barrier, peers)
    for k in range(2):
        for d in range(2):
            when(zhas[d], first(d, k).start)

    land[0, 0:HZ - mz] = jnp.zeros((HZ - mz, NY, NX), F32)
    land[1, mz:HZ] = jnp.zeros((HZ - mz, NY, NX), F32)
    for d in range(2):
        def blank(d=d):
            for it in range(ITERS):
                z0 = (0, HZ + NH)[d]
                ebuf[it, :, z0:z0 + HZ, :] = jnp.zeros((NR, HZ, NX), F32)
        when(jnp.logical_not(zfrom[d]), blank)

        def blank_rows(d=d):
            zbuf[pl.ds(row((my + NY, 0)[d], my), my)] = jnp.zeros((my, NE, NX), F32)
        when(jnp.logical_not(has[d]), blank_rows)

    def copy(send, recv, src, dst, to):
        return pltpu.make_async_remote_copy(
            src_ref=src, dst_ref=dst, send_sem=ssem.at[send], recv_sem=rsem.at[recv],
            device_id=to, device_id_type=MESH)

    ROWS = ((NY, my), (my, my + 1), (2 * my + 1, NY - 4 * my - 1), (NY - 2 * my, my), (NY - my, my))
    OUT, MID = NY - 3 * my, 2 * my
    assert len(ROWS) == NP
    ZED = ((HZ, NH), (0, HZ), (HZ + NH, HZ))
    zed_has = (None, dn_z, up_z)
    EDGE, HALO = (NY, my), (my + NY, 0)
    THERE = (f * (my + NY), (1 - f) * (my + NY))

    def gz(it, d, p):
        e = ebuf.at[it]
        src0, dst0 = ((NH, 0), (HZ, HZ + NH))[d]
        n = ROWS[p][1]
        r0 = row(*ROWS[p])
        return copy(NP * d + p, NP * d + p, e.at[pl.ds(r0, n), pl.ds(src0, HZ)],
                    e.at[pl.ds(r0, n), pl.ds(dst0, HZ)], zto[d])

    def gyc(it, d, p):
        e = ebuf.at[it]
        z0, n = ZED[p]
        k = 2 * min(p, 1) + d
        return copy(2 * NP + k, 4 * NP + k, e.at[pl.ds(row(EDGE[d], my), my), pl.ds(z0, n)],
                    e.at[pl.ds(THERE[d], my), pl.ds(z0, n)], yto[d])

    HH = NH // 2

    def sy_own(it, d, near):
        z0 = pl.multiple_of(HZ + HH * (1 - v if near else v), 8)
        return copy(2 * NP + (6 + d if near else d), 4 * NP + 6 + (6 + d if near else d),
                    cbuf.at[it, pl.ds(row(HALO[d], my), my), pl.ds(z0, HH)],
                    rybuf.at[it, d, :, pl.ds(z0, HH)], yto[d])

    def fwd(it, d, q):
        rows_ = pl.ds(row(HALO[d], my), my)
        e = ebuf.at[it]
        return copy(2 * NP + 4 + d, 4 * NP + 4 + d, e.at[rows_, pl.ds((NH, HZ)[q], HZ)],
                    e.at[rows_, pl.ds((0, HZ + NH)[q], HZ)], partner)

    def sfwd(it, d, q):
        rows_ = pl.ds(row(HALO[d], my), my)
        return copy(2 * NP + 4 + d, 4 * NP + 10 + d, cbuf.at[it, rows_, pl.ds((HZ + NH, 0)[q], HZ)],
                    sbuf.at[it, d], partner)

    def diagonal(it, d, q):
        z0, n = ZED[1 + q]
        return copy(2 * NP + 2 + d, 4 * NP + 8 + d, cbuf.at[it, pl.ds(row(HALO[d], my), my), pl.ds(z0, n)],
                    rybuf.at[it, d, :, pl.ds(0, HZ)], diag[d])

    def sz(it, d, p):
        src0 = (HZ + NH, 0)[d]
        n = ROWS[p][1]
        r0 = row(*ROWS[p])
        return copy(NP * d + p, 2 * NP + NP * d + p, cbuf.at[it, pl.ds(r0, n), pl.ds(src0, HZ)],
                    rzbuf.at[it, d, pl.ds(r0 - my, n)], zto[d])

    def sy(it, d, p):
        z0, n = ZED[p]
        k = 2 * min(p, 1) + d
        return copy(2 * NP + k, 4 * NP + 6 + k, cbuf.at[it, pl.ds(row(HALO[d], my), my), pl.ds(z0, n)],
                    rybuf.at[it, d, :, pl.ds(z0, n)], yto[d])

    def follow(before, now):
        if before is not None:
            before.wait_send()
        now.start()

    def send_gz(it, d, p):
        follow(sz(it - 1, d, p), gz(it, d, p))

    def send_sz(it, d, p):
        follow(gz(it, d, p) if it > 0 else first(d, p) if p < 2 else None, sz(it, d, p))

    def send_gy(it, d, p):
        before = None if it == 0 else sy_own(it - 1, d, False) if p == 0 else sy(it - 1, d, p)
        follow(before, gyc(it, d, p))

    def send_far(it, d):
        follow(gyc(it, d, 0), sy_own(it, d, False))

    def send_near(it, d):
        follow(sy_own(it - 1, d, True) if it > 0 else None, sy_own(it, d, True))

    def send_sy(it, d, p):
        now = diagonal(it, d, p - 1) if p > 0 and it + 1 == ITERS else sy(it, d, p)
        follow(gyc(it, d, p), now)

    def send_fwd(it, d, q):
        follow(sfwd(it - 1, d, q) if it > 0 else None, fwd(it, d, q))

    def send_sfwd(it, d, q):
        follow(fwd(it, d, q), sfwd(it, d, q))

    def gather_piece(it, p):
        for d in range(2):
            when(zhas[d], functools.partial(send_gz, it, d, p))

    def gather_own(it):
        for d in range(2):
            when(has[d], functools.partial(send_gy, it, d, 0))

    def relay(it, p, d):
        if p < 2:
            when(both(both(zfrom[d], has[p]), v == d), functools.partial(send_gy, it, p, 1 + d))

    def gather_take(it, p):
        for d in range(2):
            when(zfrom[d], gz(it, d, p).wait_recv)
            relay(it, p, d)

    def first_take(k):
        b0 = pl.multiple_of(blocks[k], CH)
        for d in range(2):
            z0 = (0, HZ + NH)[d]

            def take(d=d, z0=z0):
                first(d, k).wait_recv()
                ebuf[0, pl.ds(my + b0, CH), z0:z0 + HZ, :] = jnp.transpose(land[d, :, pl.ds(b0, CH), :], (1, 0, 2))
            when(zfrom[d], take)
            relay(0, k, d)

    def edge_own(it, d):
        def go():
            gyc(it, d, 0).wait_recv()
            for q in range(2):
                when(v == q, functools.partial(send_fwd, it, d, q))
        when(has[d], go)

    def gather_edge(it, d):
        for q in range(2):
            when(both(both(zed_has[1 + q], has[d]), v == q), gyc(it, d, 1 + q).wait_recv)
            when(both(has[d], v == 1 - q), fwd(it, d, q).wait_recv)

    def sent():
        it = ITERS - 1
        for d in range(2):
            def along_z(d=d):
                for p in range(NP):
                    sz(it, d, p).wait_send()
            when(zhas[d], along_z)

            def along_y(d=d):
                sy_own(it, d, False).wait_send()
                sy_own(it, d, True).wait_send()
                for q in range(2):
                    when(both(zed_has[1 + q], v == q), diagonal(it, d, q).wait_send)
                    when(v == q, sfwd(it, d, q).wait_send)
            when(has[d], along_y)

    def scatter_edge(it, d):
        for q in range(2):
            when(both(both(zed_has[1 + q], has[d]), v == q), functools.partial(send_sy, it, d, 1 + q))
            when(both(has[d], v == q), functools.partial(send_sfwd, it, d, q))
        when(has[d], functools.partial(send_far, it, d))

    def scatter_own(it, d):
        r0 = row(HALO[d], my)
        for q in range(2):
            def add(q=q):
                z0 = (HZ, NH)[q]
                sfwd(it, d, q).wait_recv()
                cbuf[it, pl.ds(r0, my), z0:z0 + HZ, :] += sbuf[it, d]
            when(both(has[d], v == 1 - q), add)
        when(has[d], functools.partial(send_near, it, d))

    def scatter_piece(it, p):
        for d in range(2):
            when(zhas[d], functools.partial(send_sz, it, d, p))

    def scatter_end(it, p):
        r0 = row(EDGE[p], my)
        for q in range(2):
            z0 = ZED[1 + q][0]

            def add(q=q, z0=z0):
                sy(it, p, 1 + q).wait_recv()
                cbuf[it, pl.ds(r0, my), z0:z0 + HZ, :] += rybuf[it, p, :, z0:z0 + HZ, :]
            when(both(both(zed_has[1 + q], has[p]), v == q), add)
            when(both(zed_has[1 + q], v == q), functools.partial(send_sz, it, 1 - q, p))

    def scatter_near(it, p):
        for q in range(2):
            when(v == 1 - q, functools.partial(send_sz, it, 1 - q, p))

    def scatter_take(it, p):
        n = ROWS[p][1]
        r0 = row(*ROWS[p])
        if p < 2:
            def add_y():
                sy_own(it, p, False).wait_recv()
                sy_own(it, p, True).wait_recv()
                cbuf[it, pl.ds(row(EDGE[p], my), my), HZ:HZ + NH, :] += rybuf[it, p, :, HZ:HZ + NH, :]
            when(has[p], add_y)
            if it + 1 == ITERS:
                for q in range(2):
                    def add_diagonal(q=q):
                        z0 = (NH, HZ)[q]
                        diagonal(it, p, q).wait_recv()
                        cbuf[it, pl.ds(row(EDGE[p], my), my), z0:z0 + HZ, :] += rybuf[it, p, :, 0:HZ, :]
                    when(both(both(zed_has[2 - q], has[p]), v == 1 - q), add_diagonal)
        for d in range(2):
            z0 = (HZ, NH)[d]

            def add_z(d=d, z0=z0):
                sz(it, d, p).wait_recv()
                cbuf[it, pl.ds(r0, n), z0:z0 + HZ, :] += rzbuf[it, d, pl.ds(r0 - my, n)]
            when(zfrom[d], add_z)

    with scope("Wload"):
        load_start.wait()
    ebuf[0, my:my + NY, HZ:HZ + NH, :] = jnp.transpose(stage[0], (1, 0, 2))
    gather_own(0)
    mine[...] = jnp.zeros_like(mine)
    for k, (raw, taps) in enumerate(((raw_z, KZ), (raw_y, KY), (raw_x, KX))):
        loads[k].wait()
        mine[k:k + 1, 0:taps] = raw[...] / jnp.sum(raw[...], axis=1, keepdims=True)
    swap_prof = pltpu.make_async_remote_copy(
        src_ref=mine, dst_ref=theirs, send_sem=xssem.at[0], recv_sem=xrsem.at[0],
        device_id=partner, device_id_type=MESH)
    swap_prof.start()
    swap_obs = pltpu.make_async_remote_copy(
        src_ref=obs_hbm.at[0, pl.ds((1 - v) * NH, NH)], dst_ref=obs_z.at[v],
        send_sem=xssem.at[1], recv_sem=xrsem.at[1], device_id=partner, device_id_type=MESH)
    swap_obs.start()

    with scope("Wprof"):
        swap_prof.wait()
    own, other = mine[...], theirs[...]
    prof = (jnp.where(v == 0, own, other), jnp.where(v == 0, other, own))

    def tap(view, k, a):
        return prof[view][k:k + 1, a:a + 1]

    rows = lax.broadcasted_iota(jnp.int32, (NE, 3 * NE), 0)
    cols = lax.broadcasted_iota(jnp.int32, (NE, 3 * NE), 1)
    third = cols // NE
    cols = cols - third * NE

    def banded(diff, view, k, taps):
        w = jnp.zeros(diff.shape, F32)
        for a in range(taps):
            w = jnp.where(diff == a, tap(view, k, a), w)
        return w

    off = HZ - mz
    for ref, inner, outer in ((wf, rows, cols), (wb, cols, rows)):
        second = inner >= NH
        diff = outer - jnp.where(second, inner - NH, inner) - off
        w = jnp.where(second, banded(diff, 1, 0, KZ), banded(diff, 0, 0, KZ))
        high, low = split(w)
        ref[...] = jnp.where(third == 2, low.astype(F32), high.astype(F32)).astype(BF16)
    for view in range(2):
        for back in range(2):
            for r0 in range(0, NX, 64):
                r = lax.broadcasted_iota(jnp.int32, (64, NX), 0) + r0
                c = lax.broadcasted_iota(jnp.int32, (64, NX), 1)
                diff = (c - r if back else r - c) + mx
                high, low = split(banded(diff, view, 2, KX))
                tx[view, back, 0, r0:r0 + 64, :] = high
                tx[view, back, 1, r0:r0 + 64, :] = low
    wy = [[jnp.broadcast_to(tap(view, 1, b), (NH, NX)) for b in range(KY)] for view in range(2)]

    qbuf[0:2 * my] = jnp.zeros((2 * my, NE, NX), F32)
    qbuf[2 * my + NY:] = jnp.zeros((2 * my, NE, NX), F32)

    with scope("Wobs"):
        load_obs.wait()
        swap_obs.wait()
    for view in range(2):
        obs_t[view] = jnp.transpose(obs_z[view], (1, 0, 2))

    def xblur(high, low, view, back):
        both_ = jnp.concatenate([high, low], axis=0)
        n = high.shape[0]
        d = jnp.dot(both_, tx[view, back, 0], preferred_element_type=F32)
        d2 = jnp.dot(high, tx[view, back, 1], preferred_element_type=F32)
        return d[:n] + (d[n:] + d2)

    def stacked(x):
        high, low = split(x)
        return jnp.concatenate([high, low, high], axis=0)

    for it in range(ITERS):
        def zrows(i0, n, it=it):
            with scope(f"z{it}_{i0}"):
                r0 = row(i0, n)
                for y in range(n):
                    zbuf[r0 + y] = jnp.dot(wf[...], stacked(ebuf[it, r0 + y]), preferred_element_type=F32)

        def qrows(o0, n, it=it):
            with scope(f"q{it}_{o0}"):
                y0 = row(o0 + my, n) - my
                for view in range(2):
                    z0 = view * NH
                    for y in range(n):
                        acc = wy[view][0] * zbuf[y0 + y, z0:z0 + NH, :]
                        for b in range(1, KY):
                            acc = acc + wy[view][b] * zbuf[y0 + y + b, z0:z0 + NH, :]
                        high, low = split(acc)
                        ybuf[view, 0, y * NH:(y + 1) * NH, :] = high
                        ybuf[view, 1, y * NH:(y + 1) * NH, :] = low
                for view in range(2):
                    z0 = view * NH
                    m = n * NH
                    blurred = xblur(ybuf[view, 0, 0:m], ybuf[view, 1, 0:m], view, 0)
                    quotient = obs_t[view, pl.ds(y0, n)].reshape(m, NX) / blurred
                    high, low = split(quotient)
                    ybuf[view, 2, 0:m] = high
                    ybuf[view, 3, 0:m] = low
                    qbuf[pl.ds(2 * my + y0, n), z0:z0 + NH, :] = xblur(
                        ybuf[view, 2, 0:m], ybuf[view, 3, 0:m], view, 1).reshape(n, NH, NX)

        def crows(i0, n, it=it):
            with scope(f"c{it}_{i0}"):
                r0 = row(i0, n)
                for y in range(n):
                    r = r0 + y
                    parts = []
                    for view in range(2):
                        z0 = view * NH
                        acc = wy[view][0] * qbuf[r + 2 * my, z0:z0 + NH, :]
                        for b in range(1, KY):
                            acc = acc + wy[view][b] * qbuf[r + 2 * my - b, z0:z0 + NH, :]
                        parts.append(acc)
                    cbuf[it, r] = jnp.dot(wb[...], stacked(jnp.concatenate(parts, axis=0)),
                                          preferred_element_type=F32)

        def low_edge(it=it):
            edge_own(it, 1)
            gather_edge(it, 1)
            zrows(0, my)
        if it == 0:
            with scope("Wg0_in"):
                first_take(0)
            zrows(my + CH, CH)
            with scope("Wge0own"):
                edge_own(it, 0)
            with scope("Wg0_out"):
                first_take(1)
            zrows(my, CH)
            when(has[1], low_edge)
            qrows(0, OUT)
        else:
            for p in (1, 2):
                with scope(f"Wg{it}_{p}"):
                    gather_take(it, p)
                zrows(*ROWS[p])
            when(has[1], low_edge)
            qrows(0, my + 1)
            with scope(f"Wg{it}_3"):
                gather_take(it, 3)
            zrows(*ROWS[3])
            qrows(my + 1, OUT - my - 1)

        def low_scatter(it=it):
            crows(0, my)
            scatter_edge(it, 1)

        def high_edge(it=it):
            with scope(f"Wge{it}"):
                gather_edge(it, 0)
            zrows(my + NY, my)

        def high_scatter(it=it):
            crows(my + NY, my)
            scatter_edge(it, 0)

        when(has[1], low_scatter)
        crows(*ROWS[1])
        when(jnp.logical_not(has[1]), functools.partial(scatter_piece, it, 1))
        if it == 0:
            qrows(OUT, MID)
            crows(2 * my + 1, NY - 3 * my - 1)
            scatter_piece(it, 2)
            scatter_piece(it, 3)
            when(has[0], high_edge)
            qrows(OUT + MID, my)
            when(has[0], high_scatter)
            crows(NY - my, 2 * my)
            scatter_piece(it, 4)
            scatter_near(it, 0)
            with scope(f"Wso{it}"):
                scatter_own(it, 0)
            with scope(f"Wse{it}"):
                scatter_end(it, 0)
        else:
            with scope(f"Wg{it}_0"):
                gather_take(it, 0)
            with scope(f"Wge{it}own"):
                edge_own(it, 0)
            with scope(f"Wg{it}_4"):
                gather_take(it, 4)
            zrows(NY - my, 2 * my)
            qrows(OUT, MID)
            crows(2 * my + 1, NY - 3 * my - 1)
            scatter_piece(it, 2)
            scatter_piece(it, 3)
            when(has[0], high_edge)
            qrows(OUT + MID, my)
            when(has[0], high_scatter)
            crows(NY - my, 2 * my)
            scatter_piece(it, 0)
            scatter_piece(it, 4)
            with scope(f"Wso{it}"):
                scatter_own(it, 0)

        def low_end(it=it):
            scatter_own(it, 1)
            if it + 1 < ITERS:
                scatter_near(it, 1)
                scatter_end(it, 1)
            else:
                scatter_piece(it, 1)
        when(has[1], low_end)
        def update(p, it=it):
            n = ROWS[p][1]
            r0 = row(*ROWS[p])
            with scope(f"Wst{it}_{p}"):
                scatter_take(it, p)
            new = ebuf[it, pl.ds(r0, n), HZ:HZ + NH, :] * (0.5 * cbuf[it, pl.ds(r0, n), HZ:HZ + NH, :])
            if it + 1 < ITERS:
                ebuf[it + 1, pl.ds(r0, n), HZ:HZ + NH, :] = new
            else:
                zbuf[pl.ds(r0, n), 0:NH, :] = new

        if it + 1 < ITERS:
            for p in (1, 2, 3):
                update(p)
                gather_piece(it + 1, p)
            update(0)
            gather_piece(it + 1, 0)
            gather_own(it + 1)
            update(4)
            gather_piece(it + 1, 4)
        else:
            outs = []
            def leave(k, h, count):
                b0 = pl.multiple_of(blocks[k], CH)
                stage[0, pl.ds(h, count), pl.ds(b0, CH), :] = jnp.transpose(
                    zbuf[pl.ds(my + b0, CH), pl.ds(h, count), :], (1, 0, 2))
                src = stage.at[0, pl.ds(h, count), pl.ds(b0, CH)]
                dst = out_hbm.at[pl.ds(v * NH + h, count), pl.ds(b0, CH)]
                n = len(outs) // 2
                outs.append(pltpu.make_async_copy(src, dst, lsem.at[n]))
                outs.append(pltpu.make_async_remote_copy(
                    src_ref=src, dst_ref=dst, send_sem=xssem.at[n], recv_sem=xrsem.at[n],
                    device_id=partner, device_id_type=MESH))
                outs[-1].start()
                outs[-2].start()

            def finish(p, near):
                n = ROWS[p][1]
                r0 = row(*ROWS[p])
                for q in range(2):
                    def half(q=q):
                        z0, h0 = (HZ, NH)[q], q * HH

                        def add():
                            sz(it, q, p).wait_recv()
                            cbuf[it, pl.ds(r0, n), z0:z0 + HZ, :] += rzbuf[it, q, pl.ds(r0 - my, n)]
                        when(zfrom[q], add)
                        if p == 0 and not near:
                            def add_diagonal():
                                diagonal(it, p, 1 - q).wait_recv()
                                cbuf[it, pl.ds(row(EDGE[p], my), my), z0:z0 + HZ, :] += rybuf[it, p, :, 0:HZ, :]
                            when(both(zfrom[q], has[p]), add_diagonal)
                        zbuf[pl.ds(r0, n), h0:h0 + HH, :] = (
                            ebuf[it, pl.ds(r0, n), HZ + h0:HZ + h0 + HH, :]
                            * (0.5 * cbuf[it, pl.ds(r0, n), HZ + h0:HZ + h0 + HH, :]))
                    when(v == (1 - q if near else q), half)

            for p in (1, 2, 3):
                update(p)
            leave(1, 0, NH)

            def add_own():
                sy_own(it, 0, False).wait_recv()
                sy_own(it, 0, True).wait_recv()
                cbuf[it, pl.ds(row(EDGE[0], my), my), HZ:HZ + NH, :] += rybuf[it, 0, :, HZ:HZ + NH, :]
            with scope("Wown"):
                when(has[0], add_own)
            with scope("Wnear"):
                finish(4, True)
                finish(0, True)
            leave(0, pl.multiple_of((1 - v) * HH, HH), HH)
            with scope("Wfar"):
                finish(4, False)
                finish(0, False)
            leave(0, pl.multiple_of(v * HH, HH), HH)
            with scope("Wsent2"):
                sent()
            with scope("Wout"):
                for out in outs:
                    out.wait()


def store(src, dst, sem):
    copy = pltpu.make_async_copy(src, dst, sem)
    copy.start()
    copy.wait()


def on_device(S, G, observed, start, spread_z, spread_y, spread_x):
    NZ, NY, NX = start.shape
    KZ, KY, KX = spread_z.shape[1], spread_y.shape[1], spread_x.shape[1]
    NH = NZ // 2
    my = KY // 2
    HZ = -(-(KZ // 2) // 8) * 8
    NE, NR = NH + 2 * HZ, NY + 2 * my
    dims = (NH, NY, NX, HZ, KZ, KY, KX, S, G)
    vm = pltpu.VMEM
    hbm = pl.BlockSpec(memory_space=pltpu.HBM)
    out = pl.pallas_call(
        functools.partial(kernel, dims),
        out_shape=jax.ShapeDtypeStruct((NZ, NY, NX), F32),
        in_specs=[hbm] * 5,
        out_specs=pl.BlockSpec(memory_space=pl.ANY),
        scratch_shapes=[
            vm((1, KZ), F32), vm((1, KY), F32), vm((1, KX), F32),
            vm((1, NH, NY, NX), F32), vm((2, HZ, NY, NX), F32),
            vm((2, NH, NY, NX), F32), vm((2, NY, NH, NX), F32),
            vm((8, 128), F32), vm((8, 128), F32),
            vm((NE, 3 * NE), BF16), vm((NE, 3 * NE), BF16), vm((2, 2, 2, NX, NX), BF16),
            vm((NR, NE, NX), F32), vm((2, 4, NY // 2 * NH, NX), BF16), vm((NY + 4 * my, NE, NX), F32),
            vm((ITERS, NR, NE, NX), F32), vm((ITERS, NR, NE, NX), F32),
            vm((ITERS, 2, my, NE, NX), F32), vm((ITERS, 2, NY, HZ, NX), F32), vm((ITERS, 2, my, HZ, NX), F32),
            pltpu.SemaphoreType.DMA((5,)), pltpu.SemaphoreType.DMA((18,)), pltpu.SemaphoreType.DMA((34,)),
            pltpu.SemaphoreType.DMA((3,)), pltpu.SemaphoreType.DMA((3,)),
        ],
        compiler_params=pltpu.CompilerParams(
            collective_id=0, has_side_effects=True, vmem_limit_bytes=24 << 20),
    )(*(pltpu.with_memory_space_constraint(x, pltpu.HBM) for x in (observed, start, spread_z, spread_y, spread_x)))
    return pl.pallas_call(
        store,
        out_shape=jax.ShapeDtypeStruct((NZ, NY, NX), F32),
        in_specs=[pl.BlockSpec(memory_space=pl.ANY)],
        out_specs=hbm,
        scratch_shapes=[pltpu.SemaphoreType.DMA],
        compiler_params=pltpu.CompilerParams(vmem_limit_bytes=4 << 20),
    )(out)


def solution(mesh):
    S, G = 2 * mesh.shape["gz"], mesh.shape["gy"]
    return jax.shard_map(
        functools.partial(on_device, S, G),
        mesh=mesh,
        in_specs=(
            P("view", "gz", "gy", None),
            P("gz", "gy", None),
            P("view", None),
            P("view", None),
            P("view", None),
        ),
        out_specs=P("gz", "gy", None),
        check_vma=False,
    )
```

```python
import contextlib
import functools

import jax
import jax.numpy as jnp
from jax import lax
from jax.experimental import pallas as pl
from jax.experimental.pallas import tpu as pltpu
from jax.sharding import PartitionSpec as P

ITERS = 2
MESH = pl.DeviceIdType.MESH
F32 = jnp.float32
BF16 = jnp.bfloat16


def scope(name):
    return contextlib.nullcontext()


def split(x):
    high = x.astype(BF16)
    return high, (x - high.astype(F32)).astype(BF16)


def kernel(dims, obs_hbm, start_hbm, sz_ref, sy_ref, sx_ref, out_hbm,
           raw_z, raw_y, raw_x, stage, land, obs_z, obs_t, mine, theirs, wf, wb, tx, zbuf, ybuf, qbuf,
           ebuf, cbuf, rybuf, rzbuf, sbuf, lsem, ssem, rsem, xssem, xrsem):
    NH, NY, NX, HZ, KZ, KY, KX, S, G = dims
    my, mz, mx = KY // 2, KZ // 2, KX // 2
    NE, NR, NQ = NH + 2 * HZ, NY + 2 * my, NY + 4 * my
    CH, NP = NY // 2, 5
    assert NH >= 2 * HZ
    v = lax.axis_index("view")
    gy = lax.axis_index("gy")
    s = 2 * lax.axis_index("gz") + v
    up_z, dn_z = s < S - 1, s > 0
    up_y, dn_y = gy < G - 1, gy > 0
    f = lax.rem(gy, 2)
    has = (jnp.logical_or(jnp.logical_and(f == 0, up_y), jnp.logical_and(f == 1, dn_y)),
           jnp.logical_or(jnp.logical_and(f == 0, dn_y), jnp.logical_and(f == 1, up_y)))

    def row(i0, n=1):
        return i0 + f * (NR - 2 * i0 - n)

    def qrow(j0, n=1):
        return j0 + f * (NQ - 2 * j0 - n)

    def zdev(t):
        t = lax.rem(t + S, S)
        return {"view": lax.rem(t, 2), "gz": t // 2}

    zto = (zdev(s + 1), zdev(s - 1))
    step = 1 - 2 * f
    yto = ({"gy": lax.rem(gy + step + G, G)}, {"gy": lax.rem(gy - step + G, G)})
    partner = {"view": 1 - v}
    zout = dict(zdev(s - 1 + 2 * v))
    diag = tuple({**zout, **yto[d]} for d in range(2))
    zhas, zfrom = (up_z, dn_z), (dn_z, up_z)

    def when(cond, fn):
        @pl.when(cond)
        def _():
            fn()

    def both(a, b):
        return jnp.logical_and(a, b)

    barrier = pltpu.get_barrier_semaphore()
    greet = ((up_z, zto[0]), (dn_z, zto[1]), (has[0], yto[0]), (has[1], yto[1]))
    for there, to in greet:
        @pl.when(there)
        def _(to=to):
            pl.semaphore_signal(barrier, inc=1, device_id=to, device_id_type=MESH)

    load_start = pltpu.make_async_copy(start_hbm.at[pl.ds(v * NH, NH)], stage.at[0], lsem.at[0])
    load_start.start()
    load_obs = pltpu.make_async_copy(obs_hbm.at[0, pl.ds(v * NH, NH)], obs_z.at[v], lsem.at[1])
    load_obs.start()
    loads = [pltpu.make_async_copy(ref, raw, lsem.at[2 + k])
             for k, (ref, raw) in enumerate(((sz_ref, raw_z), (sy_ref, raw_y), (sx_ref, raw_x)))]
    for load in loads:
        load.start()

    blocks = (CH * (1 - f), CH * f)

    def first(d, k):
        b0 = pl.multiple_of(blocks[k], CH)
        src0 = v * NH + (NH - mz, 0)[d]
        dst0 = (HZ - mz, 0)[d]
        return pltpu.make_async_remote_copy(
            src_ref=start_hbm.at[pl.ds(src0, mz), pl.ds(b0, CH)],
            dst_ref=land.at[d, pl.ds(dst0, mz), pl.ds(b0, CH)],
            send_sem=ssem.at[NP * d + k], recv_sem=rsem.at[NP * d + k], device_id=zto[d], device_id_type=MESH)

    peers = sum(there.astype(jnp.int32) for there, _ in greet)
    with scope("Wbar"):
        pl.semaphore_wait(barrier, peers)
    for k in range(2):
        for d in range(2):
            when(zhas[d], first(d, k).start)

    land[0, 0:HZ - mz] = jnp.zeros((HZ - mz, NY, NX), F32)
    land[1, mz:HZ] = jnp.zeros((HZ - mz, NY, NX), F32)
    for d in range(2):
        def blank(d=d):
            for it in range(ITERS):
                z0 = (0, HZ + NH)[d]
                ebuf[it, :, z0:z0 + HZ, :] = jnp.zeros((NR, HZ, NX), F32)
        when(jnp.logical_not(zfrom[d]), blank)

        def blank_rows(d=d):
            zbuf[pl.ds(row((my + NY, 0)[d], my), my)] = jnp.zeros((my, NE, NX), F32)
        when(jnp.logical_not(has[d]), blank_rows)

    def copy(send, recv, src, dst, to):
        return pltpu.make_async_remote_copy(
            src_ref=src, dst_ref=dst, send_sem=ssem.at[send], recv_sem=rsem.at[recv],
            device_id=to, device_id_type=MESH)

    ROWS = ((NY, my), (my, my + 1), (2 * my + 1, NY - 4 * my - 1), (NY - 2 * my, my), (NY - my, my))
    OUT, MID = NY - 3 * my, 2 * my
    assert len(ROWS) == NP
    ZED = ((HZ, NH), (0, HZ), (HZ + NH, HZ))
    zed_has = (None, dn_z, up_z)
    EDGE, HALO = (NY, my), (my + NY, 0)
    THERE = (f * (my + NY), (1 - f) * (my + NY))

    def gz(it, d, p):
        e = ebuf.at[it]
        src0, dst0 = ((NH, 0), (HZ, HZ + NH))[d]
        n = ROWS[p][1]
        r0 = row(*ROWS[p])
        return copy(NP * d + p, NP * d + p, e.at[pl.ds(r0, n), pl.ds(src0, HZ)],
                    e.at[pl.ds(r0, n), pl.ds(dst0, HZ)], zto[d])

    def gyc(it, d, p):
        e = ebuf.at[it]
        z0, n = ZED[p]
        k = 2 * min(p, 1) + d
        return copy(2 * NP + k, 4 * NP + k, e.at[pl.ds(row(EDGE[d], my), my), pl.ds(z0, n)],
                    e.at[pl.ds(THERE[d], my), pl.ds(z0, n)], yto[d])

    HH = NH // 2

    def sy_own(it, d, near):
        z0 = pl.multiple_of(HZ + HH * (1 - v if near else v), 8)
        return copy(2 * NP + (6 + d if near else d), 4 * NP + 6 + (6 + d if near else d),
                    cbuf.at[it, pl.ds(row(HALO[d], my), my), pl.ds(z0, HH)],
                    rybuf.at[it, d, :, pl.ds(z0, HH)], yto[d])

    def fwd(it, d, q):
        rows_ = pl.ds(row(HALO[d], my), my)
        e = ebuf.at[it]
        return copy(2 * NP + 4 + d, 4 * NP + 4 + d, e.at[rows_, pl.ds((NH, HZ)[q], HZ)],
                    e.at[rows_, pl.ds((0, HZ + NH)[q], HZ)], partner)

    def sfwd(it, d, q):
        rows_ = pl.ds(row(HALO[d], my), my)
        return copy(2 * NP + 4 + d, 4 * NP + 10 + d, cbuf.at[it, rows_, pl.ds((HZ + NH, 0)[q], HZ)],
                    sbuf.at[it, d], partner)

    def diagonal(it, d, q):
        z0, n = ZED[1 + q]
        return copy(2 * NP + 2 + d, 4 * NP + 8 + d, cbuf.at[it, pl.ds(row(HALO[d], my), my), pl.ds(z0, n)],
                    rybuf.at[it, d, :, pl.ds(0, HZ)], diag[d])

    def sz(it, d, p):
        src0 = (HZ + NH, 0)[d]
        n = ROWS[p][1]
        r0 = row(*ROWS[p])
        return copy(NP * d + p, 2 * NP + NP * d + p, cbuf.at[it, pl.ds(r0, n), pl.ds(src0, HZ)],
                    rzbuf.at[it, d, pl.ds(r0 - my, n)], zto[d])

    def sy(it, d, p):
        z0, n = ZED[p]
        k = 2 * min(p, 1) + d
        return copy(2 * NP + k, 4 * NP + 6 + k, cbuf.at[it, pl.ds(row(HALO[d], my), my), pl.ds(z0, n)],
                    rybuf.at[it, d, :, pl.ds(z0, n)], yto[d])

    def follow(before, now):
        if before is not None:
            before.wait_send()
        now.start()

    def send_gz(it, d, p):
        follow(sz(it - 1, d, p), gz(it, d, p))

    def send_sz(it, d, p):
        follow(gz(it, d, p) if it > 0 else first(d, p) if p < 2 else None, sz(it, d, p))

    def send_gy(it, d, p):
        before = None if it == 0 else sy_own(it - 1, d, False) if p == 0 else sy(it - 1, d, p)
        follow(before, gyc(it, d, p))

    def send_far(it, d):
        follow(gyc(it, d, 0), sy_own(it, d, False))

    def send_near(it, d):
        follow(sy_own(it - 1, d, True) if it > 0 else None, sy_own(it, d, True))

    def send_sy(it, d, p):
        now = diagonal(it, d, p - 1) if p > 0 and it + 1 == ITERS else sy(it, d, p)
        follow(gyc(it, d, p), now)

    def send_fwd(it, d, q):
        follow(sfwd(it - 1, d, q) if it > 0 else None, fwd(it, d, q))

    def send_sfwd(it, d, q):
        follow(fwd(it, d, q), sfwd(it, d, q))

    def gather_piece(it, p):
        for d in range(2):
            when(zhas[d], functools.partial(send_gz, it, d, p))

    def gather_own(it):
        for d in range(2):
            when(has[d], functools.partial(send_gy, it, d, 0))

    def relay(it, p, d):
        if p < 2:
            when(both(both(zfrom[d], has[p]), v == d), functools.partial(send_gy, it, p, 1 + d))

    def gather_take(it, p):
        for d in range(2):
            when(zfrom[d], gz(it, d, p).wait_recv)
            relay(it, p, d)

    def first_take(k):
        b0 = pl.multiple_of(blocks[k], CH)
        for d in range(2):
            z0 = (0, HZ + NH)[d]

            def take(d=d, z0=z0):
                first(d, k).wait_recv()
                ebuf[0, pl.ds(my + b0, CH), z0:z0 + HZ, :] = jnp.transpose(land[d, :, pl.ds(b0, CH), :], (1, 0, 2))
            when(zfrom[d], take)
            relay(0, k, d)

    def edge_own(it, d):
        def go():
            gyc(it, d, 0).wait_recv()
            for q in range(2):
                when(v == q, functools.partial(send_fwd, it, d, q))
        when(has[d], go)

    def gather_edge(it, d):
        for q in range(2):
            when(both(both(zed_has[1 + q], has[d]), v == q), gyc(it, d, 1 + q).wait_recv)
            when(both(has[d], v == 1 - q), fwd(it, d, q).wait_recv)

    def sent():
        it = ITERS - 1
        for d in range(2):
            def along_z(d=d):
                for p in range(NP):
                    sz(it, d, p).wait_send()
            when(zhas[d], along_z)

            def along_y(d=d):
                sy_own(it, d, False).wait_send()
                sy_own(it, d, True).wait_send()
                for q in range(2):
                    when(both(zed_has[1 + q], v == q), diagonal(it, d, q).wait_send)
                    when(v == q, sfwd(it, d, q).wait_send)
            when(has[d], along_y)

    def scatter_edge(it, d):
        for q in range(2):
            when(both(both(zed_has[1 + q], has[d]), v == q), functools.partial(send_sy, it, d, 1 + q))
            when(both(has[d], v == q), functools.partial(send_sfwd, it, d, q))
        when(has[d], functools.partial(send_far, it, d))

    def scatter_own(it, d):
        r0 = row(HALO[d], my)
        for q in range(2):
            def add(q=q):
                z0 = (HZ, NH)[q]
                sfwd(it, d, q).wait_recv()
                cbuf[it, pl.ds(r0, my), z0:z0 + HZ, :] += sbuf[it, d]
            when(both(has[d], v == 1 - q), add)
        when(has[d], functools.partial(send_near, it, d))

    def scatter_piece(it, p):
        for d in range(2):
            when(zhas[d], functools.partial(send_sz, it, d, p))

    def scatter_end(it, p):
        r0 = row(EDGE[p], my)
        for q in range(2):
            z0 = ZED[1 + q][0]

            def add(q=q, z0=z0):
                sy(it, p, 1 + q).wait_recv()
                cbuf[it, pl.ds(r0, my), z0:z0 + HZ, :] += rybuf[it, p, :, z0:z0 + HZ, :]
            when(both(both(zed_has[1 + q], has[p]), v == q), add)
            when(both(zed_has[1 + q], v == q), functools.partial(send_sz, it, 1 - q, p))

    def scatter_near(it, p):
        for q in range(2):
            when(v == 1 - q, functools.partial(send_sz, it, 1 - q, p))

    def scatter_take(it, p):
        n = ROWS[p][1]
        r0 = row(*ROWS[p])
        if p < 2:
            def add_y():
                sy_own(it, p, False).wait_recv()
                sy_own(it, p, True).wait_recv()
                cbuf[it, pl.ds(row(EDGE[p], my), my), HZ:HZ + NH, :] += rybuf[it, p, :, HZ:HZ + NH, :]
            when(has[p], add_y)
            if it + 1 == ITERS:
                for q in range(2):
                    def add_diagonal(q=q):
                        z0 = (NH, HZ)[q]
                        diagonal(it, p, q).wait_recv()
                        cbuf[it, pl.ds(row(EDGE[p], my), my), z0:z0 + HZ, :] += rybuf[it, p, :, 0:HZ, :]
                    when(both(both(zed_has[2 - q], has[p]), v == 1 - q), add_diagonal)
        for d in range(2):
            z0 = (HZ, NH)[d]

            def add_z(d=d, z0=z0):
                sz(it, d, p).wait_recv()
                cbuf[it, pl.ds(r0, n), z0:z0 + HZ, :] += rzbuf[it, d, pl.ds(r0 - my, n)]
            when(zfrom[d], add_z)

    with scope("Wload"):
        load_start.wait()
    ebuf[0, my:my + NY, HZ:HZ + NH, :] = jnp.transpose(stage[0], (1, 0, 2))
    gather_own(0)
    mine[...] = jnp.zeros_like(mine)
    for k, (raw, taps) in enumerate(((raw_z, KZ), (raw_y, KY), (raw_x, KX))):
        loads[k].wait()
        mine[k:k + 1, 0:taps] = raw[...] / jnp.sum(raw[...], axis=1, keepdims=True)
    swap_prof = pltpu.make_async_remote_copy(
        src_ref=mine, dst_ref=theirs, send_sem=xssem.at[0], recv_sem=xrsem.at[0],
        device_id=partner, device_id_type=MESH)
    swap_prof.start()
    swap_obs = pltpu.make_async_remote_copy(
        src_ref=obs_hbm.at[0, pl.ds((1 - v) * NH, NH)], dst_ref=obs_z.at[v],
        send_sem=xssem.at[1], recv_sem=xrsem.at[1], device_id=partner, device_id_type=MESH)
    swap_obs.start()

    with scope("Wprof"):
        swap_prof.wait()
    own, other = mine[...], theirs[...]
    prof = (jnp.where(v == 0, own, other), jnp.where(v == 0, other, own))

    def tap(view, k, a):
        return prof[view][k:k + 1, a:a + 1]

    rows = lax.broadcasted_iota(jnp.int32, (NE, 3 * NE), 0)
    cols = lax.broadcasted_iota(jnp.int32, (NE, 3 * NE), 1)
    third = cols // NE
    cols = cols - third * NE

    def banded(diff, view, k, taps):
        w = jnp.zeros(diff.shape, F32)
        for a in range(taps):
            w = jnp.where(diff == a, tap(view, k, a), w)
        return w

    off = HZ - mz
    for ref, inner, outer in ((wf, rows, cols), (wb, cols, rows)):
        second = inner >= NH
        diff = outer - jnp.where(second, inner - NH, inner) - off
        w = jnp.where(second, banded(diff, 1, 0, KZ), banded(diff, 0, 0, KZ))
        high, low = split(w)
        ref[...] = jnp.where(third == 2, low.astype(F32), high.astype(F32)).astype(BF16)
    for view in range(2):
        for back in range(2):
            for r0 in range(0, NX, 64):
                r = lax.broadcasted_iota(jnp.int32, (64, NX), 0) + r0
                c = lax.broadcasted_iota(jnp.int32, (64, NX), 1)
                diff = (c - r if back else r - c) + mx
                high, low = split(banded(diff, view, 2, KX))
                tx[view, back, 0, r0:r0 + 64, :] = high
                tx[view, back, 1, r0:r0 + 64, :] = low
    wy = [[jnp.broadcast_to(tap(view, 1, b), (NH, NX)) for b in range(KY)] for view in range(2)]
    wl = [[jnp.where(f == 0, wy[view][KY - 1 - k], wy[view][k]) for k in range(KY)] for view in range(2)]

    with scope("Wobs"):
        load_obs.wait()
        swap_obs.wait()
    for view in range(2):
        obs_t[view] = jnp.transpose(obs_z[view], (1, 0, 2))

    def xblur(high, low, view, back):
        both_ = jnp.concatenate([high, low], axis=0)
        n = high.shape[0]
        d = jnp.dot(both_, tx[view, back, 0], preferred_element_type=F32)
        d2 = jnp.dot(high, tx[view, back, 1], preferred_element_type=F32)
        return d[:n] + (d[n:] + d2)

    def stacked(x):
        high, low = split(x)
        return jnp.concatenate([high, low, high], axis=0)

    for it in range(ITERS):
        def zrows(i0, n, it=it):
            with scope(f"z{it}_{i0}"):
                r0 = row(i0, n)
                for y in range(n):
                    zbuf[r0 + y] = jnp.dot(wf[...], stacked(ebuf[it, r0 + y]), preferred_element_type=F32)

        def qrows(o0, n, it=it):
            with scope(f"q{it}_{o0}"):
                y0 = row(o0 + my, n) - my
                for view in range(2):
                    z0 = view * NH
                    for y in range(n):
                        acc = wy[view][0] * zbuf[y0 + y, z0:z0 + NH, :]
                        for b in range(1, KY):
                            acc = acc + wy[view][b] * zbuf[y0 + y + b, z0:z0 + NH, :]
                        high, low = split(acc)
                        ybuf[view, 0, y * NH:(y + 1) * NH, :] = high
                        ybuf[view, 1, y * NH:(y + 1) * NH, :] = low
                for view in range(2):
                    z0 = view * NH
                    m = n * NH
                    blurred = xblur(ybuf[view, 0, 0:m], ybuf[view, 1, 0:m], view, 0)
                    quotient = obs_t[view, pl.ds(y0, n)].reshape(m, NX) / blurred
                    high, low = split(quotient)
                    ybuf[view, 2, 0:m] = high
                    ybuf[view, 3, 0:m] = low
                    qbuf[pl.ds(2 * my + y0, n), z0:z0 + NH, :] = xblur(
                        ybuf[view, 2, 0:m], ybuf[view, 3, 0:m], view, 1).reshape(n, NH, NX)

        def crows(i0, n, it=it):
            with scope(f"c{it}_{i0}"):
                inside = i0 >= 2 * my and i0 + n <= NY
                r0 = row(i0, n)
                for y in range(n):
                    r = r0 + y if inside else row(i0 + y)
                    parts = []
                    for view in range(2):
                        z0 = view * NH
                        acc = None
                        for k in range(KY):
                            o = i0 + y - 2 * my + k
                            if inside:
                                term = wy[view][k] * qbuf[r + 2 * my - k, z0:z0 + NH, :]
                            elif 0 <= o < NY:
                                term = wl[view][k] * qbuf[qrow(2 * my + o), z0:z0 + NH, :]
                            else:
                                continue
                            acc = term if acc is None else acc + term
                        parts.append(acc)
                    cbuf[it, r] = jnp.dot(wb[...], stacked(jnp.concatenate(parts, axis=0)),
                                          preferred_element_type=F32)

        def low_edge(it=it):
            edge_own(it, 1)
            gather_edge(it, 1)
            zrows(0, my)
        if it == 0:
            with scope("Wg0_in"):
                first_take(0)
            zrows(my + CH, CH)
            with scope("Wge0own"):
                edge_own(it, 0)
            with scope("Wg0_out"):
                first_take(1)
            zrows(my, CH)
            when(has[1], low_edge)
            qrows(0, OUT)
        else:
            for p in (1, 2):
                with scope(f"Wg{it}_{p}"):
                    gather_take(it, p)
                zrows(*ROWS[p])
            when(has[1], low_edge)
            qrows(0, my + 1)
            with scope(f"Wg{it}_3"):
                gather_take(it, 3)
            zrows(*ROWS[3])
            qrows(my + 1, OUT - my - 1)

        def low_scatter(it=it):
            crows(0, my)
            scatter_edge(it, 1)

        def high_edge(it=it):
            with scope(f"Wge{it}"):
                gather_edge(it, 0)
            zrows(my + NY, my)

        def high_scatter(it=it):
            crows(my + NY, my)
            scatter_edge(it, 0)

        when(has[1], low_scatter)
        crows(*ROWS[1])
        when(jnp.logical_not(has[1]), functools.partial(scatter_piece, it, 1))
        if it == 0:
            qrows(OUT, MID)
            crows(2 * my + 1, NY - 3 * my - 1)
            scatter_piece(it, 2)
            scatter_piece(it, 3)
            when(has[0], high_edge)
            qrows(OUT + MID, my)
            when(has[0], high_scatter)
            crows(NY - my, 2 * my)
            scatter_piece(it, 4)
            scatter_near(it, 0)
            with scope(f"Wso{it}"):
                scatter_own(it, 0)
            with scope(f"Wse{it}"):
                scatter_end(it, 0)
        else:
            with scope(f"Wg{it}_0"):
                gather_take(it, 0)
            with scope(f"Wge{it}own"):
                edge_own(it, 0)
            with scope(f"Wg{it}_4"):
                gather_take(it, 4)
            zrows(NY - my, 2 * my)
            qrows(OUT, MID)
            crows(2 * my + 1, NY - 3 * my - 1)
            scatter_piece(it, 2)
            scatter_piece(it, 3)
            when(has[0], high_edge)
            qrows(OUT + MID, my)
            when(has[0], high_scatter)
            crows(NY - my, 2 * my)
            scatter_piece(it, 0)
            scatter_piece(it, 4)
            with scope(f"Wso{it}"):
                scatter_own(it, 0)

        def low_end(it=it):
            scatter_own(it, 1)
            if it + 1 < ITERS:
                scatter_near(it, 1)
                scatter_end(it, 1)
            else:
                scatter_piece(it, 1)
        when(has[1], low_end)
        def update(p, it=it):
            n = ROWS[p][1]
            r0 = row(*ROWS[p])
            with scope(f"Wst{it}_{p}"):
                scatter_take(it, p)
            new = ebuf[it, pl.ds(r0, n), HZ:HZ + NH, :] * (0.5 * cbuf[it, pl.ds(r0, n), HZ:HZ + NH, :])
            if it + 1 < ITERS:
                ebuf[it + 1, pl.ds(r0, n), HZ:HZ + NH, :] = new
            else:
                zbuf[pl.ds(r0, n), 0:NH, :] = new

        if it + 1 < ITERS:
            for p in (1, 2, 3):
                update(p)
                gather_piece(it + 1, p)
            update(0)
            gather_piece(it + 1, 0)
            gather_own(it + 1)
            update(4)
            gather_piece(it + 1, 4)
        else:
            outs = []
            def leave(k, h, count):
                b0 = pl.multiple_of(blocks[k], CH)
                stage[0, pl.ds(h, count), pl.ds(b0, CH), :] = jnp.transpose(
                    zbuf[pl.ds(my + b0, CH), pl.ds(h, count), :], (1, 0, 2))
                src = stage.at[0, pl.ds(h, count), pl.ds(b0, CH)]
                dst = out_hbm.at[pl.ds(v * NH + h, count), pl.ds(b0, CH)]
                n = len(outs) // 2
                outs.append(pltpu.make_async_copy(src, dst, lsem.at[n]))
                outs.append(pltpu.make_async_remote_copy(
                    src_ref=src, dst_ref=dst, send_sem=xssem.at[n], recv_sem=xrsem.at[n],
                    device_id=partner, device_id_type=MESH))
                outs[-1].start()
                outs[-2].start()

            def finish(p, near):
                n = ROWS[p][1]
                r0 = row(*ROWS[p])
                for q in range(2):
                    def half(q=q):
                        z0, h0 = (HZ, NH)[q], q * HH

                        def add():
                            sz(it, q, p).wait_recv()
                            cbuf[it, pl.ds(r0, n), z0:z0 + HZ, :] += rzbuf[it, q, pl.ds(r0 - my, n)]
                        when(zfrom[q], add)
                        if p == 0 and not near:
                            def add_diagonal():
                                diagonal(it, p, 1 - q).wait_recv()
                                cbuf[it, pl.ds(row(EDGE[p], my), my), z0:z0 + HZ, :] += rybuf[it, p, :, 0:HZ, :]
                            when(both(zfrom[q], has[p]), add_diagonal)
                        zbuf[pl.ds(r0, n), h0:h0 + HH, :] = (
                            ebuf[it, pl.ds(r0, n), HZ + h0:HZ + h0 + HH, :]
                            * (0.5 * cbuf[it, pl.ds(r0, n), HZ + h0:HZ + h0 + HH, :]))
                    when(v == (1 - q if near else q), half)

            for p in (1, 2, 3):
                update(p)
            leave(1, 0, NH)

            def add_own():
                sy_own(it, 0, False).wait_recv()
                sy_own(it, 0, True).wait_recv()
                cbuf[it, pl.ds(row(EDGE[0], my), my), HZ:HZ + NH, :] += rybuf[it, 0, :, HZ:HZ + NH, :]
            with scope("Wown"):
                when(has[0], add_own)
            with scope("Wnear"):
                finish(4, True)
                finish(0, True)
            leave(0, pl.multiple_of((1 - v) * HH, HH), HH)
            with scope("Wfar"):
                finish(4, False)
                finish(0, False)
            leave(0, pl.multiple_of(v * HH, HH), HH)
            with scope("Wsent2"):
                sent()
            with scope("Wout"):
                for out in outs:
                    out.wait()


def store(src, dst, sem):
    copy = pltpu.make_async_copy(src, dst, sem)
    copy.start()
    copy.wait()


def on_device(S, G, observed, start, spread_z, spread_y, spread_x):
    NZ, NY, NX = start.shape
    KZ, KY, KX = spread_z.shape[1], spread_y.shape[1], spread_x.shape[1]
    NH = NZ // 2
    my = KY // 2
    HZ = -(-(KZ // 2) // 8) * 8
    NE, NR = NH + 2 * HZ, NY + 2 * my
    dims = (NH, NY, NX, HZ, KZ, KY, KX, S, G)
    vm = pltpu.VMEM
    hbm = pl.BlockSpec(memory_space=pltpu.HBM)
    out = pl.pallas_call(
        functools.partial(kernel, dims),
        out_shape=jax.ShapeDtypeStruct((NZ, NY, NX), F32),
        in_specs=[hbm] * 5,
        out_specs=pl.BlockSpec(memory_space=pl.ANY),
        scratch_shapes=[
            vm((1, KZ), F32), vm((1, KY), F32), vm((1, KX), F32),
            vm((1, NH, NY, NX), F32), vm((2, HZ, NY, NX), F32),
            vm((2, NH, NY, NX), F32), vm((2, NY, NH, NX), F32),
            vm((8, 128), F32), vm((8, 128), F32),
            vm((NE, 3 * NE), BF16), vm((NE, 3 * NE), BF16), vm((2, 2, 2, NX, NX), BF16),
            vm((NR, NE, NX), F32), vm((2, 4, NY // 2 * NH, NX), BF16), vm((NY + 4 * my, NE, NX), F32),
            vm((ITERS, NR, NE, NX), F32), vm((ITERS, NR, NE, NX), F32),
            vm((ITERS, 2, my, NE, NX), F32), vm((ITERS, 2, NY, HZ, NX), F32), vm((ITERS, 2, my, HZ, NX), F32),
            pltpu.SemaphoreType.DMA((5,)), pltpu.SemaphoreType.DMA((18,)), pltpu.SemaphoreType.DMA((34,)),
            pltpu.SemaphoreType.DMA((3,)), pltpu.SemaphoreType.DMA((3,)),
        ],
        compiler_params=pltpu.CompilerParams(
            collective_id=0, has_side_effects=True, vmem_limit_bytes=24 << 20),
    )(*(pltpu.with_memory_space_constraint(x, pltpu.HBM) for x in (observed, start, spread_z, spread_y, spread_x)))
    return pl.pallas_call(
        store,
        out_shape=jax.ShapeDtypeStruct((NZ, NY, NX), F32),
        in_specs=[pl.BlockSpec(memory_space=pl.ANY)],
        out_specs=hbm,
        scratch_shapes=[pltpu.SemaphoreType.DMA],
        compiler_params=pltpu.CompilerParams(vmem_limit_bytes=4 << 20),
    )(out)


def solution(mesh):
    S, G = 2 * mesh.shape["gz"], mesh.shape["gy"]
    return jax.shard_map(
        functools.partial(on_device, S, G),
        mesh=mesh,
        in_specs=(
            P("view", "gz", "gy", None),
            P("gz", "gy", None),
            P("view", None),
            P("view", None),
            P("view", None),
        ),
        out_specs=P("gz", "gy", None),
        check_vma=False,
    )
```

```python
import contextlib
import functools

import jax
import jax.numpy as jnp
from jax import lax
from jax.experimental import pallas as pl
from jax.experimental.pallas import tpu as pltpu
from jax.sharding import PartitionSpec as P

ITERS = 2
MESH = pl.DeviceIdType.MESH
F32 = jnp.float32
BF16 = jnp.bfloat16


def scope(name):
    return contextlib.nullcontext()


def split(x):
    high = x.astype(BF16)
    return high, (x - high.astype(F32)).astype(BF16)


def kernel(dims, obs_hbm, start_hbm, sz_ref, sy_ref, sx_ref, out_hbm,
           raw_z, raw_y, raw_x, stage, land, obs_z, obs_t, mine, theirs, wf, wb, tx, zbuf, ybuf, qbuf,
           ebuf, cbuf, rybuf, rzbuf, sbuf, lsem, ssem, rsem, xssem, xrsem):
    NH, NY, NX, HZ, KZ, KY, KX, S, G = dims
    my, mz, mx = KY // 2, KZ // 2, KX // 2
    NE, NR, NQ = NH + 2 * HZ, NY + 2 * my, NY + 4 * my
    CH, NP = NY // 2, 5
    assert NH >= 2 * HZ
    v = lax.axis_index("view")
    gy = lax.axis_index("gy")
    s = 2 * lax.axis_index("gz") + v
    up_z, dn_z = s < S - 1, s > 0
    up_y, dn_y = gy < G - 1, gy > 0
    f = lax.rem(gy, 2)
    has = (jnp.logical_or(jnp.logical_and(f == 0, up_y), jnp.logical_and(f == 1, dn_y)),
           jnp.logical_or(jnp.logical_and(f == 0, dn_y), jnp.logical_and(f == 1, up_y)))

    def row(i0, n=1):
        return i0 + f * (NR - 2 * i0 - n)

    def qrow(j0, n=1):
        return j0 + f * (NQ - 2 * j0 - n)

    def zdev(t):
        t = lax.rem(t + S, S)
        return {"view": lax.rem(t, 2), "gz": t // 2}

    zto = (zdev(s + 1), zdev(s - 1))
    step = 1 - 2 * f
    yto = ({"gy": lax.rem(gy + step + G, G)}, {"gy": lax.rem(gy - step + G, G)})
    partner = {"view": 1 - v}
    zout = dict(zdev(s - 1 + 2 * v))
    diag = tuple({**zout, **yto[d]} for d in range(2))
    zhas, zfrom = (up_z, dn_z), (dn_z, up_z)

    def when(cond, fn):
        @pl.when(cond)
        def _():
            fn()

    def both(a, b):
        return jnp.logical_and(a, b)

    barrier = pltpu.get_barrier_semaphore()
    greet = ((up_z, zto[0]), (dn_z, zto[1]), (has[0], yto[0]), (has[1], yto[1]))
    for there, to in greet:
        @pl.when(there)
        def _(to=to):
            pl.semaphore_signal(barrier, inc=1, device_id=to, device_id_type=MESH)

    load_start = pltpu.make_async_copy(start_hbm.at[pl.ds(v * NH, NH)], stage.at[0], lsem.at[0])
    load_start.start()
    load_obs = pltpu.make_async_copy(obs_hbm.at[0, pl.ds(v * NH, NH)], obs_z.at[v], lsem.at[1])
    load_obs.start()
    loads = [pltpu.make_async_copy(ref, raw, lsem.at[2 + k])
             for k, (ref, raw) in enumerate(((sz_ref, raw_z), (sy_ref, raw_y), (sx_ref, raw_x)))]
    for load in loads:
        load.start()

    blocks = (CH * (1 - f), CH * f)

    def first(d, k):
        b0 = pl.multiple_of(blocks[k], CH)
        src0 = v * NH + (NH - mz, 0)[d]
        dst0 = (HZ - mz, 0)[d]
        return pltpu.make_async_remote_copy(
            src_ref=start_hbm.at[pl.ds(src0, mz), pl.ds(b0, CH)],
            dst_ref=land.at[d, pl.ds(dst0, mz), pl.ds(b0, CH)],
            send_sem=ssem.at[NP * d + k], recv_sem=rsem.at[NP * d + k], device_id=zto[d], device_id_type=MESH)

    peers = sum(there.astype(jnp.int32) for there, _ in greet)
    with scope("Wbar"):
        pl.semaphore_wait(barrier, peers)
    for k in range(2):
        for d in range(2):
            when(zhas[d], first(d, k).start)

    land[0, 0:HZ - mz] = jnp.zeros((HZ - mz, NY, NX), F32)
    land[1, mz:HZ] = jnp.zeros((HZ - mz, NY, NX), F32)
    for d in range(2):
        def blank(d=d):
            for it in range(ITERS):
                z0 = (0, HZ + NH)[d]
                ebuf[it, :, z0:z0 + HZ, :] = jnp.zeros((NR, HZ, NX), F32)
        when(jnp.logical_not(zfrom[d]), blank)

        def blank_rows(d=d):
            zbuf[pl.ds(row((my + NY, 0)[d], my), my)] = jnp.zeros((my, NE, NX), F32)
        when(jnp.logical_not(has[d]), blank_rows)

    def copy(send, recv, src, dst, to):
        return pltpu.make_async_remote_copy(
            src_ref=src, dst_ref=dst, send_sem=ssem.at[send], recv_sem=rsem.at[recv],
            device_id=to, device_id_type=MESH)

    ROWS = ((NY, my), (my, my + 1), (2 * my + 1, NY - 4 * my - 1), (NY - 2 * my, my), (NY - my, my), (NY - my, 2 * my))
    LAST = NP
    OUT, MID = NY - 3 * my, 2 * my
    assert len(ROWS) == NP + 1
    ZED = ((HZ, NH), (0, HZ), (HZ + NH, HZ))
    zed_has = (None, dn_z, up_z)
    EDGE, HALO = (NY, my), (my + NY, 0)
    THERE = (f * (my + NY), (1 - f) * (my + NY))

    def gz(it, d, p):
        e = ebuf.at[it]
        src0, dst0 = ((NH, 0), (HZ, HZ + NH))[d]
        n = ROWS[p][1]
        r0 = row(*ROWS[p])
        return copy(NP * d + p, NP * d + p, e.at[pl.ds(r0, n), pl.ds(src0, HZ)],
                    e.at[pl.ds(r0, n), pl.ds(dst0, HZ)], zto[d])

    def gyc(it, d, p):
        e = ebuf.at[it]
        z0, n = ZED[p]
        k = 2 * min(p, 1) + d
        return copy(2 * NP + k, 4 * NP + k, e.at[pl.ds(row(EDGE[d], my), my), pl.ds(z0, n)],
                    e.at[pl.ds(THERE[d], my), pl.ds(z0, n)], yto[d])

    HH = NH // 2

    def sy_own(it, d, near):
        z0 = pl.multiple_of(HZ + HH * (1 - v if near else v), 8)
        return copy(2 * NP + (6 + d if near else d), 4 * NP + 6 + (6 + d if near else d),
                    cbuf.at[it, pl.ds(row(HALO[d], my), my), pl.ds(z0, HH)],
                    rybuf.at[it, d, :, pl.ds(z0, HH)], yto[d])

    def fwd(it, d, q):
        rows_ = pl.ds(row(HALO[d], my), my)
        e = ebuf.at[it]
        return copy(2 * NP + 4 + d, 4 * NP + 4 + d, e.at[rows_, pl.ds((NH, HZ)[q], HZ)],
                    e.at[rows_, pl.ds((0, HZ + NH)[q], HZ)], partner)

    def sfwd(it, d, q):
        rows_ = pl.ds(row(HALO[d], my), my)
        return copy(2 * NP + 4 + d, 4 * NP + 10 + d, cbuf.at[it, rows_, pl.ds((HZ + NH, 0)[q], HZ)],
                    sbuf.at[it, d], partner)

    def diagonal(it, d, q):
        z0, n = ZED[1 + q]
        return copy(2 * NP + 2 + d, 4 * NP + 8 + d, cbuf.at[it, pl.ds(row(HALO[d], my), my), pl.ds(z0, n)],
                    rybuf.at[it, d, :, pl.ds(0, HZ)], diag[d])

    def sz(it, d, p):
        src0 = (HZ + NH, 0)[d]
        n = ROWS[p][1]
        r0 = row(*ROWS[p])
        k = NP * d + p % NP
        return copy(k, 2 * NP + k, cbuf.at[it, pl.ds(r0, n), pl.ds(src0, HZ)],
                    rzbuf.at[it, d, pl.ds(r0 - my, n)], zto[d])

    def sy(it, d, p):
        z0, n = ZED[p]
        k = 2 * min(p, 1) + d
        return copy(2 * NP + k, 4 * NP + 6 + k, cbuf.at[it, pl.ds(row(HALO[d], my), my), pl.ds(z0, n)],
                    rybuf.at[it, d, :, pl.ds(z0, n)], yto[d])

    def follow(before, now):
        if before is not None:
            before.wait_send()
        now.start()

    def send_gz(it, d, p):
        follow(sz(it - 1, d, p), gz(it, d, p))

    def send_sz(it, d, p):
        follow(gz(it, d, p % NP) if it > 0 else first(d, p) if p < 2 else None, sz(it, d, p))

    def send_gy(it, d, p):
        before = None if it == 0 else sy_own(it - 1, d, False) if p == 0 else sy(it - 1, d, p)
        follow(before, gyc(it, d, p))

    def send_far(it, d):
        follow(gyc(it, d, 0), sy_own(it, d, False))

    def send_near(it, d):
        follow(sy_own(it - 1, d, True) if it > 0 else None, sy_own(it, d, True))

    def send_sy(it, d, p):
        now = diagonal(it, d, p - 1) if p > 0 and it + 1 == ITERS else sy(it, d, p)
        follow(gyc(it, d, p), now)

    def send_fwd(it, d, q):
        follow(sfwd(it - 1, d, q) if it > 0 else None, fwd(it, d, q))

    def send_sfwd(it, d, q):
        follow(fwd(it, d, q), sfwd(it, d, q))

    def gather_piece(it, p):
        for d in range(2):
            when(zhas[d], functools.partial(send_gz, it, d, p))

    def gather_own(it):
        for d in range(2):
            when(has[d], functools.partial(send_gy, it, d, 0))

    def relay(it, p, d):
        if p < 2:
            when(both(both(zfrom[d], has[p]), v == d), functools.partial(send_gy, it, p, 1 + d))

    def gather_take(it, p):
        for d in range(2):
            when(zfrom[d], gz(it, d, p).wait_recv)
            relay(it, p, d)

    def first_take(k):
        b0 = pl.multiple_of(blocks[k], CH)
        for d in range(2):
            z0 = (0, HZ + NH)[d]

            def take(d=d, z0=z0):
                first(d, k).wait_recv()
                ebuf[0, pl.ds(my + b0, CH), z0:z0 + HZ, :] = jnp.transpose(land[d, :, pl.ds(b0, CH), :], (1, 0, 2))
            when(zfrom[d], take)
            relay(0, k, d)

    def edge_own(it, d):
        def go():
            gyc(it, d, 0).wait_recv()
            for q in range(2):
                when(v == q, functools.partial(send_fwd, it, d, q))
        when(has[d], go)

    def gather_edge(it, d):
        for q in range(2):
            when(both(both(zed_has[1 + q], has[d]), v == q), gyc(it, d, 1 + q).wait_recv)
            when(both(has[d], v == 1 - q), fwd(it, d, q).wait_recv)

    def sent():
        it = ITERS - 1
        for d in range(2):
            def along_z(d=d):
                gz(it, d, 4).wait_send()
                for p in (1, 2, 3, LAST):
                    sz(it, d, p).wait_send()
            when(zhas[d], along_z)

            def along_y(d=d):
                sy_own(it, d, False).wait_send()
                sy_own(it, d, True).wait_send()
                for q in range(2):
                    when(both(zed_has[1 + q], v == q), diagonal(it, d, q).wait_send)
                    when(v == q, sfwd(it, d, q).wait_send)
            when(has[d], along_y)

    def scatter_edge(it, d):
        for q in range(2):
            when(both(both(zed_has[1 + q], has[d]), v == q), functools.partial(send_sy, it, d, 1 + q))
            when(both(has[d], v == q), functools.partial(send_sfwd, it, d, q))
        when(has[d], functools.partial(send_far, it, d))

    def scatter_own(it, d):
        r0 = row(HALO[d], my)
        for q in range(2):
            def add(q=q):
                z0 = (HZ, NH)[q]
                sfwd(it, d, q).wait_recv()
                cbuf[it, pl.ds(r0, my), z0:z0 + HZ, :] += sbuf[it, d]
            when(both(has[d], v == 1 - q), add)
        when(has[d], functools.partial(send_near, it, d))

    def scatter_piece(it, p):
        for d in range(2):
            when(zhas[d], functools.partial(send_sz, it, d, p))

    def scatter_end(it, p):
        r0 = row(EDGE[p], my)
        for q in range(2):
            z0 = ZED[1 + q][0]

            def add(q=q, z0=z0):
                sy(it, p, 1 + q).wait_recv()
                cbuf[it, pl.ds(r0, my), z0:z0 + HZ, :] += rybuf[it, p, :, z0:z0 + HZ, :]
            when(both(both(zed_has[1 + q], has[p]), v == q), add)
            when(both(zed_has[1 + q], v == q), functools.partial(send_sz, it, 1 - q, p))

    def scatter_near(it, p):
        for q in range(2):
            when(v == 1 - q, functools.partial(send_sz, it, 1 - q, p))

    def scatter_take(it, p):
        n = ROWS[p][1]
        r0 = row(*ROWS[p])
        if p < 2:
            def add_y():
                sy_own(it, p, False).wait_recv()
                sy_own(it, p, True).wait_recv()
                cbuf[it, pl.ds(row(EDGE[p], my), my), HZ:HZ + NH, :] += rybuf[it, p, :, HZ:HZ + NH, :]
            when(has[p], add_y)
            if it + 1 == ITERS:
                for q in range(2):
                    def add_diagonal(q=q):
                        z0 = (NH, HZ)[q]
                        diagonal(it, p, q).wait_recv()
                        cbuf[it, pl.ds(row(EDGE[p], my), my), z0:z0 + HZ, :] += rybuf[it, p, :, 0:HZ, :]
                    when(both(both(zed_has[2 - q], has[p]), v == 1 - q), add_diagonal)
        for d in range(2):
            z0 = (HZ, NH)[d]

            def add_z(d=d, z0=z0):
                sz(it, d, p).wait_recv()
                cbuf[it, pl.ds(r0, n), z0:z0 + HZ, :] += rzbuf[it, d, pl.ds(r0 - my, n)]
            when(zfrom[d], add_z)

    with scope("Wload"):
        load_start.wait()
    ebuf[0, my:my + NY, HZ:HZ + NH, :] = jnp.transpose(stage[0], (1, 0, 2))
    gather_own(0)
    mine[...] = jnp.zeros_like(mine)
    for k, (raw, taps) in enumerate(((raw_z, KZ), (raw_y, KY), (raw_x, KX))):
        loads[k].wait()
        mine[k:k + 1, 0:taps] = raw[...] / jnp.sum(raw[...], axis=1, keepdims=True)
    swap_prof = pltpu.make_async_remote_copy(
        src_ref=mine, dst_ref=theirs, send_sem=xssem.at[0], recv_sem=xrsem.at[0],
        device_id=partner, device_id_type=MESH)
    swap_prof.start()
    swap_obs = pltpu.make_async_remote_copy(
        src_ref=obs_hbm.at[0, pl.ds((1 - v) * NH, NH)], dst_ref=obs_z.at[v],
        send_sem=xssem.at[1], recv_sem=xrsem.at[1], device_id=partner, device_id_type=MESH)
    swap_obs.start()

    with scope("Wprof"):
        swap_prof.wait()
    own, other = mine[...], theirs[...]
    prof = (jnp.where(v == 0, own, other), jnp.where(v == 0, other, own))

    def tap(view, k, a):
        return prof[view][k:k + 1, a:a + 1]

    rows = lax.broadcasted_iota(jnp.int32, (NE, 3 * NE), 0)
    cols = lax.broadcasted_iota(jnp.int32, (NE, 3 * NE), 1)
    third = cols // NE
    cols = cols - third * NE

    def banded(diff, view, k, taps):
        w = jnp.zeros(diff.shape, F32)
        for a in range(taps):
            w = jnp.where(diff == a, tap(view, k, a), w)
        return w

    off = HZ - mz
    for ref, inner, outer in ((wf, rows, cols), (wb, cols, rows)):
        second = inner >= NH
        diff = outer - jnp.where(second, inner - NH, inner) - off
        w = jnp.where(second, banded(diff, 1, 0, KZ), banded(diff, 0, 0, KZ))
        high, low = split(w)
        ref[...] = jnp.where(third == 2, low.astype(F32), high.astype(F32)).astype(BF16)
    for view in range(2):
        for back in range(2):
            for r0 in range(0, NX, 64):
                r = lax.broadcasted_iota(jnp.int32, (64, NX), 0) + r0
                c = lax.broadcasted_iota(jnp.int32, (64, NX), 1)
                diff = (c - r if back else r - c) + mx
                high, low = split(banded(diff, view, 2, KX))
                tx[view, back, 0, r0:r0 + 64, :] = high
                tx[view, back, 1, r0:r0 + 64, :] = low
    wy = [[jnp.broadcast_to(tap(view, 1, b), (NH, NX)) for b in range(KY)] for view in range(2)]
    wl = [[jnp.where(f == 0, wy[view][KY - 1 - k], wy[view][k]) for k in range(KY)] for view in range(2)]

    with scope("Wobs"):
        load_obs.wait()
        swap_obs.wait()
    for view in range(2):
        obs_t[view] = jnp.transpose(obs_z[view], (1, 0, 2))

    def xblur(high, low, view, back):
        both_ = jnp.concatenate([high, low], axis=0)
        n = high.shape[0]
        d = jnp.dot(both_, tx[view, back, 0], preferred_element_type=F32)
        d2 = jnp.dot(high, tx[view, back, 1], preferred_element_type=F32)
        return d[:n] + (d[n:] + d2)

    def stacked(x):
        high, low = split(x)
        return jnp.concatenate([high, low, high], axis=0)

    for it in range(ITERS):
        def zrows(i0, n, it=it):
            with scope(f"z{it}_{i0}"):
                r0 = row(i0, n)
                for y in range(n):
                    zbuf[r0 + y] = jnp.dot(wf[...], stacked(ebuf[it, r0 + y]), preferred_element_type=F32)

        def qrows(o0, n, it=it):
            with scope(f"q{it}_{o0}"):
                y0 = row(o0 + my, n) - my
                for view in range(2):
                    z0 = view * NH
                    for y in range(n):
                        acc = wy[view][0] * zbuf[y0 + y, z0:z0 + NH, :]
                        for b in range(1, KY):
                            acc = acc + wy[view][b] * zbuf[y0 + y + b, z0:z0 + NH, :]
                        high, low = split(acc)
                        ybuf[view, 0, y * NH:(y + 1) * NH, :] = high
                        ybuf[view, 1, y * NH:(y + 1) * NH, :] = low
                for view in range(2):
                    z0 = view * NH
                    m = n * NH
                    blurred = xblur(ybuf[view, 0, 0:m], ybuf[view, 1, 0:m], view, 0)
                    quotient = obs_t[view, pl.ds(y0, n)].reshape(m, NX) / blurred
                    high, low = split(quotient)
                    ybuf[view, 2, 0:m] = high
                    ybuf[view, 3, 0:m] = low
                    qbuf[pl.ds(2 * my + y0, n), z0:z0 + NH, :] = xblur(
                        ybuf[view, 2, 0:m], ybuf[view, 3, 0:m], view, 1).reshape(n, NH, NX)

        def crows(i0, n, it=it):
            with scope(f"c{it}_{i0}"):
                inside = i0 >= 2 * my and i0 + n <= NY
                r0 = row(i0, n)
                for y in range(n):
                    r = r0 + y if inside else row(i0 + y)
                    parts = []
                    for view in range(2):
                        z0 = view * NH
                        acc = None
                        for k in range(KY):
                            o = i0 + y - 2 * my + k
                            if inside:
                                term = wy[view][k] * qbuf[r + 2 * my - k, z0:z0 + NH, :]
                            elif 0 <= o < NY:
                                term = wl[view][k] * qbuf[qrow(2 * my + o), z0:z0 + NH, :]
                            else:
                                continue
                            acc = term if acc is None else acc + term
                        parts.append(acc)
                    cbuf[it, r] = jnp.dot(wb[...], stacked(jnp.concatenate(parts, axis=0)),
                                          preferred_element_type=F32)

        def low_edge(it=it):
            edge_own(it, 1)
            gather_edge(it, 1)
            zrows(0, my)
        if it == 0:
            with scope("Wg0_in"):
                first_take(0)
            zrows(my + CH, CH)
            with scope("Wge0own"):
                edge_own(it, 0)
            with scope("Wg0_out"):
                first_take(1)
            zrows(my, CH)
            when(has[1], low_edge)
            qrows(0, OUT)
        else:
            for p in (1, 2):
                with scope(f"Wg{it}_{p}"):
                    gather_take(it, p)
                zrows(*ROWS[p])
            when(has[1], low_edge)
            qrows(0, my + 1)
            with scope(f"Wg{it}_3"):
                gather_take(it, 3)
            zrows(*ROWS[3])
            qrows(my + 1, OUT - my - 1)

        def low_scatter(it=it):
            crows(0, my)
            scatter_edge(it, 1)

        def high_edge(it=it):
            with scope(f"Wge{it}"):
                gather_edge(it, 0)
            zrows(my + NY, my)

        def high_scatter(it=it):
            crows(my + NY, my)
            scatter_edge(it, 0)

        when(has[1], low_scatter)
        crows(*ROWS[1])
        when(jnp.logical_not(has[1]), functools.partial(scatter_piece, it, 1))
        if it == 0:
            qrows(OUT, MID)
            crows(2 * my + 1, NY - 3 * my - 1)
            scatter_piece(it, 2)
            scatter_piece(it, 3)
            when(has[0], high_edge)
            qrows(OUT + MID, my)
            when(has[0], high_scatter)
            crows(NY - my, 2 * my)
            scatter_piece(it, 4)
            scatter_near(it, 0)
            with scope(f"Wso{it}"):
                scatter_own(it, 0)
            with scope(f"Wse{it}"):
                scatter_end(it, 0)
        else:
            with scope(f"Wg{it}_0"):
                gather_take(it, 0)
            with scope(f"Wge{it}own"):
                edge_own(it, 0)
            with scope(f"Wg{it}_4"):
                gather_take(it, 4)
            zrows(NY - my, 2 * my)
            qrows(OUT, MID)
            crows(2 * my + 1, NY - 3 * my - 1)
            scatter_piece(it, 2)
            scatter_piece(it, 3)
            when(has[0], high_edge)
            qrows(OUT + MID, my)
            when(has[0], high_scatter)
            crows(NY - my, 2 * my)
            scatter_piece(it, LAST)
            with scope(f"Wso{it}"):
                scatter_own(it, 0)

        def low_end(it=it):
            scatter_own(it, 1)
            if it + 1 < ITERS:
                scatter_near(it, 1)
                scatter_end(it, 1)
            else:
                scatter_piece(it, 1)
        when(has[1], low_end)
        def update(p, it=it):
            n = ROWS[p][1]
            r0 = row(*ROWS[p])
            with scope(f"Wst{it}_{p}"):
                scatter_take(it, p)
            new = ebuf[it, pl.ds(r0, n), HZ:HZ + NH, :] * (0.5 * cbuf[it, pl.ds(r0, n), HZ:HZ + NH, :])
            if it + 1 < ITERS:
                ebuf[it + 1, pl.ds(r0, n), HZ:HZ + NH, :] = new
            else:
                zbuf[pl.ds(r0, n), 0:NH, :] = new

        if it + 1 < ITERS:
            for p in (1, 2, 3):
                update(p)
                gather_piece(it + 1, p)
            update(0)
            gather_piece(it + 1, 0)
            gather_own(it + 1)
            update(4)
            gather_piece(it + 1, 4)
        else:
            outs = []
            def leave(k, h, count):
                b0 = pl.multiple_of(blocks[k], CH)
                stage[0, pl.ds(h, count), pl.ds(b0, CH), :] = jnp.transpose(
                    zbuf[pl.ds(my + b0, CH), pl.ds(h, count), :], (1, 0, 2))
                src = stage.at[0, pl.ds(h, count), pl.ds(b0, CH)]
                dst = out_hbm.at[pl.ds(v * NH + h, count), pl.ds(b0, CH)]
                n = len(outs) // 2
                outs.append(pltpu.make_async_copy(src, dst, lsem.at[n]))
                outs.append(pltpu.make_async_remote_copy(
                    src_ref=src, dst_ref=dst, send_sem=xssem.at[n], recv_sem=xrsem.at[n],
                    device_id=partner, device_id_type=MESH))
                outs[-1].start()
                outs[-2].start()

            def finish(p, near):
                n = ROWS[p][1]
                r0 = row(*ROWS[p])
                for q in range(2):
                    def half(q=q):
                        z0, h0 = (HZ, NH)[q], q * HH

                        def add():
                            sz(it, q, p).wait_recv()
                            cbuf[it, pl.ds(r0, n), z0:z0 + HZ, :] += rzbuf[it, q, pl.ds(r0 - my, n)]
                        when(zfrom[q], add)
                        if not near:
                            def add_diagonal():
                                diagonal(it, 0, 1 - q).wait_recv()
                                cbuf[it, pl.ds(row(EDGE[0], my), my), z0:z0 + HZ, :] += rybuf[it, 0, :, 0:HZ, :]
                            when(both(zfrom[q], has[0]), add_diagonal)
                        zbuf[pl.ds(r0, n), h0:h0 + HH, :] = (
                            ebuf[it, pl.ds(r0, n), HZ + h0:HZ + h0 + HH, :]
                            * (0.5 * cbuf[it, pl.ds(r0, n), HZ + h0:HZ + h0 + HH, :]))
                    when(v == (1 - q if near else q), half)

            for p in (1, 2, 3):
                update(p)
            leave(1, 0, NH)

            def add_own():
                sy_own(it, 0, False).wait_recv()
                sy_own(it, 0, True).wait_recv()
                cbuf[it, pl.ds(row(EDGE[0], my), my), HZ:HZ + NH, :] += rybuf[it, 0, :, HZ:HZ + NH, :]
            with scope("Wown"):
                when(has[0], add_own)
            with scope("Wnear"):
                finish(LAST, True)
            leave(0, pl.multiple_of((1 - v) * HH, HH), HH)
            with scope("Wfar"):
                finish(LAST, False)
            leave(0, pl.multiple_of(v * HH, HH), HH)
            with scope("Wsent2"):
                sent()
            with scope("Wout"):
                for out in outs:
                    out.wait()


def store(src, dst, sem):
    copy = pltpu.make_async_copy(src, dst, sem)
    copy.start()
    copy.wait()


def on_device(S, G, observed, start, spread_z, spread_y, spread_x):
    NZ, NY, NX = start.shape
    KZ, KY, KX = spread_z.shape[1], spread_y.shape[1], spread_x.shape[1]
    NH = NZ // 2
    my = KY // 2
    HZ = -(-(KZ // 2) // 8) * 8
    NE, NR = NH + 2 * HZ, NY + 2 * my
    dims = (NH, NY, NX, HZ, KZ, KY, KX, S, G)
    vm = pltpu.VMEM
    hbm = pl.BlockSpec(memory_space=pltpu.HBM)
    out = pl.pallas_call(
        functools.partial(kernel, dims),
        out_shape=jax.ShapeDtypeStruct((NZ, NY, NX), F32),
        in_specs=[hbm] * 5,
        out_specs=pl.BlockSpec(memory_space=pl.ANY),
        scratch_shapes=[
            vm((1, KZ), F32), vm((1, KY), F32), vm((1, KX), F32),
            vm((1, NH, NY, NX), F32), vm((2, HZ, NY, NX), F32),
            vm((2, NH, NY, NX), F32), vm((2, NY, NH, NX), F32),
            vm((8, 128), F32), vm((8, 128), F32),
            vm((NE, 3 * NE), BF16), vm((NE, 3 * NE), BF16), vm((2, 2, 2, NX, NX), BF16),
            vm((NR, NE, NX), F32), vm((2, 4, NY // 2 * NH, NX), BF16), vm((NY + 4 * my, NE, NX), F32),
            vm((ITERS, NR, NE, NX), F32), vm((ITERS, NR, NE, NX), F32),
            vm((ITERS, 2, my, NE, NX), F32), vm((ITERS, 2, NY, HZ, NX), F32), vm((ITERS, 2, my, HZ, NX), F32),
            pltpu.SemaphoreType.DMA((5,)), pltpu.SemaphoreType.DMA((18,)), pltpu.SemaphoreType.DMA((34,)),
            pltpu.SemaphoreType.DMA((3,)), pltpu.SemaphoreType.DMA((3,)),
        ],
        compiler_params=pltpu.CompilerParams(
            collective_id=0, has_side_effects=True, vmem_limit_bytes=24 << 20),
    )(*(pltpu.with_memory_space_constraint(x, pltpu.HBM) for x in (observed, start, spread_z, spread_y, spread_x)))
    return pl.pallas_call(
        store,
        out_shape=jax.ShapeDtypeStruct((NZ, NY, NX), F32),
        in_specs=[pl.BlockSpec(memory_space=pl.ANY)],
        out_specs=hbm,
        scratch_shapes=[pltpu.SemaphoreType.DMA],
        compiler_params=pltpu.CompilerParams(vmem_limit_bytes=4 << 20),
    )(out)


def solution(mesh):
    S, G = 2 * mesh.shape["gz"], mesh.shape["gy"]
    return jax.shard_map(
        functools.partial(on_device, S, G),
        mesh=mesh,
        in_specs=(
            P("view", "gz", "gy", None),
            P("gz", "gy", None),
            P("view", None),
            P("view", None),
            P("view", None),
        ),
        out_specs=P("gz", "gy", None),
        check_vma=False,
    )
```

```python
import contextlib
import functools

import jax
import jax.numpy as jnp
from jax import lax
from jax.experimental import pallas as pl
from jax.experimental.pallas import tpu as pltpu
from jax.sharding import PartitionSpec as P

ITERS = 2
MESH = pl.DeviceIdType.MESH
F32 = jnp.float32
BF16 = jnp.bfloat16


def scope(name):
    return contextlib.nullcontext()


def split(x):
    high = x.astype(BF16)
    return high, (x - high.astype(F32)).astype(BF16)


def kernel(dims, obs_hbm, start_hbm, sz_ref, sy_ref, sx_ref, out_hbm,
           raw_z, raw_y, raw_x, stage, land, obs_z, obs_t, mine, theirs, wf, wb, tx, zbuf, ybuf, qbuf,
           ebuf, cbuf, rybuf, rzbuf, sbuf, lsem, ssem, rsem, xssem, xrsem):
    NH, NY, NX, HZ, KZ, KY, KX, S, G = dims
    my, mz, mx = KY // 2, KZ // 2, KX // 2
    NE, NR, NQ = NH + 2 * HZ, NY + 2 * my, NY + 4 * my
    CH, NP = NY // 2, 5
    assert NH >= 2 * HZ
    v = lax.axis_index("view")
    gy = lax.axis_index("gy")
    s = 2 * lax.axis_index("gz") + v
    up_z, dn_z = s < S - 1, s > 0
    up_y, dn_y = gy < G - 1, gy > 0
    f = lax.rem(gy, 2)
    has = (jnp.logical_or(jnp.logical_and(f == 0, up_y), jnp.logical_and(f == 1, dn_y)),
           jnp.logical_or(jnp.logical_and(f == 0, dn_y), jnp.logical_and(f == 1, up_y)))

    def row(i0, n=1):
        return i0 + f * (NR - 2 * i0 - n)

    def qrow(j0, n=1):
        return j0 + f * (NQ - 2 * j0 - n)

    def zdev(t):
        t = lax.rem(t + S, S)
        return {"view": lax.rem(t, 2), "gz": t // 2}

    zto = (zdev(s + 1), zdev(s - 1))
    step = 1 - 2 * f
    yto = ({"gy": lax.rem(gy + step + G, G)}, {"gy": lax.rem(gy - step + G, G)})
    partner = {"view": 1 - v}
    zout = dict(zdev(s - 1 + 2 * v))
    diag = tuple({**zout, **yto[d]} for d in range(2))
    zhas, zfrom = (up_z, dn_z), (dn_z, up_z)

    def when(cond, fn):
        @pl.when(cond)
        def _():
            fn()

    def both(a, b):
        return jnp.logical_and(a, b)

    barrier = pltpu.get_barrier_semaphore()
    greet = ((up_z, zto[0]), (dn_z, zto[1]), (has[0], yto[0]), (has[1], yto[1]))
    for there, to in greet:
        @pl.when(there)
        def _(to=to):
            pl.semaphore_signal(barrier, inc=1, device_id=to, device_id_type=MESH)

    load_start = pltpu.make_async_copy(start_hbm.at[pl.ds(v * NH, NH)], stage.at[0], lsem.at[0])
    load_start.start()
    load_obs = pltpu.make_async_copy(obs_hbm.at[0, pl.ds(v * NH, NH)], obs_z.at[v], lsem.at[1])
    load_obs.start()
    loads = [pltpu.make_async_copy(ref, raw, lsem.at[2 + k])
             for k, (ref, raw) in enumerate(((sz_ref, raw_z), (sy_ref, raw_y), (sx_ref, raw_x)))]
    for load in loads:
        load.start()

    blocks = (CH * (1 - f), CH * f)

    def first(d, k):
        b0 = pl.multiple_of(blocks[k], CH)
        src0 = v * NH + (NH - mz, 0)[d]
        dst0 = (HZ - mz, 0)[d]
        return pltpu.make_async_remote_copy(
            src_ref=start_hbm.at[pl.ds(src0, mz), pl.ds(b0, CH)],
            dst_ref=land.at[d, pl.ds(dst0, mz), pl.ds(b0, CH)],
            send_sem=ssem.at[NP * d + k], recv_sem=rsem.at[NP * d + k], device_id=zto[d], device_id_type=MESH)

    peers = sum(there.astype(jnp.int32) for there, _ in greet)
    with scope("Wbar"):
        pl.semaphore_wait(barrier, peers)
    for k in range(2):
        for d in range(2):
            when(zhas[d], first(d, k).start)

    land[0, 0:HZ - mz] = jnp.zeros((HZ - mz, NY, NX), F32)
    land[1, mz:HZ] = jnp.zeros((HZ - mz, NY, NX), F32)
    for d in range(2):
        def blank(d=d):
            for it in range(ITERS):
                z0 = (0, HZ + NH)[d]
                ebuf[it, :, z0:z0 + HZ, :] = jnp.zeros((NR, HZ, NX), F32)
        when(jnp.logical_not(zfrom[d]), blank)

        def blank_rows(d=d):
            zbuf[pl.ds(row((my + NY, 0)[d], my), my)] = jnp.zeros((my, NE, NX), F32)
        when(jnp.logical_not(has[d]), blank_rows)

    def copy(send, recv, src, dst, to):
        return pltpu.make_async_remote_copy(
            src_ref=src, dst_ref=dst, send_sem=ssem.at[send], recv_sem=rsem.at[recv],
            device_id=to, device_id_type=MESH)

    ROWS = ((NY, my), (my, my + 1), (2 * my + 1, NY - 4 * my - 1), (NY - 2 * my, my), (NY - my, my))
    OUT, MID = NY - 3 * my, 2 * my
    assert len(ROWS) == NP
    ZED = ((HZ, NH), (0, HZ), (HZ + NH, HZ))
    zed_has = (None, dn_z, up_z)
    EDGE, HALO = (NY, my), (my + NY, 0)
    THERE = (f * (my + NY), (1 - f) * (my + NY))

    def gz(it, d, p):
        e = ebuf.at[it]
        src0, dst0 = ((NH, 0), (HZ, HZ + NH))[d]
        n = ROWS[p][1]
        r0 = row(*ROWS[p])
        return copy(NP * d + p, NP * d + p, e.at[pl.ds(r0, n), pl.ds(src0, HZ)],
                    e.at[pl.ds(r0, n), pl.ds(dst0, HZ)], zto[d])

    def gyc(it, d, p):
        e = ebuf.at[it]
        z0, n = ZED[p]
        k = 2 * min(p, 1) + d
        return copy(2 * NP + k, 4 * NP + k, e.at[pl.ds(row(EDGE[d], my), my), pl.ds(z0, n)],
                    e.at[pl.ds(THERE[d], my), pl.ds(z0, n)], yto[d])

    HH = NH // 2

    def sy_own(it, d, near):
        z0 = pl.multiple_of(HZ + HH * (1 - v if near else v), 8)
        return copy(2 * NP + (6 + d if near else d), 4 * NP + 6 + (6 + d if near else d),
                    cbuf.at[it, pl.ds(row(HALO[d], my), my), pl.ds(z0, HH)],
                    rybuf.at[it, d, :, pl.ds(z0, HH)], yto[d])

    def fwd(it, d, q):
        rows_ = pl.ds(row(HALO[d], my), my)
        e = ebuf.at[it]
        return copy(2 * NP + 4 + d, 4 * NP + 4 + d, e.at[rows_, pl.ds((NH, HZ)[q], HZ)],
                    e.at[rows_, pl.ds((0, HZ + NH)[q], HZ)], partner)

    def sfwd(it, d, q):
        rows_ = pl.ds(row(HALO[d], my), my)
        return copy(2 * NP + 4 + d, 4 * NP + 10 + d, cbuf.at[it, rows_, pl.ds((HZ + NH, 0)[q], HZ)],
                    sbuf.at[it, d], partner)

    def diagonal(it, d, q):
        z0, n = ZED[1 + q]
        return copy(2 * NP + 2 + d, 4 * NP + 8 + d, cbuf.at[it, pl.ds(row(HALO[d], my), my), pl.ds(z0, n)],
                    rybuf.at[it, d, :, pl.ds(0, HZ)], diag[d])

    def sz(it, d, p):
        src0 = (HZ + NH, 0)[d]
        n = ROWS[p][1]
        r0 = row(*ROWS[p])
        return copy(NP * d + p, 2 * NP + NP * d + p, cbuf.at[it, pl.ds(r0, n), pl.ds(src0, HZ)],
                    rzbuf.at[it, d, pl.ds(r0 - my, n)], zto[d])

    def sy(it, d, p):
        z0, n = ZED[p]
        k = 2 * min(p, 1) + d
        return copy(2 * NP + k, 4 * NP + 6 + k, cbuf.at[it, pl.ds(row(HALO[d], my), my), pl.ds(z0, n)],
                    rybuf.at[it, d, :, pl.ds(z0, n)], yto[d])

    def follow(before, now):
        if before is not None:
            before.wait_send()
        now.start()

    def send_gz(it, d, p):
        follow(sz(it - 1, d, p), gz(it, d, p))

    def send_sz(it, d, p):
        follow(gz(it, d, p) if it > 0 else first(d, p) if p < 2 else None, sz(it, d, p))

    def send_gy(it, d, p):
        before = None if it == 0 else sy_own(it - 1, d, False) if p == 0 else sy(it - 1, d, p)
        follow(before, gyc(it, d, p))

    def send_far(it, d):
        follow(gyc(it, d, 0), sy_own(it, d, False))

    def send_near(it, d):
        follow(sy_own(it - 1, d, True) if it > 0 else None, sy_own(it, d, True))

    def send_sy(it, d, p):
        now = diagonal(it, d, p - 1) if p > 0 and it + 1 == ITERS else sy(it, d, p)
        follow(gyc(it, d, p), now)

    def send_fwd(it, d, q):
        follow(sfwd(it - 1, d, q) if it > 0 else None, fwd(it, d, q))

    def send_sfwd(it, d, q):
        follow(fwd(it, d, q), sfwd(it, d, q))

    def gather_piece(it, p):
        for d in range(2):
            when(zhas[d], functools.partial(send_gz, it, d, p))

    def gather_own(it):
        for d in range(2):
            when(has[d], functools.partial(send_gy, it, d, 0))

    def relay(it, p, d):
        if p < 2:
            when(both(both(zfrom[d], has[p]), v == d), functools.partial(send_gy, it, p, 1 + d))

    def gather_take(it, p):
        for d in range(2):
            when(zfrom[d], gz(it, d, p).wait_recv)
            relay(it, p, d)

    def first_take(k):
        b0 = pl.multiple_of(blocks[k], CH)
        for d in range(2):
            z0 = (0, HZ + NH)[d]

            def take(d=d, z0=z0):
                first(d, k).wait_recv()
                ebuf[0, pl.ds(my + b0, CH), z0:z0 + HZ, :] = jnp.transpose(land[d, :, pl.ds(b0, CH), :], (1, 0, 2))
            when(zfrom[d], take)
            relay(0, k, d)

    def edge_own(it, d):
        def go():
            gyc(it, d, 0).wait_recv()
            for q in range(2):
                when(v == q, functools.partial(send_fwd, it, d, q))
        when(has[d], go)

    def gather_edge(it, d):
        for q in range(2):
            when(both(both(zed_has[1 + q], has[d]), v == q), gyc(it, d, 1 + q).wait_recv)
            when(both(has[d], v == 1 - q), fwd(it, d, q).wait_recv)

    def sent():
        it = ITERS - 1
        for d in range(2):
            def along_z(d=d):
                for p in range(NP):
                    sz(it, d, p).wait_send()
            when(zhas[d], along_z)

            def along_y(d=d):
                sy_own(it, d, False).wait_send()
                sy_own(it, d, True).wait_send()
                for q in range(2):
                    when(both(zed_has[1 + q], v == q), diagonal(it, d, q).wait_send)
                    when(v == q, sfwd(it, d, q).wait_send)
            when(has[d], along_y)

    def scatter_edge(it, d):
        for q in range(2):
            when(both(both(zed_has[1 + q], has[d]), v == q), functools.partial(send_sy, it, d, 1 + q))
            when(both(has[d], v == q), functools.partial(send_sfwd, it, d, q))
        when(has[d], functools.partial(send_far, it, d))

    def scatter_own(it, d):
        r0 = row(HALO[d], my)
        for q in range(2):
            def add(q=q):
                z0 = (HZ, NH)[q]
                sfwd(it, d, q).wait_recv()
                cbuf[it, pl.ds(r0, my), z0:z0 + HZ, :] += sbuf[it, d]
            when(both(has[d], v == 1 - q), add)
        when(has[d], functools.partial(send_near, it, d))

    def scatter_piece(it, p):
        for d in range(2):
            when(zhas[d], functools.partial(send_sz, it, d, p))

    def scatter_end(it, p):
        r0 = row(EDGE[p], my)
        for q in range(2):
            z0 = ZED[1 + q][0]

            def add(q=q, z0=z0):
                sy(it, p, 1 + q).wait_recv()
                cbuf[it, pl.ds(r0, my), z0:z0 + HZ, :] += rybuf[it, p, :, z0:z0 + HZ, :]
            when(both(both(zed_has[1 + q], has[p]), v == q), add)
            when(both(zed_has[1 + q], v == q), functools.partial(send_sz, it, 1 - q, p))

    def scatter_near(it, p):
        for q in range(2):
            when(v == 1 - q, functools.partial(send_sz, it, 1 - q, p))

    def scatter_take(it, p):
        n = ROWS[p][1]
        r0 = row(*ROWS[p])
        if p < 2:
            def add_y():
                sy_own(it, p, False).wait_recv()
                sy_own(it, p, True).wait_recv()
                cbuf[it, pl.ds(row(EDGE[p], my), my), HZ:HZ + NH, :] += rybuf[it, p, :, HZ:HZ + NH, :]
            when(has[p], add_y)
            if it + 1 == ITERS:
                for q in range(2):
                    def add_diagonal(q=q):
                        z0 = (NH, HZ)[q]
                        diagonal(it, p, q).wait_recv()
                        cbuf[it, pl.ds(row(EDGE[p], my), my), z0:z0 + HZ, :] += rybuf[it, p, :, 0:HZ, :]
                    when(both(both(zed_has[2 - q], has[p]), v == 1 - q), add_diagonal)
        for d in range(2):
            z0 = (HZ, NH)[d]

            def add_z(d=d, z0=z0):
                sz(it, d, p).wait_recv()
                cbuf[it, pl.ds(r0, n), z0:z0 + HZ, :] += rzbuf[it, d, pl.ds(r0 - my, n)]
            when(zfrom[d], add_z)

    with scope("Wload"):
        load_start.wait()
    ebuf[0, my:my + NY, HZ:HZ + NH, :] = jnp.transpose(stage[0], (1, 0, 2))
    gather_own(0)
    mine[...] = jnp.zeros_like(mine)
    for k, (raw, taps) in enumerate(((raw_z, KZ), (raw_y, KY), (raw_x, KX))):
        loads[k].wait()
        mine[k:k + 1, 0:taps] = raw[...] / jnp.sum(raw[...], axis=1, keepdims=True)
    swap_prof = pltpu.make_async_remote_copy(
        src_ref=mine, dst_ref=theirs, send_sem=xssem.at[0], recv_sem=xrsem.at[0],
        device_id=partner, device_id_type=MESH)
    swap_prof.start()
    swap_obs = pltpu.make_async_remote_copy(
        src_ref=obs_hbm.at[0, pl.ds((1 - v) * NH, NH)], dst_ref=obs_z.at[v],
        send_sem=xssem.at[1], recv_sem=xrsem.at[1], device_id=partner, device_id_type=MESH)
    swap_obs.start()

    with scope("Wprof"):
        swap_prof.wait()
    own, other = mine[...], theirs[...]
    prof = (jnp.where(v == 0, own, other), jnp.where(v == 0, other, own))

    def tap(view, k, a):
        return prof[view][k:k + 1, a:a + 1]

    rows = lax.broadcasted_iota(jnp.int32, (NE, 3 * NE), 0)
    cols = lax.broadcasted_iota(jnp.int32, (NE, 3 * NE), 1)
    third = cols // NE
    cols = cols - third * NE

    def banded(diff, view, k, taps):
        w = jnp.zeros(diff.shape, F32)
        for a in range(taps):
            w = jnp.where(diff == a, tap(view, k, a), w)
        return w

    off = HZ - mz
    for ref, inner, outer in ((wf, rows, cols), (wb, cols, rows)):
        second = inner >= NH
        diff = outer - jnp.where(second, inner - NH, inner) - off
        w = jnp.where(second, banded(diff, 1, 0, KZ), banded(diff, 0, 0, KZ))
        high, low = split(w)
        ref[...] = jnp.where(third == 2, low.astype(F32), high.astype(F32)).astype(BF16)
    for view in range(2):
        for back in range(2):
            for r0 in range(0, NX, 64):
                r = lax.broadcasted_iota(jnp.int32, (64, NX), 0) + r0
                c = lax.broadcasted_iota(jnp.int32, (64, NX), 1)
                diff = (c - r if back else r - c) + mx
                high, low = split(banded(diff, view, 2, KX))
                tx[view, back, 0, r0:r0 + 64, :] = high
                tx[view, back, 1, r0:r0 + 64, :] = low
    wy = [[jnp.broadcast_to(tap(view, 1, b), (NH, NX)) for b in range(KY)] for view in range(2)]
    wl = [[jnp.where(f == 0, wy[view][KY - 1 - k], wy[view][k]) for k in range(KY)] for view in range(2)]

    with scope("Wobs"):
        load_obs.wait()
        swap_obs.wait()
    for view in range(2):
        obs_t[view] = jnp.transpose(obs_z[view], (1, 0, 2))

    def xblur(high, low, view, back):
        both_ = jnp.concatenate([high, low], axis=0)
        n = high.shape[0]
        d = jnp.dot(both_, tx[view, back, 0], preferred_element_type=F32)
        d2 = jnp.dot(high, tx[view, back, 1], preferred_element_type=F32)
        return d[:n] + (d[n:] + d2)

    def stacked(x):
        high, low = split(x)
        return jnp.concatenate([high, low, high], axis=0)

    for it in range(ITERS):
        def zrows(i0, n, it=it):
            with scope(f"z{it}_{i0}"):
                r0 = row(i0, n)
                for y in range(n):
                    zbuf[r0 + y] = jnp.dot(wf[...], stacked(ebuf[it, r0 + y]), preferred_element_type=F32)

        def qrows(o0, n, it=it):
            with scope(f"q{it}_{o0}"):
                y0 = row(o0 + my, n) - my
                for view in range(2):
                    z0 = view * NH
                    for y in range(n):
                        acc = wy[view][0] * zbuf[y0 + y, z0:z0 + NH, :]
                        for b in range(1, KY):
                            acc = acc + wy[view][b] * zbuf[y0 + y + b, z0:z0 + NH, :]
                        high, low = split(acc)
                        ybuf[view, 0, y * NH:(y + 1) * NH, :] = high
                        ybuf[view, 1, y * NH:(y + 1) * NH, :] = low
                for view in range(2):
                    z0 = view * NH
                    m = n * NH
                    blurred = xblur(ybuf[view, 0, 0:m], ybuf[view, 1, 0:m], view, 0)
                    quotient = obs_t[view, pl.ds(y0, n)].reshape(m, NX) / blurred
                    high, low = split(quotient)
                    ybuf[view, 2, 0:m] = high
                    ybuf[view, 3, 0:m] = low
                    qbuf[pl.ds(2 * my + y0, n), z0:z0 + NH, :] = xblur(
                        ybuf[view, 2, 0:m], ybuf[view, 3, 0:m], view, 1).reshape(n, NH, NX)

        def crows(i0, n, it=it):
            with scope(f"c{it}_{i0}"):
                inside = i0 >= 2 * my and i0 + n <= NY
                r0 = row(i0, n)
                for y in range(n):
                    r = r0 + y if inside else row(i0 + y)
                    parts = []
                    for view in range(2):
                        z0 = view * NH
                        acc = None
                        for k in range(KY):
                            o = i0 + y - 2 * my + k
                            if inside:
                                term = wy[view][k] * qbuf[r + 2 * my - k, z0:z0 + NH, :]
                            elif 0 <= o < NY:
                                term = wl[view][k] * qbuf[qrow(2 * my + o), z0:z0 + NH, :]
                            else:
                                continue
                            acc = term if acc is None else acc + term
                        parts.append(acc)
                    cbuf[it, r] = jnp.dot(wb[...], stacked(jnp.concatenate(parts, axis=0)),
                                          preferred_element_type=F32)

        def low_edge(it=it):
            edge_own(it, 1)
            gather_edge(it, 1)
            zrows(0, my)
        if it == 0:
            with scope("Wg0_in"):
                first_take(0)
            zrows(my + CH, CH)
            with scope("Wge0own"):
                edge_own(it, 0)
            with scope("Wg0_out"):
                first_take(1)
            zrows(my, CH)
            when(has[1], low_edge)
            qrows(0, OUT)
        else:
            for p in (1, 2):
                with scope(f"Wg{it}_{p}"):
                    gather_take(it, p)
                zrows(*ROWS[p])
            when(has[1], low_edge)
            qrows(0, my + 1)
            with scope(f"Wg{it}_3"):
                gather_take(it, 3)
            zrows(*ROWS[3])
            qrows(my + 1, OUT - my - 1)

        def low_scatter(it=it):
            crows(0, my)
            scatter_edge(it, 1)

        def high_edge(it=it):
            with scope(f"Wge{it}"):
                gather_edge(it, 0)
            zrows(my + NY, my)

        def high_scatter(it=it):
            crows(my + NY, my)
            scatter_edge(it, 0)

        when(has[1], low_scatter)
        crows(*ROWS[1])
        when(jnp.logical_not(has[1]), functools.partial(scatter_piece, it, 1))
        if it == 0:
            qrows(OUT, MID)
            crows(2 * my + 1, NY - 3 * my - 1)
            scatter_piece(it, 2)
            scatter_piece(it, 3)
            when(has[0], high_edge)
            qrows(OUT + MID, my)
            when(has[0], high_scatter)
            crows(*ROWS[4])
            scatter_piece(it, 4)
            crows(*ROWS[0])
            scatter_near(it, 0)
            with scope(f"Wso{it}"):
                scatter_own(it, 0)
            with scope(f"Wse{it}"):
                scatter_end(it, 0)
        else:
            with scope(f"Wg{it}_0"):
                gather_take(it, 0)
            with scope(f"Wge{it}own"):
                edge_own(it, 0)
            with scope(f"Wg{it}_4"):
                gather_take(it, 4)
            zrows(NY - my, 2 * my)
            qrows(OUT, MID)
            crows(2 * my + 1, NY - 3 * my - 1)
            scatter_piece(it, 2)
            scatter_piece(it, 3)
            when(has[0], high_edge)
            qrows(OUT + MID, my)
            when(has[0], high_scatter)
            crows(NY - my, 2 * my)
            scatter_piece(it, 0)
            scatter_piece(it, 4)
            with scope(f"Wso{it}"):
                scatter_own(it, 0)

        def low_end(it=it):
            scatter_own(it, 1)
            if it + 1 < ITERS:
                scatter_near(it, 1)
                scatter_end(it, 1)
            else:
                scatter_piece(it, 1)
        when(has[1], low_end)
        def update(p, it=it):
            n = ROWS[p][1]
            r0 = row(*ROWS[p])
            with scope(f"Wst{it}_{p}"):
                scatter_take(it, p)
            new = ebuf[it, pl.ds(r0, n), HZ:HZ + NH, :] * (0.5 * cbuf[it, pl.ds(r0, n), HZ:HZ + NH, :])
            if it + 1 < ITERS:
                ebuf[it + 1, pl.ds(r0, n), HZ:HZ + NH, :] = new
            else:
                zbuf[pl.ds(r0, n), 0:NH, :] = new

        if it + 1 < ITERS:
            for p in (1, 2, 3):
                update(p)
                gather_piece(it + 1, p)
            update(0)
            gather_piece(it + 1, 0)
            gather_own(it + 1)
            update(4)
            gather_piece(it + 1, 4)
        else:
            outs = []
            def leave(k, h, count):
                b0 = pl.multiple_of(blocks[k], CH)
                stage[0, pl.ds(h, count), pl.ds(b0, CH), :] = jnp.transpose(
                    zbuf[pl.ds(my + b0, CH), pl.ds(h, count), :], (1, 0, 2))
                src = stage.at[0, pl.ds(h, count), pl.ds(b0, CH)]
                dst = out_hbm.at[pl.ds(v * NH + h, count), pl.ds(b0, CH)]
                n = len(outs) // 2
                outs.append(pltpu.make_async_copy(src, dst, lsem.at[n]))
                outs.append(pltpu.make_async_remote_copy(
                    src_ref=src, dst_ref=dst, send_sem=xssem.at[n], recv_sem=xrsem.at[n],
                    device_id=partner, device_id_type=MESH))
                outs[-1].start()
                outs[-2].start()

            def finish(p, near):
                n = ROWS[p][1]
                r0 = row(*ROWS[p])
                for q in range(2):
                    def half(q=q):
                        z0, h0 = (HZ, NH)[q], q * HH

                        def add():
                            sz(it, q, p).wait_recv()
                            cbuf[it, pl.ds(r0, n), z0:z0 + HZ, :] += rzbuf[it, q, pl.ds(r0 - my, n)]
                        when(zfrom[q], add)
                        if p == 0 and not near:
                            def add_diagonal():
                                diagonal(it, p, 1 - q).wait_recv()
                                cbuf[it, pl.ds(row(EDGE[p], my), my), z0:z0 + HZ, :] += rybuf[it, p, :, 0:HZ, :]
                            when(both(zfrom[q], has[p]), add_diagonal)
                        zbuf[pl.ds(r0, n), h0:h0 + HH, :] = (
                            ebuf[it, pl.ds(r0, n), HZ + h0:HZ + h0 + HH, :]
                            * (0.5 * cbuf[it, pl.ds(r0, n), HZ + h0:HZ + h0 + HH, :]))
                    when(v == (1 - q if near else q), half)

            for p in (1, 2, 3):
                update(p)
            leave(1, 0, NH)

            def add_own():
                sy_own(it, 0, False).wait_recv()
                sy_own(it, 0, True).wait_recv()
                cbuf[it, pl.ds(row(EDGE[0], my), my), HZ:HZ + NH, :] += rybuf[it, 0, :, HZ:HZ + NH, :]
            with scope("Wown"):
                when(has[0], add_own)
            with scope("Wnear"):
                finish(4, True)
                finish(0, True)
            leave(0, pl.multiple_of((1 - v) * HH, HH), HH)
            with scope("Wfar"):
                finish(4, False)
                finish(0, False)
            leave(0, pl.multiple_of(v * HH, HH), HH)
            with scope("Wsent2"):
                sent()
            with scope("Wout"):
                for out in outs:
                    out.wait()


def store(src, dst, sem):
    copy = pltpu.make_async_copy(src, dst, sem)
    copy.start()
    copy.wait()


def on_device(S, G, observed, start, spread_z, spread_y, spread_x):
    NZ, NY, NX = start.shape
    KZ, KY, KX = spread_z.shape[1], spread_y.shape[1], spread_x.shape[1]
    NH = NZ // 2
    my = KY // 2
    HZ = -(-(KZ // 2) // 8) * 8
    NE, NR = NH + 2 * HZ, NY + 2 * my
    dims = (NH, NY, NX, HZ, KZ, KY, KX, S, G)
    vm = pltpu.VMEM
    hbm = pl.BlockSpec(memory_space=pltpu.HBM)
    out = pl.pallas_call(
        functools.partial(kernel, dims),
        out_shape=jax.ShapeDtypeStruct((NZ, NY, NX), F32),
        in_specs=[hbm] * 5,
        out_specs=pl.BlockSpec(memory_space=pl.ANY),
        scratch_shapes=[
            vm((1, KZ), F32), vm((1, KY), F32), vm((1, KX), F32),
            vm((1, NH, NY, NX), F32), vm((2, HZ, NY, NX), F32),
            vm((2, NH, NY, NX), F32), vm((2, NY, NH, NX), F32),
            vm((8, 128), F32), vm((8, 128), F32),
            vm((NE, 3 * NE), BF16), vm((NE, 3 * NE), BF16), vm((2, 2, 2, NX, NX), BF16),
            vm((NR, NE, NX), F32), vm((2, 4, NY // 2 * NH, NX), BF16), vm((NY + 4 * my, NE, NX), F32),
            vm((ITERS, NR, NE, NX), F32), vm((ITERS, NR, NE, NX), F32),
            vm((ITERS, 2, my, NE, NX), F32), vm((ITERS, 2, NY, HZ, NX), F32), vm((ITERS, 2, my, HZ, NX), F32),
            pltpu.SemaphoreType.DMA((5,)), pltpu.SemaphoreType.DMA((18,)), pltpu.SemaphoreType.DMA((34,)),
            pltpu.SemaphoreType.DMA((3,)), pltpu.SemaphoreType.DMA((3,)),
        ],
        compiler_params=pltpu.CompilerParams(
            collective_id=0, has_side_effects=True, vmem_limit_bytes=24 << 20),
    )(*(pltpu.with_memory_space_constraint(x, pltpu.HBM) for x in (observed, start, spread_z, spread_y, spread_x)))
    return pl.pallas_call(
        store,
        out_shape=jax.ShapeDtypeStruct((NZ, NY, NX), F32),
        in_specs=[pl.BlockSpec(memory_space=pl.ANY)],
        out_specs=hbm,
        scratch_shapes=[pltpu.SemaphoreType.DMA],
        compiler_params=pltpu.CompilerParams(vmem_limit_bytes=4 << 20),
    )(out)


def solution(mesh):
    S, G = 2 * mesh.shape["gz"], mesh.shape["gy"]
    return jax.shard_map(
        functools.partial(on_device, S, G),
        mesh=mesh,
        in_specs=(
            P("view", "gz", "gy", None),
            P("gz", "gy", None),
            P("view", None),
            P("view", None),
            P("view", None),
        ),
        out_specs=P("gz", "gy", None),
        check_vma=False,
    )
```
